512 devices in a mesh: firm: 16 (over z), worker: 8 (over y, core), probe: 4 (over x).
Axes of the slice: x: 4, y: 4, z: 16, core: 2. Of those that a mesh axis runs over, the one named last changes fastest.
Arguments:
- tiles: bfloat16 [16384, 128, 128], P(('firm', 'worker')), may hold values from -0.046875 to 0.046875
- tile_rows: int32 [128, 128], P(('firm', 'worker')), may hold values from 0 to 3
- tile_firms: int32 [128, 128], P(('firm', 'worker')), may hold values from 0 to 127
- worker_ids: int32 [128, 512], P(('firm', 'worker')), may hold values from 0 to 127, never falling along the last dimension, each value on 1 to 8 neighbouring positions
- sign_words: int32 [32, 512, 5], P('probe', ('firm', 'worker')), may hold values from 0 to 1073741823
- regular: float32 [16384], P('firm'), may hold values from 0.5 to 4
Outputs:
- solution: float32 [32, 16384], P('probe', 'firm')
- residual: float32 [32, 16384], P('probe', 'firm')
The draws below stay inside these ranges and needn't reach their ends.
Inputs may be any that keep to these rules, and one draw needn't show every extreme that they name: `worker_ids`: within each row shard the worker ids never fall, and each of the ids 0 to 127 has 1 to 8 rows. `sign_words`: only the bits that the steps read carry signs.
All inputs are finite; a program needn't handle non-finite values.
Results may differ from the reference program's by a relative error of at most 0.0064.
Values may be sent and summed in bfloat16 or wider, within the bound.
No kernel may reach another device: no remote copies, remote signals or barrier semaphores. Data moves between devices by JAX's collectives and lax.ppermute only.
A program may use at most 64 MiB of HBM per device.

```python
import math
import jax
import jax.numpy as jnp
import numpy as np
from jax import lax

TILE = 128
PROBES = 32
ITERS = 2
YEARS = 8
ROWB_DEV = 4
TILES_DEV = 128
SHARDS = 128
FB_TOTAL = 128
FIRMS = 16384
ROWS_DEV = 512
SHARD_WORKERS = 128
WORDS = 5


def touch_ends(entries, rng, smallest, largest):
    dims = entries.shape
    spot = [jax.random.randint(jax.random.fold_in(rng, axis), (), 0, dims[axis]) for axis in range(len(dims))]
    entries = entries.at[tuple(spot)].set(smallest)
    longest = dims.index(max(dims))
    spot[longest] = (spot[longest] + 1) % dims[longest]
    return entries.at[tuple(spot)].set(largest)


def levels(rng, dims, shards, least, largest):
    gain, own = 1.0, jax.random.fold_in(rng, 6)
    for dim, parts in shards:
        draws = jnp.exp(jax.random.uniform(jax.random.fold_in(own, dim), (parts,), jnp.float32, least / len(shards), largest / len(shards)))
        gain = gain * jnp.repeat(draws, dims[dim] // parts).reshape([-1 if axis == dim else 1 for axis in range(len(dims))])
    return gain


def rank_table(amount, lean):
    portions = [(1 << 20) // math.isqrt(rank ** lean) + 1 for rank in range(1, amount + 1)]
    spread = 1 + sum(portions) // (1 << 30)
    return np.cumsum(np.array([max(1, weight // spread) for weight in portions]))


def skewed_ids(key, extent, amount, skew):
    table = rank_table(amount, skew)
    pick = jax.random.randint(jax.random.fold_in(key, 1), extent, 0, int(table[amount - 1]))
    grade = jnp.searchsorted(jnp.asarray(table, jnp.int32), pick, side="right")
    return jax.random.permutation(jax.random.fold_in(key, 2), amount)[grade].astype(jnp.int32)


def profile(amount, total, most, lean):
    weights = [(1 << 20) // math.isqrt(grade ** lean) + 1 for grade in range(2, amount + 1)]
    spare, holding = total - most - (amount - 1), [1] * (amount - 1)
    while spare > 0:
        candidates = [i for i in range(amount - 1) if holding[i] < most]
        pool, budget = sum([weights[i] for i in candidates]), spare
        for i in candidates:
            extra = min(most - holding[i], max(1, budget * weights[i] // pool), spare)
            holding[i] = holding[i] + extra
            spare = spare - extra
    return np.array([most] + holding)


def ragged(own_key, number_of, total, most, lean):
    if number_of == 2:
        one = jax.random.randint(own_key, (), max(1, total - most), min(most, total - 1) + 1)
        return jnp.stack([one, total - one])
    tallies = jnp.asarray(profile(number_of, total, most, lean), jnp.int32)
    pairs = (number_of - 1) // 2
    donor, sink = tallies[1:1 + 2 * pairs:2], tallies[2:2 + 2 * pairs:2]
    slack = jnp.minimum(donor - 1, most - sink)
    moved = jax.random.randint(jax.random.fold_in(own_key, 1), (pairs,), 0, 1 << 20) % (slack + 1)
    tallies = tallies.at[1:1 + 2 * pairs:2].set(donor - moved).at[2:2 + 2 * pairs:2].set(sink + moved)
    return tallies[jax.random.permutation(jax.random.fold_in(own_key, 2), number_of)]


def normal_values(own_key, dims, scale, limit, pieces=(), held_as=jnp.bfloat16):
    result = jax.random.normal(own_key, dims, jnp.float32) * scale
    if len(pieces) > 0:
        result = levels(own_key, dims, pieces, -0.22, 0.18) * result
    return jnp.clip(result, min=-limit, max=limit).astype(held_as)


def setup_inputs(seed: int = 0) -> dict:
    key_list = jax.random.split(jax.random.key(seed), 7)
    tiles = normal_values(key_list[0], (SHARDS * TILES_DEV, TILE, TILE), (TILE * SHARDS * TILES_DEV // FB_TOTAL) ** -0.5, 0.046875, ((0, 128),))
    tile_rows = touch_ends(jax.random.randint(key_list[1], (SHARDS, TILES_DEV), 0, ROWB_DEV), jax.random.fold_in(key_list[1], 1), 0, ROWB_DEV - 1).astype(jnp.int32)
    tile_firms = touch_ends(skewed_ids(key_list[2], (SHARDS, TILES_DEV), FB_TOTAL, 1), jax.random.fold_in(key_list[2], 3), 0, FB_TOTAL - 1).astype(jnp.int32)
    worker_ids = jax.vmap(lambda own: jnp.searchsorted(jnp.cumsum(ragged(own, SHARD_WORKERS, ROWS_DEV, YEARS, 0)), jnp.arange(ROWS_DEV), side="right"))(jax.random.split(key_list[3], SHARDS)).reshape((SHARDS, ROWS_DEV)).astype(jnp.int32)
    sign_words = touch_ends(jax.random.randint(key_list[4], (PROBES, SHARDS * ROWB_DEV, WORDS), 0, 1073741824), jax.random.fold_in(key_list[4], 1), 0, 1073741823).astype(jnp.int32)
    regular = jnp.clip(jnp.exp(math.log(4.0) - 2.0794415 * jax.random.uniform(key_list[5], (FIRMS,), jnp.float32) ** levels(key_list[5], (FIRMS,), ((0, 16),), -0.2, 0.2)), 0.5, 4.0)
    return dict(tiles=tiles, tile_rows=tile_rows, tile_firms=tile_firms, worker_ids=worker_ids, sign_words=sign_words, regular=regular)


largest_value = lax.Precision.HIGHEST

def unpack_signs(words):
    position = np.arange(TILE)
    word_of = jnp.asarray(position // 30, jnp.int32)
    bit_of = jnp.asarray(position % 30, jnp.int32)
    selected_rows = jnp.take(words, word_of, axis=2)
    bit_values = jnp.bitwise_and(jnp.right_shift(selected_rows, bit_of), 1)
    return (2 * bit_values - 1).astype(jnp.float32).reshape(words.shape[0], words.shape[1] * TILE)

def demean(values, worker_row):
    onehot = (worker_row[:, None] == jnp.arange(SHARD_WORKERS)[None, :]).astype(jnp.float32)
    totals = jnp.dot(values, onehot, precision=largest_value)
    counts = jnp.sum(onehot, axis=0)
    return values - jnp.dot(totals / counts, onehot.T, precision=largest_value)

def forward_rows(field_bf, tile_group, row_ids, firm_ids):
    selected_rows = field_bf[firm_ids].astype(jnp.float32)
    block_products = jnp.einsum('awl,agl->awg', selected_rows, tile_group.astype(jnp.float32), precision=largest_value)
    summed = jax.ops.segment_sum(block_products, row_ids, num_segments=ROWB_DEV)
    return jnp.transpose(summed, (1, 0, 2)).reshape(summed.shape[1], ROWS_DEV)

def adjoint_blocks(rows_bf, tile_group, row_ids, firm_ids):
    feature_blocks = rows_bf.reshape(rows_bf.shape[0], ROWB_DEV, TILE)[:, row_ids].astype(jnp.float32)
    block_products = jnp.einsum('wqx,qxk->qwk', feature_blocks, tile_group.astype(jnp.float32), precision=largest_value)
    return jax.ops.segment_sum(block_products, firm_ids, num_segments=FB_TOTAL)

def gram_of(left_part, right_part):
    return jnp.einsum('bpf,bqf->pq', left_part, right_part, precision=largest_value)

def symmetric(matrix):
    return 0.5 * (matrix + matrix.T)

def combine_rows(weights, field):
    return jnp.einsum('pq,bpf->bqf', weights, field, precision=largest_value)

def solve_spd(matrix, target):
    factor = jnp.linalg.cholesky(matrix)
    inner = lax.linalg.triangular_solve(factor, target, left_side=True, lower=True)
    return lax.linalg.triangular_solve(factor, inner, left_side=True, lower=True, transpose_a=True)

def to_rows(field):
    return jnp.transpose(field, (1, 0, 2)).reshape(PROBES, FIRMS)

def reference(tiles, tile_rows, tile_firms, worker_ids, sign_words, regular):
    tile_sets = tiles.reshape(SHARDS, TILES_DEV, TILE, TILE)
    word_sets = jnp.transpose(sign_words.reshape(PROBES, SHARDS, ROWB_DEV, WORDS), (1, 0, 2, 3))
    reg_blocks = regular.reshape(FB_TOTAL, 1, TILE)
    empty = jnp.zeros((FB_TOTAL, PROBES, TILE), jnp.float32)

    def start_step(total, inputs):
        tile_group, row_ids, firm_ids, worker_row, words = inputs
        demeaned = demean(unpack_signs(words), worker_row).astype(jnp.bfloat16)
        return (total + adjoint_blocks(demeaned, tile_group, row_ids, firm_ids), None)
    right_side, unused = lax.scan(start_step, empty, (tile_sets, tile_rows, tile_firms, worker_ids, word_sets))

    def operator(field):
        field_bf = field.astype(jnp.bfloat16)

        def apply_step(total, inputs):
            tile_group, row_ids, firm_ids, worker_row = inputs
            rows_image = forward_rows(field_bf, tile_group, row_ids, firm_ids)
            demeaned = demean(rows_image, worker_row).astype(jnp.bfloat16)
            return (total + adjoint_blocks(demeaned, tile_group, row_ids, firm_ids), None)
        total, leftover = lax.scan(apply_step, empty, (tile_sets, tile_rows, tile_firms, worker_ids))
        return total + reg_blocks * field
    solution = jnp.zeros_like(right_side)
    residual = right_side
    direction = right_side
    current = symmetric(gram_of(residual, residual))
    for turn_index in range(ITERS):
        mapped = operator(direction)
        curvature = symmetric(gram_of(direction, mapped))
        step_size = solve_spd(curvature, current)
        solution = solution + combine_rows(step_size, direction)
        residual = residual - combine_rows(step_size, mapped)
        if turn_index + 1 < ITERS:
            following = symmetric(gram_of(residual, residual))
            carry_mix = solve_spd(current, following)
            direction = residual + combine_rows(carry_mix, direction)
            current = following
    return (to_rows(solution), to_rows(residual))
```

```python
import jax
import jax.numpy as jnp
import numpy as np
from jax import lax
from jax.sharding import PartitionSpec as P

TILE = 128
ROWB_DEV = 4
ROWS_DEV = 512
SHARD_WORKERS = 128


largest_value = lax.Precision.HIGHEST


def unpack_signs(words):
    position = np.arange(TILE)
    word_of = jnp.asarray(position // 30, jnp.int32)
    bit_of = jnp.asarray(position % 30, jnp.int32)
    selected_rows = jnp.take(words, word_of, axis=2)
    bit_values = jnp.bitwise_and(jnp.right_shift(selected_rows, bit_of), 1)
    return (2 * bit_values - 1).astype(jnp.float32).reshape(words.shape[0], words.shape[1] * TILE)


def demean(values, worker_row):
    onehot = (worker_row[:, None] == jnp.arange(SHARD_WORKERS)[None, :]).astype(jnp.float32)
    totals = jnp.dot(values, onehot, precision=largest_value)
    counts = jnp.sum(onehot, axis=0)
    return values - jnp.dot(totals / counts, onehot.T, precision=largest_value)


def symmetric(matrix):
    return 0.5 * (matrix + matrix.T)


def product(left, right):
    return jnp.dot(left, right, precision=largest_value)


def cross(left, right):
    return lax.dot_general(left, right, (((1,), (1,)), ((), ())), precision=largest_value)


def solve_spd(matrix, target):
    factor = jnp.linalg.cholesky(matrix)
    inner = lax.linalg.triangular_solve(factor, target, left_side=True, lower=True)
    return lax.linalg.triangular_solve(factor, inner, left_side=True, lower=True, transpose_a=True)


def everyone(rows, axis, size):
    copies = jnp.broadcast_to(rows[None], (size,) + rows.shape)
    return lax.all_to_all(copies, axis, 0, 0, tiled=True)


def local(tiles, tile_rows, tile_firms, worker_ids, sign_words, regular):
    probe_dev = sign_words.shape[0]
    firms = lax.axis_size("firm")
    workers = lax.axis_size("worker")
    probes = lax.axis_size("probe")
    blocks = firms * workers
    row_ids = tile_rows[0]
    firm_ids = tile_firms[0]
    worker_row = worker_ids[0]
    places = (firm_ids % workers) * firms + firm_ids // workers
    place_hot = (places[None, :] == jnp.arange(blocks)[:, None]).astype(jnp.float32)
    row_hot = (row_ids[None, :] == jnp.arange(ROWB_DEV)[:, None]).astype(jnp.float32)
    reg_own = lax.dynamic_slice_in_dim(regular, lax.axis_index("worker") * TILE, TILE)[None, :]

    def adjoint(demeaned):
        feature_blocks = demeaned.reshape(probe_dev, ROWB_DEV, TILE)[:, row_ids]
        block_products = jnp.einsum(
            "wqx,qxk->qwk", feature_blocks, tiles, preferred_element_type=jnp.float32
        )
        return jnp.einsum("gt,tpf->gpf", place_hot, block_products, precision=largest_value)

    def forward(collected):
        block_products = jnp.einsum(
            "awl,agl->awg", collected[places], tiles, preferred_element_type=jnp.float32
        )
        summed = jnp.einsum(
            "bt,tpr->pbr", row_hot, block_products, precision=largest_value
        ).reshape(probe_dev, ROWS_DEV)
        return demean(summed, worker_row)

    def owner_total(parts, extra):
        kept = firms * probe_dev
        chunk = parts.reshape(workers, kept, TILE)
        if extra is not None:
            added = extra.shape[0]
            chunk = jnp.concatenate(
                [chunk, jnp.broadcast_to(extra[None], (workers, added, TILE))], axis=1
            )
        got = jnp.sum(lax.all_to_all(chunk, "worker", 0, 0, tiled=True), axis=0)
        chunk = got[:kept].reshape(firms, probe_dev, TILE)
        if extra is not None:
            chunk = jnp.concatenate(
                [chunk, jnp.broadcast_to(got[None, kept:], (firms, added, TILE))], axis=1
            )
        return jnp.sum(lax.all_to_all(chunk, "firm", 0, 0, tiled=True), axis=0)

    def collect(own):
        rounded = own.astype(jnp.bfloat16)
        column = everyone(rounded, "firm", firms)
        return everyone(column, "worker", workers).reshape(blocks, probe_dev, TILE)

    signs_demeaned = demean(unpack_signs(sign_words), worker_row).astype(jnp.bfloat16)
    first = owner_total(adjoint(signs_demeaned), None)

    first_rows = forward(collect(first))
    above = jnp.sum(first_rows * first_rows, axis=1) + jnp.sum(first * first * reg_own, axis=1)
    below = jnp.sum(first * first, axis=1)
    lane = jnp.arange(TILE)[None, :]
    extra = jnp.where(lane < TILE // 2, above[:, None], below[:, None])
    got = owner_total(adjoint(first_rows.astype(jnp.bfloat16)), extra)
    quotient = got[probe_dev:, :1] / got[probe_dev:, TILE // 2 : TILE // 2 + 1]
    second = first - (got[:probe_dev] + reg_own * first) / quotient

    second_rows = forward(collect(second))
    mine = jnp.concatenate([first, second], axis=0)
    mine_rows = jnp.concatenate([first_rows, second_rows], axis=0)
    sent = jnp.concatenate(
        [mine, jnp.transpose(mine_rows.reshape(-1, ROWB_DEV, TILE), (1, 0, 2)).reshape(-1, TILE)],
        axis=0,
    )
    given = everyone(sent, "probe", probes)
    given = given.reshape(probes, 1 + ROWB_DEV, 2, probe_dev, TILE)
    total = probes * probe_dev
    basis = jnp.transpose(given[:, 0], (1, 0, 2, 3)).reshape(2 * total, TILE)
    basis_rows = jnp.transpose(given[:, 1:], (2, 0, 3, 1, 4)).reshape(2 * total, ROWS_DEV)
    grams = cross(mine, basis)
    mapped_grams = cross(mine_rows, basis_rows) + cross(mine * reg_own, basis)
    extra = jnp.concatenate([grams, mapped_grams], axis=1)
    got = owner_total(adjoint(second_rows.astype(jnp.bfloat16)), extra)
    third = got[:probe_dev] + reg_own * second

    given = everyone(jnp.concatenate([third, got[probe_dev:]], axis=0), "probe", probes)
    given = given.reshape(probes, 3, probe_dev, TILE)
    third_all = given[:, 0].reshape(total, TILE)
    tables = jnp.transpose(given[:, 1:], (1, 0, 2, 3)).reshape(2 * total, TILE)
    grams = symmetric(tables[:, : 2 * total])
    mapped_grams = symmetric(tables[:, 2 * total :])
    current = grams[:total, :total]
    curvature = mapped_grams[:total, :total]
    scale = (jnp.diagonal(curvature) / jnp.diagonal(current))[None, :]
    step_first = solve_spd(curvature, current)
    onto_second = step_first.T * scale
    onto_first = jnp.eye(total) - onto_second
    residual_mix = jnp.concatenate([onto_first, onto_second], axis=1)
    following = symmetric(cross(product(residual_mix, grams), residual_mix))
    carry_mix = solve_spd(current, following)
    direction_mix = jnp.concatenate([onto_first + carry_mix.T, onto_second], axis=1)
    curvature = symmetric(cross(product(direction_mix, mapped_grams), direction_mix))
    step_second = solve_spd(curvature, following)
    begin = lax.axis_index("probe") * probe_dev
    first_own = lax.dynamic_slice_in_dim(step_first, begin, probe_dev, 1).T
    second_own = lax.dynamic_slice_in_dim(step_second, begin, probe_dev, 1).T
    residual_own = lax.dynamic_slice_in_dim(residual_mix, begin, probe_dev, 0)
    moved = product(second_own, direction_mix)
    image = moved[:, :total] * scale
    solution_own = product(moved, basis) + product(first_own, basis[:total])
    residual_own = product(
        residual_own + jnp.concatenate([-image, image], axis=1), basis
    ) - product(moved[:, total:], third_all)
    outs = everyone(jnp.concatenate([solution_own, residual_own], axis=0), "worker", workers)
    outs = jnp.transpose(outs.reshape(workers, 2, probe_dev, TILE), (1, 2, 0, 3))
    outs = outs.reshape(2, probe_dev, workers * TILE)
    return (outs[0], outs[1])


def solution(mesh):
    placed = (
        P(("firm", "worker"), None, None),
        P(("firm", "worker"), None),
        P(("firm", "worker"), None),
        P(("firm", "worker"), None),
        P("probe", ("firm", "worker"), None),
        P("firm"),
    )
    return jax.shard_map(
        local,
        mesh=mesh,
        in_specs=placed,
        out_specs=(P("probe", "firm"), P("probe", "firm")),
        check_vma=False,
    )
```

```python
import jax
import jax.numpy as jnp
from jax import lax
from jax.experimental import pallas as pl
from jax.experimental.pallas import tpu as pltpu
from jax.sharding import PartitionSpec as P

TILE = 128
ROWB_DEV = 4
ROWS_DEV = 512
SHARD_WORKERS = 128
BITS = 30
CHUNKS = 8

largest_value = lax.Precision.HIGHEST
f32 = jnp.float32
bf16 = jnp.bfloat16


def dot(left, right, dims, precision=None):
    return lax.dot_general(
        left, right, ((dims[:1], dims[1:]), ((), ())), precision=precision, preferred_element_type=f32
    )


def exact(left, right, dims):
    return dot(left, right, dims, largest_value)


def three_parts(values):
    high = values.astype(bf16)
    rest = values - high.astype(f32)
    middle = rest.astype(bf16)
    low = (rest - middle.astype(f32)).astype(bf16)
    return high, middle, low


def demean(values, worker_ids):
    probes = values.shape[0]
    workers = lax.broadcasted_iota(jnp.int32, (SHARD_WORKERS, ROWS_DEV), 0)
    onehot = jnp.where(workers == worker_ids, 1.0, 0.0).astype(bf16)
    stacked = jnp.concatenate([*(part.astype(f32) for part in three_parts(values)), jnp.ones_like(values)], axis=0)
    sums = dot(stacked.astype(bf16), onehot, (1, 1))
    totals = (sums[2 * probes : 3 * probes] + sums[probes : 2 * probes]) + sums[:probes]
    means = totals / sums[3 * probes :]
    stacked = jnp.concatenate([part.astype(f32) for part in three_parts(means)], axis=0)
    spread = dot(stacked.astype(bf16), onehot, (1, 0))
    return values - ((spread[2 * probes : 3 * probes] + spread[probes : 2 * probes]) + spread[:probes])


def tile_copy(tiles_hbm, tiles, arrived, chunk):
    size = tiles.shape[0] // CHUNKS
    part = pl.ds(chunk * size, size)
    return pltpu.make_async_copy(tiles_hbm.at[part], tiles.at[part], arrived.at[chunk])


def forward(tile_rows, tile_firms, field, tiles, total, copies, workers, firms):
    size = tiles.shape[0] // CHUNKS
    total[...] = jnp.zeros_like(total)

    def chunk_step(chunk, carry):
        copies(chunk)
        for item in range(size):
            tile = chunk * size + item
            firm = tile_firms[0, tile]
            place = lax.rem(firm, workers) * firms + lax.div(firm, workers)
            image = dot(field[place], tiles[tile], (1, 1))
            row = tile_rows[0, tile]
            total[row] = total[row] + image
        return carry

    lax.fori_loop(0, CHUNKS, chunk_step, 0)


def adjoint(tile_rows, tile_firms, rows, tiles, out, copies, workers, stride):
    size = tiles.shape[0] // CHUNKS
    out[...] = jnp.zeros_like(out)

    def chunk_step(chunk, carry):
        copies(chunk)
        for item in range(size):
            tile = chunk * size + item
            firm = tile_firms[0, tile]
            place = lax.rem(firm, workers) * stride + lax.div(firm, workers)
            image = dot(rows[tile_rows[0, tile]], tiles[tile], (1, 0))
            out[place] = out[place] + image
        return carry

    lax.fori_loop(0, CHUNKS, chunk_step, 0)


def put_rows(rows, values):
    for block in range(ROWB_DEV):
        rows[block] = values[:, block * TILE : (block + 1) * TILE].astype(bf16)


def take_rows(total):
    return jnp.concatenate([total[block] for block in range(ROWB_DEV)], axis=1)


def start_body(workers, firms, tile_rows, tile_firms, words, worker_ids, tiles_hbm, out, tiles, rows, arrived):
    for chunk in range(CHUNKS):
        tile_copy(tiles_hbm, tiles, arrived, chunk).start()
    probes = words.shape[0]
    lanes = lax.broadcasted_iota(jnp.int32, (probes, TILE), 1)
    signs = []
    for block in range(ROWB_DEV):
        block_words = words[:, block, :]
        chosen = jnp.zeros((probes, TILE), jnp.int32)
        bit = lanes
        for word in range(block_words.shape[1]):
            here = (lanes >= word * BITS) & (lanes < (word + 1) * BITS)
            chosen = jnp.where(here, jnp.broadcast_to(block_words[:, word : word + 1], (probes, TILE)), chosen)
            bit = jnp.where(here, lanes - word * BITS, bit)
        signs.append((2 * (lax.shift_right_logical(chosen, bit) & 1) - 1).astype(f32))
    put_rows(rows, demean(jnp.concatenate(signs, axis=1), worker_ids[...]))
    wait = lambda chunk: tile_copy(tiles_hbm, tiles, arrived, chunk).wait()
    adjoint(tile_rows, tile_firms, rows, tiles, out, wait, workers, firms)


def middle_body(
    workers, firms, tile_rows, tile_firms, index, field, first, regular, worker_ids, tiles_hbm,
    out, tiles, rows, total, arrived,
):
    for chunk in range(CHUNKS):
        tile_copy(tiles_hbm, tiles, arrived, chunk).start()
    wait = lambda chunk: tile_copy(tiles_hbm, tiles, arrived, chunk).wait()
    forward(tile_rows, tile_firms, field, tiles, total, wait, workers, firms)
    values = demean(take_rows(total), worker_ids[...])
    put_rows(rows, values)
    adjoint(tile_rows, tile_firms, rows, tiles, out, lambda chunk: None, workers, firms + 1)
    own = first[...]
    squares = own * own
    above = jnp.sum(values * values, axis=1, keepdims=True)
    above = above + jnp.sum(squares * regular[pl.ds(index[0], 1), :], axis=1, keepdims=True)
    below = jnp.sum(squares, axis=1, keepdims=True)
    lanes = lax.broadcasted_iota(jnp.int32, own.shape, 1)
    extra = jnp.where(lanes < TILE // 2, above, below)
    for worker in range(workers):
        out[worker * (firms + 1) + firms] = extra


def rows_body(
    workers, firms, tile_rows, tile_firms, field, first, second, quotient, worker_ids, tiles_hbm,
    out, tiles, total, arrived,
):
    for chunk in range(CHUNKS):
        tile_copy(tiles_hbm, tiles, arrived, chunk).start()
    wait = lambda chunk: tile_copy(tiles_hbm, tiles, arrived, chunk).wait()
    forward(tile_rows, tile_firms, field, tiles, total, wait, workers, firms)
    values = demean(take_rows(total), worker_ids[...])
    for probe in range(out.shape[0]):
        out[probe, 0] = first[...]
        out[probe, 1] = second[...]
        out[probe, 2] = quotient[...]
        for block in range(ROWB_DEV):
            out[probe, 3 + block] = values[:, block * TILE : (block + 1) * TILE]


def last_body(
    workers, firms, tile_rows, tile_firms, index, given, regular, tiles_hbm, out, tiles, rows, arrived
):
    for chunk in range(CHUNKS):
        tile_copy(tiles_hbm, tiles, arrived, chunk).start()
    gather = lambda item: jnp.concatenate([given[probe, item] for probe in range(given.shape[0])], axis=0)
    own = lambda item: given[index[1], item]
    first, second = own(0), own(1)
    first_all, second_all = gather(0), gather(1)
    images = exact(second * regular[pl.ds(index[0], 1), :], second_all, (1, 1))
    for block in range(ROWB_DEV):
        mine = own(3 + block)
        rows[block] = mine.astype(bf16)
        images = images + exact(mine, gather(3 + block), (1, 1))
    extra = jnp.concatenate(
        [
            exact(first, first_all, (1, 1)),
            exact(first, second_all, (1, 1)),
            exact(second, second_all, (1, 1)),
            images,
        ],
        axis=1,
    )
    wait = lambda chunk: tile_copy(tiles_hbm, tiles, arrived, chunk).wait()
    adjoint(tile_rows, tile_firms, rows, tiles, out, wait, workers, firms + 1)
    for worker in range(workers):
        out[worker * (firms + 1) + firms] = extra


def eliminate(table, pivots):
    size, width = table.shape
    lanes = lax.broadcasted_iota(jnp.int32, (size, width), 1)
    lines = lax.broadcasted_iota(jnp.int32, (size, width), 0)
    for step in range(size):
        line = table[step : step + 1, :]
        column = jnp.broadcast_to(table[:, pivots[0] + step : pivots[0] + step + 1], (size, width))
        pivot = jnp.broadcast_to(line[:, pivots[0] + step : pivots[0] + step + 1], (1, width))
        for begin in pivots[1:]:
            at = begin + step
            column = jnp.where(lanes < begin, column, jnp.broadcast_to(table[:, at : at + 1], (size, width)))
            pivot = jnp.where(lanes[:1] < begin, pivot, jnp.broadcast_to(line[:, at : at + 1], (1, width)))
        line = line / pivot
        table = jnp.where(lines == step, line, table - column * line)
    return table


def final_body(index, given, last, out, scratch):
    size = given.shape[0] * given.shape[2]
    gather = lambda ref, item: jnp.concatenate([ref[probe, item] for probe in range(ref.shape[0])], axis=0)
    lines = lax.broadcasted_iota(jnp.int32, (size, size), 0)
    lanes = lax.broadcasted_iota(jnp.int32, (size, size), 1)
    unit = jnp.where(lines == lanes, 1.0, 0.0)
    turned = lambda matrix: exact(matrix, unit, (0, 0))
    tables = gather(last, 1)
    same = tables[:, :size]
    mixed = tables[:, size : 2 * size]
    other = tables[:, 2 * size : 3 * size]
    other_mapped = tables[:, 3 * size :]
    scale = gather(given, 2)[:, :size]
    current = 0.5 * (same + turned(same))
    other = 0.5 * (other + turned(other))
    other_mapped = 0.5 * (other_mapped + turned(other_mapped))
    same_mapped = scale * turned(current - mixed)
    same_mapped = 0.5 * (same_mapped + turned(same_mapped))
    mixed_mapped = scale * (mixed - other)
    solved = eliminate(jnp.concatenate([same_mapped, current, current, unit], axis=1), (0, 2 * size))
    step_first = solved[:, size : 2 * size]
    inverse = solved[:, 3 * size :]
    onto_second = scale * step_first
    onto_first = unit - onto_second

    def quadratic(upper, lower, one, cross, two):
        top = exact(one, upper, (1, 0)) + exact(cross, lower, (1, 0))
        bottom = exact(cross, upper, (0, 0)) + exact(two, lower, (1, 0))
        value = exact(upper, top, (0, 0)) + exact(lower, bottom, (0, 0))
        return 0.5 * (value + turned(value))

    following = quadratic(onto_first, onto_second, current, mixed, other)
    direction = onto_first + exact(inverse, following, (1, 0))
    curvature = quadratic(direction, onto_second, same_mapped, mixed_mapped, other_mapped)
    step_second = eliminate(jnp.concatenate([curvature, following], axis=1), (0,))[:, size:]
    moved_first = exact(direction, step_second, (1, 0))
    moved_second = exact(onto_second, step_second, (1, 0))
    image = scale * moved_first
    basis = jnp.concatenate([gather(given, 0), gather(given, 1), gather(last, 0)], axis=0)
    scratch[0] = exact(jnp.concatenate([step_first + moved_first, moved_second], axis=0), basis[: 2 * size], (0, 0))
    scratch[1] = exact(
        jnp.concatenate([onto_first - image, onto_second + image, -moved_second], axis=0), basis, (0, 0)
    )
    probes = given.shape[2]
    begin = pl.multiple_of(index[1] * probes, probes)
    for worker in range(out.shape[0]):
        out[worker, 0] = scratch[0, pl.ds(begin, probes), :]
        out[worker, 1] = scratch[1, pl.ds(begin, probes), :]


def kernel(body, shape, places, scratch, name, cost):
    return pl.pallas_call(
        body,
        out_shape=jax.ShapeDtypeStruct(shape, f32),
        in_specs=[pl.BlockSpec(memory_space=place) for place in places],
        out_specs=pl.BlockSpec(memory_space=pltpu.VMEM),
        scratch_shapes=scratch,
        cost_estimate=pl.CostEstimate(flops=cost, transcendentals=0, bytes_accessed=1 << 22),
        name=name,
    )


def exchange(chunks, axis, beside=()):
    chunks, beside = lax.optimization_barrier((chunks, beside))
    got = lax.all_to_all(chunks, axis, 0, 0, tiled=True)
    return lax.optimization_barrier((got, beside))


def copies(rows, size):
    return jnp.broadcast_to(rows[None], (size,) + rows.shape)


def local(tiles, tile_rows, tile_firms, worker_ids, sign_words, regular):
    probe_dev = sign_words.shape[0]
    firms = lax.axis_size("firm")
    workers = lax.axis_size("worker")
    probes = lax.axis_size("probe")
    count = tiles.shape[0]
    reg_blocks = regular.reshape(workers, TILE)
    index = jnp.stack([lax.axis_index("worker"), lax.axis_index("probe")]).astype(jnp.int32)
    reg_own = lax.dynamic_slice_in_dim(reg_blocks, index[0], 1, 0)
    beside = (index, reg_own)

    tiles_vmem = pltpu.VMEM(tiles.shape, bf16)
    rows_vmem = pltpu.VMEM((ROWB_DEV, probe_dev, TILE), bf16)
    total_vmem = pltpu.VMEM((ROWB_DEV, probe_dev, TILE), f32)
    arrived = pltpu.SemaphoreType.DMA((CHUNKS,))
    VMEM, SMEM, ANY = pltpu.VMEM, pltpu.SMEM, pl.ANY
    cost = 2 * count * probe_dev * TILE * TILE

    def owner_total(parts, beside):
        chunk = parts.reshape(workers, -1, TILE)
        got, beside = exchange(chunk, "worker", beside)
        got = jnp.sum(got, axis=0)
        kept = firms * probe_dev
        chunk = got[:kept].reshape(firms, probe_dev, TILE)
        if got.shape[0] > kept:
            chunk = jnp.concatenate([chunk, copies(got[kept:], firms)], axis=1)
        got, beside = exchange(chunk, "firm", beside)
        return jnp.sum(got, axis=0), beside

    def collect(own, beside):
        column, beside = exchange(copies(own.astype(bf16), firms), "firm", beside)
        field, beside = exchange(copies(column, workers), "worker", beside)
        return field.reshape(workers * firms, probe_dev, TILE), beside

    def bind(body):
        return lambda *refs: body(workers, firms, *refs)

    parts = kernel(
        bind(start_body), (workers * firms, probe_dev, TILE), [SMEM, SMEM, VMEM, VMEM, ANY],
        [tiles_vmem, rows_vmem, arrived], "start", cost,
    )(tile_rows, tile_firms, sign_words, worker_ids, tiles)
    first, beside = owner_total(parts, beside)

    field, (first, index, reg_own) = collect(first, (first, *beside))
    parts = kernel(
        bind(middle_body), (workers * (firms + 1), probe_dev, TILE),
        [SMEM, SMEM, SMEM, VMEM, VMEM, VMEM, VMEM, ANY],
        [tiles_vmem, rows_vmem, total_vmem, arrived], "middle", 2 * cost,
    )(tile_rows, tile_firms, index, field, first, reg_blocks, worker_ids, tiles)
    got, (first, index, reg_own) = owner_total(parts, (first, index, reg_own))
    quotient = got[probe_dev:, :1] / got[probe_dev:, TILE // 2 : TILE // 2 + 1]
    second = first - (got[:probe_dev] + reg_own * first) / quotient
    quotient = jnp.broadcast_to(quotient, second.shape)

    field, (first, second, quotient, index, reg_own) = collect(second, (first, second, quotient, index, reg_own))
    sent = kernel(
        bind(rows_body), (probes, 3 + ROWB_DEV, probe_dev, TILE),
        [SMEM, SMEM, VMEM, VMEM, VMEM, VMEM, VMEM, ANY],
        [tiles_vmem, total_vmem, arrived], "rows", cost,
    )(tile_rows, tile_firms, field, first, second, quotient, worker_ids, tiles)
    given, (second, index, reg_own) = exchange(sent, "probe", (second, index, reg_own))
    parts = kernel(
        bind(last_body), (workers * (firms + 1), probe_dev, TILE),
        [SMEM, SMEM, SMEM, VMEM, VMEM, ANY],
        [tiles_vmem, rows_vmem, arrived], "last", cost,
    )(tile_rows, tile_firms, index, given, reg_blocks, tiles)
    got, (second, index, reg_own, given) = owner_total(parts, (second, index, reg_own, given))
    third = got[:probe_dev] + reg_own * second
    sent = jnp.stack([third, got[probe_dev:]], axis=0)
    last, (index, given) = exchange(copies(sent, probes), "probe", (index, given))
    outs = kernel(
        final_body, (workers, 2, probe_dev, TILE), [SMEM, VMEM, VMEM],
        [pltpu.VMEM((2, probes * probe_dev, TILE), f32)], "final", cost // 4,
    )(index, given, last)
    outs, _ = exchange(outs, "worker")
    outs = jnp.transpose(outs, (1, 2, 0, 3)).reshape(2, probe_dev, workers * TILE)
    return (outs[0], outs[1])


def solution(mesh):
    placed = (
        P(("firm", "worker"), None, None),
        P(("firm", "worker"), None),
        P(("firm", "worker"), None),
        P(("firm", "worker"), None),
        P("probe", ("firm", "worker"), None),
        P("firm"),
    )
    return jax.shard_map(
        local,
        mesh=mesh,
        in_specs=placed,
        out_specs=(P("probe", "firm"), P("probe", "firm")),
        check_vma=False,
    )
```

```python
import jax
import jax.numpy as jnp
from jax import lax
from jax.experimental import pallas as pl
from jax.experimental.pallas import tpu as pltpu
from jax.sharding import PartitionSpec as P

TILE = 128
ROWB_DEV = 4
ROWS_DEV = 512
SHARD_WORKERS = 128
BITS = 30
CHUNKS = 8

largest_value = lax.Precision.HIGHEST
f32 = jnp.float32
bf16 = jnp.bfloat16


def dot(left, right, dims, precision=None):
    return lax.dot_general(
        left, right, ((dims[:1], dims[1:]), ((), ())), precision=precision, preferred_element_type=f32
    )


def exact(left, right, dims):
    return dot(left, right, dims, largest_value)


def three_parts(values):
    high = values.astype(bf16)
    rest = values - high.astype(f32)
    middle = rest.astype(bf16)
    low = (rest - middle.astype(f32)).astype(bf16)
    return high, middle, low


def demean(values, worker_ids):
    probes = values.shape[0]
    workers = lax.broadcasted_iota(jnp.int32, (SHARD_WORKERS, ROWS_DEV), 0)
    onehot = jnp.where(workers == worker_ids, 1.0, 0.0).astype(bf16)
    stacked = jnp.concatenate([*(part.astype(f32) for part in three_parts(values)), jnp.ones_like(values)], axis=0)
    sums = dot(stacked.astype(bf16), onehot, (1, 1))
    totals = (sums[2 * probes : 3 * probes] + sums[probes : 2 * probes]) + sums[:probes]
    means = totals / sums[3 * probes :]
    stacked = jnp.concatenate([part.astype(f32) for part in three_parts(means)], axis=0)
    spread = dot(stacked.astype(bf16), onehot, (1, 0))
    return values - ((spread[2 * probes : 3 * probes] + spread[probes : 2 * probes]) + spread[:probes])


def fetch(tiles_hbm, tiles, arrived):
    size = tiles.shape[0] // CHUNKS

    def copy(chunk):
        part = pl.ds(chunk * size, size)
        return pltpu.make_async_copy(tiles_hbm.at[part], tiles.at[part], arrived.at[chunk])

    for chunk in range(CHUNKS):
        copy(chunk).start()
    return lambda chunk: copy(chunk).wait()


def place_of(firm, workers, stride):
    return (firm & (workers - 1)) * stride + (firm >> (workers.bit_length() - 1))


def pair(upper, lower):
    return jnp.concatenate([upper.astype(f32), lower.astype(f32)], axis=0).astype(bf16)


def forward(tile_rows, tile_firms, field, tiles, workers, firms, wait):
    total = None
    size = tiles.shape[0] // CHUNKS
    for tile in range(0, tiles.shape[0], 2):
        if tile % size == 0:
            wait(tile // size)
        pieces = [field[place_of(tile_firms[0, tile + item], workers, firms)] for item in range(2)]
        probes = pieces[0].shape[0]
        weights = jnp.concatenate([tiles[tile], tiles[tile + 1]], axis=0)
        both = dot(pair(*pieces), weights, (1, 1))
        if total is None:
            total = [jnp.zeros((probes, TILE), f32) for block in range(ROWB_DEV)]
        for item in range(2):
            image = both[item * probes : (item + 1) * probes, item * TILE : (item + 1) * TILE]
            row = tile_rows[0, tile + item]
            total = [old + jnp.where(row == block, image, 0.0) for block, old in enumerate(total)]
    return total


def adjoint(tile_rows, tile_firms, rows, tiles, out, workers, stride, wait=None):
    out[...] = jnp.zeros_like(out)
    probes = rows.shape[1]
    size = tiles.shape[0] // CHUNKS
    for tile in range(0, tiles.shape[0], 2):
        if wait is not None and tile % size == 0:
            wait(tile // size)
        pieces = [rows[tile_rows[0, tile + item]] for item in range(2)]
        weights = jnp.concatenate([tiles[tile], tiles[tile + 1]], axis=1)
        both = dot(pair(*pieces), weights, (1, 0))
        for item in range(2):
            image = both[item * probes : (item + 1) * probes, item * TILE : (item + 1) * TILE]
            place = place_of(tile_firms[0, tile + item], workers, stride)
            out[place] = out[place] + image


def put_rows(rows, values):
    for block in range(ROWB_DEV):
        rows[block] = values[:, block * TILE : (block + 1) * TILE].astype(bf16).astype(f32)


def add_ridge(out, place, regular, worker, own):
    out[place] = out[place] + regular[pl.ds(worker, 1), :] * own


def start_body(workers, firms, tile_rows, tile_firms, words, worker_ids, tiles_hbm, out, tiles, rows, arrived):
    wait = fetch(tiles_hbm, tiles, arrived)
    words_row, blocks, probes = words.shape
    lanes = lax.broadcasted_iota(jnp.int32, (probes, TILE), 1)
    lines = lax.broadcasted_iota(jnp.int32, (probes, TILE), 0)
    word_of = lax.div(lanes, jnp.int32(BITS))
    bit = lanes - word_of * BITS
    chosen = [jnp.zeros((probes, TILE), jnp.int32) for block in range(blocks)]
    for word in range(words_row):
        for probe in range(probes):
            here = (word_of == word) & (lines == probe)
            chosen = [jnp.where(here, words[word, block, probe], old) for block, old in enumerate(chosen)]
    signs = [(2 * (lax.shift_right_logical(old, bit) & 1) - 1).astype(f32) for old in chosen]
    put_rows(rows, demean(jnp.concatenate(signs, axis=1), worker_ids[...]))
    adjoint(tile_rows, tile_firms, rows, tiles, out, workers, firms, wait)


def middle_body(
    workers, firms, tile_rows, tile_firms, worker, firm, field, first, regular, worker_ids, tiles_hbm,
    out, tiles, rows, arrived,
):
    wait = fetch(tiles_hbm, tiles, arrived)
    total = forward(tile_rows, tile_firms, field, tiles, workers, firms, wait)
    values = demean(jnp.concatenate(total, axis=1), worker_ids[...])
    put_rows(rows, values)
    adjoint(tile_rows, tile_firms, rows, tiles, out, workers, firms + 1)
    own = first[...]
    add_ridge(out, worker[0] * (firms + 1) + firm[0], regular, worker[0], own)
    squares = own * own
    above = jnp.sum(values * values, axis=1, keepdims=True)
    above = above + jnp.sum(squares * regular[pl.ds(worker[0], 1), :], axis=1, keepdims=True)
    below = jnp.sum(squares, axis=1, keepdims=True)
    lanes = lax.broadcasted_iota(jnp.int32, own.shape, 1)
    extra = jnp.where(lanes < TILE // 2, above, below)
    for other in range(workers):
        out[other * (firms + 1) + firms] = extra


def rows_body(
    workers, firms, tile_rows, tile_firms, field, first, second, quotient, worker_ids, tiles_hbm,
    out, tiles, rows, arrived,
):
    wait = fetch(tiles_hbm, tiles, arrived)
    total = forward(tile_rows, tile_firms, field, tiles, workers, firms, wait)
    values = demean(jnp.concatenate(total, axis=1), worker_ids[...])
    for probe in range(out.shape[0]):
        out[probe, 0] = first[...]
        out[probe, 1] = second[...]
        out[probe, 2] = quotient[...]
        for block in range(ROWB_DEV):
            out[probe, 3 + block] = values[:, block * TILE : (block + 1) * TILE]


def last_body(
    workers, firms, tile_rows, tile_firms, worker, firm, probe, given, regular, tiles_hbm,
    out, tiles, rows, arrived,
):
    wait = fetch(tiles_hbm, tiles, arrived)
    gather = lambda item: jnp.concatenate([given[other, item] for other in range(given.shape[0])], axis=0)
    own = lambda item: given[probe[0], item]
    first, second = own(0), own(1)
    first_all, second_all = gather(0), gather(1)
    mine = [own(3 + block) for block in range(ROWB_DEV)]
    for block in range(ROWB_DEV):
        rows[block] = mine[block].astype(bf16).astype(f32)
    adjoint(tile_rows, tile_firms, rows, tiles, out, workers, firms + 1, wait)
    add_ridge(out, worker[0] * (firms + 1) + firm[0], regular, worker[0], second)
    left = jnp.concatenate([*mine, second * regular[pl.ds(worker[0], 1), :]], axis=1)
    right = jnp.concatenate([*(gather(3 + block) for block in range(ROWB_DEV)), second_all], axis=1)
    extra = jnp.concatenate(
        [
            exact(first, first_all, (1, 1)),
            exact(first, second_all, (1, 1)),
            exact(second, second_all, (1, 1)),
            exact(left, right, (1, 1)),
        ],
        axis=1,
    )
    for other in range(workers):
        out[other * (firms + 1) + firms] = extra


def eliminate(table, pivots):
    size, width = table.shape
    lanes = lax.broadcasted_iota(jnp.int32, (size, width), 1)
    lines = lax.broadcasted_iota(jnp.int32, (size, width), 0)

    def spread(at):
        column = jnp.broadcast_to(table[:, pivots[0] + at : pivots[0] + at + 1], (size, width))
        for begin in pivots[1:]:
            other = jnp.broadcast_to(table[:, begin + at : begin + at + 1], (size, width))
            column = jnp.where(lanes < begin, column, other)
        return column

    for step in range(0, size, 2):
        one, two = spread(step), spread(step + 1)
        first, second = table[step : step + 1, :], table[step + 1 : step + 2, :]
        a, b = one[step : step + 1, :], two[step : step + 1, :]
        c, d = one[step + 1 : step + 2, :], two[step + 1 : step + 2, :]
        inverse = 1.0 / (a * d - b * c)
        upper = (d * first - b * second) * inverse
        lower = (a * second - c * first) * inverse
        table = table - one * upper - two * lower
        table = jnp.where(lines == step, upper, jnp.where(lines == step + 1, lower, table))
    return table


def final_body(probe, given, last, out, scratch):
    size = given.shape[0] * given.shape[2]
    gather = lambda ref, item: jnp.concatenate([ref[other, item] for other in range(ref.shape[0])], axis=0)
    half = lambda matrix: 0.5 * (matrix + matrix.T)
    lines = lax.broadcasted_iota(jnp.int32, (size, size), 0)
    lanes = lax.broadcasted_iota(jnp.int32, (size, size), 1)
    unit = jnp.where(lines == lanes, 1.0, 0.0)
    tables = gather(last, 1)
    current = half(tables[:, :size])
    mixed = tables[:, size : 2 * size]
    other = tables[:, 2 * size : 3 * size]
    other_mapped = tables[:, 3 * size :]
    scale = gather(given, 2)[:, :size]
    same_mapped = half(scale * (current - mixed).T)
    mixed_mapped = scale * (mixed - other)

    def whole(one, cross, two):
        return jnp.concatenate(
            [jnp.concatenate([one, cross], axis=1), jnp.concatenate([cross.T, two], axis=1)], axis=0
        )

    grams = whole(current, mixed, other)
    mapped_grams = whole(same_mapped, mixed_mapped, other_mapped)
    solved = eliminate(jnp.concatenate([same_mapped, current, current, unit], axis=1), (0, 2 * size))
    step_first = solved[:, size : 2 * size]
    inverse = solved[:, 3 * size :]
    onto_second = scale * step_first
    onto_first = unit - onto_second
    mix = jnp.concatenate([onto_first, onto_second], axis=0)
    following = half(exact(mix, exact(grams, mix, (1, 0)), (0, 0)))
    direction = onto_first + exact(inverse, following, (1, 0))
    mix = jnp.concatenate([direction, onto_second], axis=0)
    curvature = half(exact(mix, exact(mapped_grams, mix, (1, 0)), (0, 0)))
    step_second = eliminate(jnp.concatenate([curvature, following], axis=1), (0,))[:, size:]
    moved = exact(mix, step_second, (1, 0))
    moved_first, moved_second = moved[:size], moved[size:]
    image = scale * moved_first
    basis = jnp.concatenate([gather(given, 0), gather(given, 1), gather(last, 0)], axis=0)
    scratch[0] = exact(jnp.concatenate([step_first + moved_first, moved_second], axis=0), basis[: 2 * size], (0, 0))
    scratch[1] = exact(
        jnp.concatenate([onto_first - image, onto_second + image, -moved_second], axis=0), basis, (0, 0)
    )
    probes = given.shape[2]
    begin = pl.multiple_of(probe[0] * probes, probes)
    for worker in range(out.shape[0]):
        out[worker, 0] = scratch[0, pl.ds(begin, probes), :]
        out[worker, 1] = scratch[1, pl.ds(begin, probes), :]


def kernel(body, shapes, places, scratch, name, cost):
    return pl.pallas_call(
        body,
        out_shape=shapes,
        in_specs=[pl.BlockSpec(memory_space=place) for place in places],
        out_specs=jax.tree.map(lambda _: pl.BlockSpec(memory_space=pltpu.VMEM), shapes),
        scratch_shapes=scratch,
        compiler_params=pltpu.CompilerParams(vmem_limit_bytes=10 << 20),
        cost_estimate=pl.CostEstimate(flops=cost, transcendentals=0, bytes_accessed=1 << 22),
        name=name,
    )


def exchange(chunks, axis, beside=()):
    chunks, beside = lax.optimization_barrier((chunks, beside))
    got = lax.all_to_all(chunks, axis, 0, 0, tiled=True)
    return lax.optimization_barrier((got, beside))


def copies(rows, size):
    return jnp.broadcast_to(rows[None], (size,) + rows.shape)


def local(tiles, tile_rows, tile_firms, worker_ids, sign_words, regular):
    probe_dev = sign_words.shape[0]
    firms = lax.axis_size("firm")
    workers = lax.axis_size("worker")
    probes = lax.axis_size("probe")
    count = tiles.shape[0]
    reg_blocks = regular.reshape(workers, TILE)
    words = jnp.transpose(sign_words, (2, 1, 0))
    at = tuple(lax.axis_index(axis).reshape(1) for axis in ("firm", "worker", "probe"))

    VMEM, SMEM, HBM = pltpu.VMEM, pltpu.SMEM, pltpu.HBM
    scratch = [
        VMEM(tiles.shape, bf16), VMEM((ROWB_DEV, probe_dev, TILE), f32), pltpu.SemaphoreType.DMA((CHUNKS,))
    ]
    cost = 2 * count * probe_dev * TILE * TILE
    tiles = pltpu.with_memory_space_constraint(tiles, HBM)

    def shape(*dims):
        return jax.ShapeDtypeStruct(dims, f32)

    def owner_total(parts, beside):
        chunk = parts.reshape(workers, -1, TILE)
        got, beside = exchange(chunk, "worker", beside)
        got = jnp.sum(got, axis=0)
        kept = firms * probe_dev
        chunk = got[:kept].reshape(firms, probe_dev, TILE)
        if got.shape[0] > kept:
            chunk = jnp.concatenate([chunk, copies(got[kept:], firms)], axis=1)
        got, beside = exchange(chunk, "firm", beside)
        return jnp.sum(got, axis=0), beside

    def collect(own, beside):
        column, beside = exchange(copies(own.astype(bf16), firms), "firm", beside)
        field, beside = exchange(copies(column, workers), "worker", beside)
        return field.reshape(workers * firms, probe_dev, TILE), beside

    def bind(body):
        return lambda *refs: body(workers, firms, *refs)

    parts = kernel(
        bind(start_body), shape(workers * firms, probe_dev, TILE),
        [SMEM, SMEM, SMEM, VMEM, HBM], scratch, "start", cost,
    )(tile_rows, tile_firms, words, worker_ids, tiles)
    first, at = owner_total(parts, at)

    field, (first, *at) = collect(first, (first, *at))
    firm, worker, _ = at
    parts = kernel(
        bind(middle_body), shape(workers * (firms + 1), probe_dev, TILE),
        [SMEM, SMEM, SMEM, SMEM, VMEM, VMEM, VMEM, VMEM, HBM], scratch, "middle", 2 * cost,
    )(tile_rows, tile_firms, worker, firm, field, first, reg_blocks, worker_ids, tiles)
    got, (first, *at) = owner_total(parts, (first, *at))
    quotient = got[probe_dev:, :1] / got[probe_dev:, TILE // 2 : TILE // 2 + 1]
    quotient = jnp.broadcast_to(quotient, first.shape)
    second = first - got[:probe_dev] / quotient

    field, (first, second, quotient, *at) = collect(second, (first, second, quotient, *at))
    sent = kernel(
        bind(rows_body), shape(probes, 3 + ROWB_DEV, probe_dev, TILE),
        [SMEM, SMEM, VMEM, VMEM, VMEM, VMEM, VMEM, HBM], scratch, "rows", cost,
    )(tile_rows, tile_firms, field, first, second, quotient, worker_ids, tiles)
    given, at = exchange(sent, "probe", at)
    firm, worker, probe = at
    parts = kernel(
        bind(last_body), shape(workers * (firms + 1), probe_dev, TILE),
        [SMEM, SMEM, SMEM, SMEM, SMEM, VMEM, VMEM, HBM], scratch, "last", cost,
    )(tile_rows, tile_firms, worker, firm, probe, given, reg_blocks, tiles)
    got, (given, *at) = owner_total(parts, (given, *at))
    sent = copies(got.reshape(2, probe_dev, TILE), probes)
    last, (given, *at) = exchange(sent, "probe", (given, *at))
    outs = kernel(
        final_body, shape(workers, 2, probe_dev, TILE), [SMEM, VMEM, VMEM],
        [VMEM((2, probes * probe_dev, TILE), f32)], "final", cost // 4,
    )(at[2], given, last)
    outs, _ = exchange(outs, "worker")
    outs = jnp.transpose(outs, (1, 2, 0, 3)).reshape(2, probe_dev, workers * TILE)
    return (outs[0], outs[1])


def solution(mesh):
    placed = (
        P(("firm", "worker"), None, None),
        P(("firm", "worker"), None),
        P(("firm", "worker"), None),
        P(("firm", "worker"), None),
        P("probe", ("firm", "worker"), None),
        P("firm"),
    )
    return jax.shard_map(
        local,
        mesh=mesh,
        in_specs=placed,
        out_specs=(P("probe", "firm"), P("probe", "firm")),
        check_vma=False,
    )
```

```python
import jax
import jax.numpy as jnp
from jax import lax
from jax.experimental import pallas as pl
from jax.experimental.pallas import tpu as pltpu
from jax.sharding import PartitionSpec as P

TILE = 128
ROWB_DEV = 4
ROWS_DEV = 512
SHARD_WORKERS = 128
BITS = 30
CHUNKS = 4

largest_value = lax.Precision.HIGHEST
f32 = jnp.float32
bf16 = jnp.bfloat16


def dot(left, right, dims, precision=None):
    return lax.dot_general(
        left, right, ((dims[:1], dims[1:]), ((), ())), precision=precision, preferred_element_type=f32
    )


def exact(left, right, dims):
    return dot(left, right, dims, largest_value)


def three_parts(values):
    high = values.astype(bf16)
    rest = values - high.astype(f32)
    middle = rest.astype(bf16)
    low = (rest - middle.astype(f32)).astype(bf16)
    return high, middle, low


def demean(values, worker_ids):
    probes = values.shape[0]
    workers = lax.broadcasted_iota(jnp.int32, (SHARD_WORKERS, ROWS_DEV), 0)
    onehot = jnp.where(workers == worker_ids, 1.0, 0.0).astype(bf16)
    stacked = jnp.concatenate([*(part.astype(f32) for part in three_parts(values)), jnp.ones_like(values)], axis=0)
    sums = dot(stacked.astype(bf16), onehot, (1, 1))
    totals = (sums[2 * probes : 3 * probes] + sums[probes : 2 * probes]) + sums[:probes]
    means = totals / sums[3 * probes :]
    stacked = jnp.concatenate([part.astype(f32) for part in three_parts(means)], axis=0)
    spread = dot(stacked.astype(bf16), onehot, (1, 0))
    return values - ((spread[2 * probes : 3 * probes] + spread[probes : 2 * probes]) + spread[:probes])


def fetch(tiles_hbm, tiles, arrived, small):
    size = tiles.shape[0] // CHUNKS
    tables = [pltpu.make_async_copy(*both, arrived.at[CHUNKS + item]) for item, both in enumerate(small)]
    for table in tables:
        table.start()

    def copy(chunk):
        part = pl.ds(chunk * size, size)
        return pltpu.make_async_copy(tiles_hbm.at[part], tiles.at[part], arrived.at[chunk])

    for chunk in range(CHUNKS):
        copy(chunk).start()
    for table in tables:
        table.wait()
    return lambda chunk: copy(chunk).wait()


def place_of(firm, workers, stride):
    return (firm & (workers - 1)) * stride + (firm >> (workers.bit_length() - 1))


def pair(upper, lower):
    return jnp.concatenate([upper.astype(f32), lower.astype(f32)], axis=0).astype(bf16)


def forward(tile_rows, tile_firms, field, tiles, workers, firms, wait):
    total = None
    size = tiles.shape[0] // CHUNKS
    for tile in range(0, tiles.shape[0], 2):
        if tile % size == 0:
            wait(tile // size)
        pieces = [field[place_of(tile_firms[0, tile + item], workers, firms)] for item in range(2)]
        probes = pieces[0].shape[0]
        weights = jnp.concatenate([tiles[tile], tiles[tile + 1]], axis=0)
        both = dot(pair(*pieces), weights, (1, 1))
        if total is None:
            total = [jnp.zeros((probes, TILE), f32) for block in range(ROWB_DEV)]
        for item in range(2):
            image = both[item * probes : (item + 1) * probes, item * TILE : (item + 1) * TILE]
            row = tile_rows[0, tile + item]
            total = [old + jnp.where(row == block, image, 0.0) for block, old in enumerate(total)]
    return total


def adjoint(tile_rows, tile_firms, rows, tiles, out, workers, stride, wait=None):
    out[...] = jnp.zeros_like(out)
    probes = rows.shape[1]
    size = tiles.shape[0] // CHUNKS
    for tile in range(0, tiles.shape[0], 2):
        if wait is not None and tile % (2 * size) == 0:
            wait(tile // size)
            wait(tile // size + 1)
        pieces = [rows[tile_rows[0, tile + item]] for item in range(2)]
        weights = jnp.concatenate([tiles[tile], tiles[tile + 1]], axis=1)
        both = dot(pair(*pieces), weights, (1, 0))
        for item in range(2):
            image = both[item * probes : (item + 1) * probes, item * TILE : (item + 1) * TILE]
            place = place_of(tile_firms[0, tile + item], workers, stride)
            out[place] = out[place] + image


def put_rows(rows, values):
    for block in range(ROWB_DEV):
        rows[block] = values[:, block * TILE : (block + 1) * TILE].astype(bf16).astype(f32)


def add_ridge(out, place, regular, worker, own):
    out[place] = out[place] + regular[pl.ds(worker, 1), :] * own


def start_body(
    workers, firms, rows_hbm, firms_hbm, words_hbm, ids_hbm, tiles_hbm,
    out, tiles, rows, arrived, tile_rows, tile_firms, words, worker_ids,
):
    small = [(rows_hbm, tile_rows), (firms_hbm, tile_firms), (words_hbm, words), (ids_hbm, worker_ids)]
    wait = fetch(tiles_hbm, tiles, arrived, small)
    words_row, blocks, probes = words.shape
    lanes = lax.broadcasted_iota(jnp.int32, (probes, TILE), 1)
    lines = lax.broadcasted_iota(jnp.int32, (probes, TILE), 0)
    word_of = lax.div(lanes, jnp.int32(BITS))
    bit = lanes - word_of * BITS
    chosen = [jnp.zeros((probes, TILE), jnp.int32) for block in range(blocks)]
    for word in range(words_row):
        for probe in range(probes):
            here = (word_of == word) & (lines == probe)
            chosen = [jnp.where(here, words[word, block, probe], old) for block, old in enumerate(chosen)]
    signs = [(2 * (lax.shift_right_logical(old, bit) & 1) - 1).astype(f32) for old in chosen]
    put_rows(rows, demean(jnp.concatenate(signs, axis=1), worker_ids[...]))
    adjoint(tile_rows, tile_firms, rows, tiles, out, workers, firms, wait)


def middle_body(
    workers, firms, rows_hbm, firms_hbm, worker, firm, field, first, regular, worker_ids, tiles_hbm,
    out, tiles, rows, arrived, tile_rows, tile_firms,
):
    wait = fetch(tiles_hbm, tiles, arrived, [(rows_hbm, tile_rows), (firms_hbm, tile_firms)])
    total = forward(tile_rows, tile_firms, field, tiles, workers, firms, wait)
    values = demean(jnp.concatenate(total, axis=1), worker_ids[...])
    put_rows(rows, values)
    adjoint(tile_rows, tile_firms, rows, tiles, out, workers, firms + 1)
    own = first[...]
    add_ridge(out, worker[0] * (firms + 1) + firm[0], regular, worker[0], own)
    squares = own * own
    above = jnp.sum(values * values, axis=1, keepdims=True)
    above = above + jnp.sum(squares * regular[pl.ds(worker[0], 1), :], axis=1, keepdims=True)
    below = jnp.sum(squares, axis=1, keepdims=True)
    lanes = lax.broadcasted_iota(jnp.int32, own.shape, 1)
    extra = jnp.where(lanes < TILE // 2, above, below)
    for other in range(workers):
        out[other * (firms + 1) + firms] = extra


def rows_body(
    workers, firms, rows_hbm, firms_hbm, field, first, second, quotient, worker_ids, tiles_hbm,
    out, tiles, rows, arrived, tile_rows, tile_firms,
):
    wait = fetch(tiles_hbm, tiles, arrived, [(rows_hbm, tile_rows), (firms_hbm, tile_firms)])
    total = forward(tile_rows, tile_firms, field, tiles, workers, firms, wait)
    values = demean(jnp.concatenate(total, axis=1), worker_ids[...])
    for probe in range(out.shape[0]):
        out[probe, 0] = first[...]
        out[probe, 1] = second[...]
        out[probe, 2] = quotient[...]
        for block in range(ROWB_DEV):
            out[probe, 3 + block] = values[:, block * TILE : (block + 1) * TILE]


def last_body(
    workers, firms, rows_hbm, firms_hbm, worker, firm, probe, given, regular, tiles_hbm,
    out, tiles, rows, arrived, tile_rows, tile_firms,
):
    wait = fetch(tiles_hbm, tiles, arrived, [(rows_hbm, tile_rows), (firms_hbm, tile_firms)])
    gather = lambda item: jnp.concatenate([given[other, item] for other in range(given.shape[0])], axis=0)
    own = lambda item: given[probe[0], item]
    first, second = own(0), own(1)
    first_all, second_all = gather(0), gather(1)
    mine = [own(3 + block) for block in range(ROWB_DEV)]
    for block in range(ROWB_DEV):
        rows[block] = mine[block].astype(bf16).astype(f32)
    left = jnp.concatenate([*mine, second * regular[pl.ds(worker[0], 1), :]], axis=1)
    right = jnp.concatenate([*(gather(3 + block) for block in range(ROWB_DEV)), second_all], axis=1)
    extra = jnp.concatenate(
        [
            exact(first, first_all, (1, 1)),
            exact(first, second_all, (1, 1)),
            exact(second, second_all, (1, 1)),
            exact(left, right, (1, 1)),
        ],
        axis=1,
    )
    adjoint(tile_rows, tile_firms, rows, tiles, out, workers, firms + 1, wait)
    add_ridge(out, worker[0] * (firms + 1) + firm[0], regular, worker[0], second)
    for other in range(workers):
        out[other * (firms + 1) + firms] = extra


def eliminate(table, pivots):
    size, width = table.shape
    lanes = lax.broadcasted_iota(jnp.int32, (size, width), 1)
    lines = lax.broadcasted_iota(jnp.int32, (size, width), 0)

    def spread(at):
        column = jnp.broadcast_to(table[:, pivots[0] + at : pivots[0] + at + 1], (size, width))
        for begin in pivots[1:]:
            other = jnp.broadcast_to(table[:, begin + at : begin + at + 1], (size, width))
            column = jnp.where(lanes < begin, column, other)
        return column

    for step in range(0, size, 2):
        one, two = spread(step), spread(step + 1)
        first, second = table[step : step + 1, :], table[step + 1 : step + 2, :]
        a, b = one[step : step + 1, :], two[step : step + 1, :]
        c, d = one[step + 1 : step + 2, :], two[step + 1 : step + 2, :]
        inverse = 1.0 / (a * d - b * c)
        upper = (d * first - b * second) * inverse
        lower = (a * second - c * first) * inverse
        table = table - one * upper - two * lower
        table = jnp.where(lines == step, upper, jnp.where(lines == step + 1, lower, table))
    return table


def final_body(probe, given, last, out, scratch):
    size = given.shape[0] * given.shape[2]
    gather = lambda ref, item: jnp.concatenate([ref[other, item] for other in range(ref.shape[0])], axis=0)
    half = lambda matrix: 0.5 * (matrix + matrix.T)
    lines = lax.broadcasted_iota(jnp.int32, (size, size), 0)
    lanes = lax.broadcasted_iota(jnp.int32, (size, size), 1)
    unit = jnp.where(lines == lanes, 1.0, 0.0)
    tables = gather(last, 1)
    current = half(tables[:, :size])
    mixed = tables[:, size : 2 * size]
    other = tables[:, 2 * size : 3 * size]
    other_mapped = tables[:, 3 * size :]
    scale = gather(given, 2)[:, :size]
    same_mapped = half(scale * (current - mixed).T)
    mixed_mapped = scale * (mixed - other)

    def whole(one, cross, two):
        return jnp.concatenate(
            [jnp.concatenate([one, cross], axis=1), jnp.concatenate([cross.T, two], axis=1)], axis=0
        )

    grams = whole(current, mixed, other)
    mapped_grams = whole(same_mapped, mixed_mapped, other_mapped)
    solved = eliminate(jnp.concatenate([same_mapped, current, current, unit], axis=1), (0, 2 * size))
    step_first = solved[:, size : 2 * size]
    inverse = solved[:, 3 * size :]
    onto_second = scale * step_first
    onto_first = unit - onto_second
    mix = jnp.concatenate([onto_first, onto_second], axis=0)
    following = half(exact(mix, exact(grams, mix, (1, 0)), (0, 0)))
    direction = onto_first + exact(inverse, following, (1, 0))
    mix = jnp.concatenate([direction, onto_second], axis=0)
    curvature = half(exact(mix, exact(mapped_grams, mix, (1, 0)), (0, 0)))
    step_second = eliminate(jnp.concatenate([curvature, following], axis=1), (0,))[:, size:]
    moved = exact(mix, step_second, (1, 0))
    moved_first, moved_second = moved[:size], moved[size:]
    image = scale * moved_first
    basis = jnp.concatenate([gather(given, 0), gather(given, 1), gather(last, 0)], axis=0)
    scratch[0] = exact(jnp.concatenate([step_first + moved_first, moved_second], axis=0), basis[: 2 * size], (0, 0))
    scratch[1] = exact(
        jnp.concatenate([onto_first - image, onto_second + image, -moved_second], axis=0), basis, (0, 0)
    )
    probes = given.shape[2]
    begin = pl.multiple_of(probe[0] * probes, probes)
    for worker in range(out.shape[0]):
        out[worker, 0] = scratch[0, pl.ds(begin, probes), :]
        out[worker, 1] = scratch[1, pl.ds(begin, probes), :]


def kernel(body, shapes, places, scratch, name, cost):
    return pl.pallas_call(
        body,
        out_shape=shapes,
        in_specs=[pl.BlockSpec(memory_space=place) for place in places],
        out_specs=jax.tree.map(lambda _: pl.BlockSpec(memory_space=pltpu.VMEM), shapes),
        scratch_shapes=scratch,
        compiler_params=pltpu.CompilerParams(vmem_limit_bytes=10 << 20),
        cost_estimate=pl.CostEstimate(flops=cost, transcendentals=0, bytes_accessed=1 << 22),
        name=name,
    )


def exchange(chunks, axis, beside=()):
    chunks, beside = lax.optimization_barrier((chunks, beside))
    got = lax.all_to_all(chunks, axis, 0, 0, tiled=True)
    return lax.optimization_barrier((got, beside))


def copies(rows, size):
    return jnp.broadcast_to(rows[None], (size,) + rows.shape)


def local(tiles, tile_rows, tile_firms, worker_ids, sign_words, regular):
    probe_dev = sign_words.shape[0]
    firms = lax.axis_size("firm")
    workers = lax.axis_size("worker")
    probes = lax.axis_size("probe")
    count = tiles.shape[0]
    reg_blocks = regular.reshape(workers, TILE)
    words = jnp.transpose(sign_words, (2, 1, 0))
    at = tuple(lax.axis_index(axis).reshape(1) for axis in ("firm", "worker", "probe"))

    VMEM, SMEM, HBM = pltpu.VMEM, pltpu.SMEM, pltpu.HBM
    scratch = [
        VMEM(tiles.shape, bf16), VMEM((ROWB_DEV, probe_dev, TILE), f32), pltpu.SemaphoreType.DMA((CHUNKS + 4,)),
        SMEM(tile_rows.shape, jnp.int32), SMEM(tile_firms.shape, jnp.int32),
    ]
    cost = 2 * count * probe_dev * TILE * TILE
    tiles, tile_rows, tile_firms = (
        pltpu.with_memory_space_constraint(array, HBM) for array in (tiles, tile_rows, tile_firms)
    )

    def shape(*dims):
        return jax.ShapeDtypeStruct(dims, f32)

    def owner_total(parts, beside):
        chunk = parts.reshape(workers, -1, TILE)
        got, beside = exchange(chunk, "worker", beside)
        got = jnp.sum(got, axis=0)
        kept = firms * probe_dev
        chunk = got[:kept].reshape(firms, probe_dev, TILE)
        if got.shape[0] > kept:
            chunk = jnp.concatenate([chunk, copies(got[kept:], firms)], axis=1)
        got, beside = exchange(chunk, "firm", beside)
        return jnp.sum(got, axis=0), beside

    def collect(own, beside):
        column, beside = exchange(copies(own.astype(bf16), firms), "firm", beside)
        field, beside = exchange(copies(column, workers), "worker", beside)
        return field.reshape(workers * firms, probe_dev, TILE), beside

    def bind(body):
        return lambda *refs: body(workers, firms, *refs)

    parts = kernel(
        bind(start_body), shape(workers * firms, probe_dev, TILE),
        [HBM] * 5, [*scratch, SMEM(words.shape, jnp.int32), VMEM(worker_ids.shape, jnp.int32)], "start", cost,
    )(
        tile_rows, tile_firms, pltpu.with_memory_space_constraint(words, HBM),
        pltpu.with_memory_space_constraint(worker_ids, HBM), tiles,
    )
    first, at = owner_total(parts, at)

    field, (first, *at) = collect(first, (first, *at))
    firm, worker, _ = at
    parts = kernel(
        bind(middle_body), shape(workers * (firms + 1), probe_dev, TILE),
        [HBM, HBM, SMEM, SMEM, VMEM, VMEM, VMEM, VMEM, HBM], scratch, "middle", 2 * cost,
    )(tile_rows, tile_firms, worker, firm, field, first, reg_blocks, worker_ids, tiles)
    got, (first, *at) = owner_total(parts, (first, *at))
    quotient = got[probe_dev:, :1] / got[probe_dev:, TILE // 2 : TILE // 2 + 1]
    quotient = jnp.broadcast_to(quotient, first.shape)
    second = first - got[:probe_dev] / quotient

    field, (first, second, quotient, *at) = collect(second, (first, second, quotient, *at))
    sent = kernel(
        bind(rows_body), shape(probes, 3 + ROWB_DEV, probe_dev, TILE),
        [HBM, HBM, VMEM, VMEM, VMEM, VMEM, VMEM, HBM], scratch, "rows", cost,
    )(tile_rows, tile_firms, field, first, second, quotient, worker_ids, tiles)
    given, at = exchange(sent, "probe", at)
    firm, worker, probe = at
    parts = kernel(
        bind(last_body), shape(workers * (firms + 1), probe_dev, TILE),
        [HBM, HBM, SMEM, SMEM, SMEM, VMEM, VMEM, HBM], scratch, "last", cost,
    )(tile_rows, tile_firms, worker, firm, probe, given, reg_blocks, tiles)
    got, (given, *at) = owner_total(parts, (given, *at))
    sent = copies(got.reshape(2, probe_dev, TILE), probes)
    last, (given, *at) = exchange(sent, "probe", (given, *at))
    outs = kernel(
        final_body, shape(workers, 2, probe_dev, TILE), [SMEM, VMEM, VMEM],
        [VMEM((2, probes * probe_dev, TILE), f32)], "final", cost // 4,
    )(at[2], given, last)
    outs, _ = exchange(outs, "worker")
    outs = jnp.transpose(outs, (1, 2, 0, 3)).reshape(2, probe_dev, workers * TILE)
    return (outs[0], outs[1])


def solution(mesh):
    placed = (
        P(("firm", "worker"), None, None),
        P(("firm", "worker"), None),
        P(("firm", "worker"), None),
        P(("firm", "worker"), None),
        P("probe", ("firm", "worker"), None),
        P("firm"),
    )
    return jax.shard_map(
        local,
        mesh=mesh,
        in_specs=placed,
        out_specs=(P("probe", "firm"), P("probe", "firm")),
        check_vma=False,
    )
```

```python
import jax
import jax.numpy as jnp
from jax import lax
from jax.experimental import pallas as pl
from jax.experimental.pallas import tpu as pltpu
from jax.sharding import PartitionSpec as P

TILE = 128
ROWB_DEV = 4
ROWS_DEV = 512
SHARD_WORKERS = 128
BITS = 30
CHUNKS = 4

largest_value = lax.Precision.HIGHEST
f32 = jnp.float32
bf16 = jnp.bfloat16


def dot(left, right, dims, precision=None):
    return lax.dot_general(
        left, right, ((dims[:1], dims[1:]), ((), ())), precision=precision, preferred_element_type=f32
    )


def exact(left, right, dims):
    return dot(left, right, dims, largest_value)


def three_parts(values):
    high = values.astype(bf16)
    rest = values - high.astype(f32)
    middle = rest.astype(bf16)
    low = (rest - middle.astype(f32)).astype(bf16)
    return high, middle, low


def demean(values, worker_ids):
    probes = values.shape[0]
    workers = lax.broadcasted_iota(jnp.int32, (SHARD_WORKERS, ROWS_DEV), 0)
    onehot = jnp.where(workers == worker_ids, 1.0, 0.0).astype(bf16)
    stacked = jnp.concatenate([*(part.astype(f32) for part in three_parts(values)), jnp.ones_like(values)], axis=0)
    sums = dot(stacked.astype(bf16), onehot, (1, 1))
    totals = (sums[2 * probes : 3 * probes] + sums[probes : 2 * probes]) + sums[:probes]
    means = totals / sums[3 * probes :]
    stacked = jnp.concatenate([part.astype(f32) for part in three_parts(means)], axis=0)
    spread = dot(stacked.astype(bf16), onehot, (1, 0))
    return values - ((spread[2 * probes : 3 * probes] + spread[probes : 2 * probes]) + spread[:probes])


def fetch(tiles_hbm, tiles, arrived, small):
    size = tiles.shape[0] // CHUNKS

    def copy(chunk):
        part = pl.ds(chunk * size, size)
        return pltpu.make_async_copy(tiles_hbm.at[part], tiles.at[part], arrived.at[chunk])

    tables = fetch_small(arrived, small)
    for chunk in range(CHUNKS):
        copy(chunk).start()
    for table in tables:
        table.wait()
    return lambda chunk: copy(chunk).wait()


def fetch_small(arrived, small):
    tables = [pltpu.make_async_copy(*both, arrived.at[CHUNKS + item]) for item, both in enumerate(small)]
    for table in tables:
        table.start()
    return tables


def place_of(firm, workers, stride):
    return (firm & (workers - 1)) * stride + (firm >> (workers.bit_length() - 1))


def pair(upper, lower):
    return jnp.concatenate([upper.astype(f32), lower.astype(f32)], axis=0).astype(bf16)


def forward(tile_rows, tile_firms, field, tiles, workers, firms):
    total = None
    for tile in range(0, tiles.shape[0], 2):
        pieces = [field[place_of(tile_firms[0, tile + item], workers, firms)] for item in range(2)]
        probes = pieces[0].shape[0]
        weights = jnp.concatenate([tiles[tile], tiles[tile + 1]], axis=0)
        both = dot(pair(*pieces), weights, (1, 1))
        if total is None:
            total = [jnp.zeros((probes, TILE), f32) for block in range(ROWB_DEV)]
        for item in range(2):
            image = both[item * probes : (item + 1) * probes, item * TILE : (item + 1) * TILE]
            row = tile_rows[0, tile + item]
            total = [old + jnp.where(row == block, image, 0.0) for block, old in enumerate(total)]
    return total


def adjoint(tile_rows, tile_firms, rows, tiles, out, workers, stride, wait=None):
    out[...] = jnp.zeros_like(out)
    probes = rows.shape[1]
    size = tiles.shape[0] // CHUNKS
    for tile in range(0, tiles.shape[0], 2):
        if wait is not None and tile % (2 * size) == 0:
            wait(tile // size)
            wait(tile // size + 1)
        pieces = [rows[tile_rows[0, tile + item]] for item in range(2)]
        weights = jnp.concatenate([tiles[tile], tiles[tile + 1]], axis=1)
        both = dot(pair(*pieces), weights, (1, 0))
        for item in range(2):
            image = both[item * probes : (item + 1) * probes, item * TILE : (item + 1) * TILE]
            place = place_of(tile_firms[0, tile + item], workers, stride)
            out[place] = out[place] + image


def put_rows(rows, values):
    for block in range(ROWB_DEV):
        rows[block] = values[:, block * TILE : (block + 1) * TILE].astype(bf16).astype(f32)


def add_ridge(out, place, regular, worker, own):
    out[place] = out[place] + regular[pl.ds(worker, 1), :] * own


def start_body(
    workers, firms, rows_hbm, firms_hbm, words_hbm, ids_hbm, tiles_hbm,
    out, tiles, rows, arrived, tile_rows, tile_firms, words, worker_ids,
):
    small = [(rows_hbm, tile_rows), (firms_hbm, tile_firms), (words_hbm, words), (ids_hbm, worker_ids)]
    wait = fetch(tiles_hbm, tiles, arrived, small)
    words_row, blocks, probes = words.shape
    lanes = lax.broadcasted_iota(jnp.int32, (probes, TILE), 1)
    lines = lax.broadcasted_iota(jnp.int32, (probes, TILE), 0)
    word_of = lax.div(lanes, jnp.int32(BITS))
    bit = lanes - word_of * BITS
    chosen = [jnp.zeros((probes, TILE), jnp.int32) for block in range(blocks)]
    for word in range(words_row):
        for probe in range(probes):
            here = (word_of == word) & (lines == probe)
            chosen = [jnp.where(here, words[word, block, probe], old) for block, old in enumerate(chosen)]
    signs = [(2 * (lax.shift_right_logical(old, bit) & 1) - 1).astype(f32) for old in chosen]
    put_rows(rows, demean(jnp.concatenate(signs, axis=1), worker_ids[...]))
    adjoint(tile_rows, tile_firms, rows, tiles, out, workers, firms, wait)


def middle_body(
    workers, firms, tile_rows, tile_firms, worker, firm, field, first, regular, worker_ids, tiles, out, rows
):
    total = forward(tile_rows, tile_firms, field, tiles, workers, firms)
    values = demean(jnp.concatenate(total, axis=1), worker_ids[...])
    put_rows(rows, values)
    adjoint(tile_rows, tile_firms, rows, tiles, out, workers, firms + 1)
    own = first[...]
    add_ridge(out, worker[0] * (firms + 1) + firm[0], regular, worker[0], own)
    squares = own * own
    above = jnp.sum(values * values, axis=1, keepdims=True)
    above = above + jnp.sum(squares * regular[pl.ds(worker[0], 1), :], axis=1, keepdims=True)
    below = jnp.sum(squares, axis=1, keepdims=True)
    lanes = lax.broadcasted_iota(jnp.int32, own.shape, 1)
    extra = jnp.where(lanes < TILE // 2, above, below)
    for other in range(workers):
        out[other * (firms + 1) + firms] = extra


def rows_body(workers, firms, tile_rows, tile_firms, field, first, second, quotient, worker_ids, tiles, out):
    total = forward(tile_rows, tile_firms, field, tiles, workers, firms)
    values = demean(jnp.concatenate(total, axis=1), worker_ids[...])
    for probe in range(out.shape[0]):
        out[probe, 0] = first[...]
        out[probe, 1] = second[...]
        out[probe, 2] = quotient[...]
        for block in range(ROWB_DEV):
            out[probe, 3 + block] = values[:, block * TILE : (block + 1) * TILE]


def last_body(
    workers, firms, tile_rows, tile_firms, worker, firm, probe, given, regular, tiles, out, rows
):
    gather = lambda item: jnp.concatenate([given[other, item] for other in range(given.shape[0])], axis=0)
    own = lambda item: given[probe[0], item]
    first, second = own(0), own(1)
    first_all, second_all = gather(0), gather(1)
    mine = [own(3 + block) for block in range(ROWB_DEV)]
    for block in range(ROWB_DEV):
        rows[block] = mine[block].astype(bf16).astype(f32)
    left = jnp.concatenate([*mine, second * regular[pl.ds(worker[0], 1), :]], axis=1)
    right = jnp.concatenate([*(gather(3 + block) for block in range(ROWB_DEV)), second_all], axis=1)
    extra = jnp.concatenate(
        [
            exact(first, first_all, (1, 1)),
            exact(first, second_all, (1, 1)),
            exact(second, second_all, (1, 1)),
            exact(left, right, (1, 1)),
        ],
        axis=1,
    )
    adjoint(tile_rows, tile_firms, rows, tiles, out, workers, firms + 1)
    add_ridge(out, worker[0] * (firms + 1) + firm[0], regular, worker[0], second)
    for other in range(workers):
        out[other * (firms + 1) + firms] = extra


def eliminate(table, pivots):
    size, width = table.shape
    lanes = lax.broadcasted_iota(jnp.int32, (size, width), 1)
    lines = lax.broadcasted_iota(jnp.int32, (size, width), 0)

    def spread(at):
        column = jnp.broadcast_to(table[:, pivots[0] + at : pivots[0] + at + 1], (size, width))
        for begin in pivots[1:]:
            other = jnp.broadcast_to(table[:, begin + at : begin + at + 1], (size, width))
            column = jnp.where(lanes < begin, column, other)
        return column

    for step in range(0, size, 2):
        one, two = spread(step), spread(step + 1)
        first, second = table[step : step + 1, :], table[step + 1 : step + 2, :]
        a, b = one[step : step + 1, :], two[step : step + 1, :]
        c, d = one[step + 1 : step + 2, :], two[step + 1 : step + 2, :]
        inverse = 1.0 / (a * d - b * c)
        upper = (d * first - b * second) * inverse
        lower = (a * second - c * first) * inverse
        table = table - one * upper - two * lower
        table = jnp.where(lines == step, upper, jnp.where(lines == step + 1, lower, table))
    return table


def final_body(probe, given, last, out, scratch):
    size = given.shape[0] * given.shape[2]
    gather = lambda ref, item: jnp.concatenate([ref[other, item] for other in range(ref.shape[0])], axis=0)
    half = lambda matrix: 0.5 * (matrix + matrix.T)
    lines = lax.broadcasted_iota(jnp.int32, (size, size), 0)
    lanes = lax.broadcasted_iota(jnp.int32, (size, size), 1)
    unit = jnp.where(lines == lanes, 1.0, 0.0)
    tables = gather(last, 1)
    current = half(tables[:, :size])
    mixed = tables[:, size : 2 * size]
    other = tables[:, 2 * size : 3 * size]
    other_mapped = tables[:, 3 * size :]
    scale = gather(given, 2)[:, :size]
    same_mapped = half(scale * (current - mixed).T)
    mixed_mapped = scale * (mixed - other)

    def whole(one, cross, two):
        return jnp.concatenate(
            [jnp.concatenate([one, cross], axis=1), jnp.concatenate([cross.T, two], axis=1)], axis=0
        )

    grams = whole(current, mixed, other)
    mapped_grams = whole(same_mapped, mixed_mapped, other_mapped)
    solved = eliminate(jnp.concatenate([same_mapped, current, current, unit], axis=1), (0, 2 * size))
    step_first = solved[:, size : 2 * size]
    inverse = solved[:, 3 * size :]
    onto_second = scale * step_first
    onto_first = unit - onto_second
    mix = jnp.concatenate([onto_first, onto_second], axis=0)
    following = half(exact(mix, exact(grams, mix, (1, 0)), (0, 0)))
    direction = onto_first + exact(inverse, following, (1, 0))
    mix = jnp.concatenate([direction, onto_second], axis=0)
    curvature = half(exact(mix, exact(mapped_grams, mix, (1, 0)), (0, 0)))
    step_second = eliminate(jnp.concatenate([curvature, following], axis=1), (0,))[:, size:]
    moved = exact(mix, step_second, (1, 0))
    moved_first, moved_second = moved[:size], moved[size:]
    image = scale * moved_first
    basis = jnp.concatenate([gather(given, 0), gather(given, 1), gather(last, 0)], axis=0)
    scratch[0] = exact(jnp.concatenate([step_first + moved_first, moved_second], axis=0), basis[: 2 * size], (0, 0))
    scratch[1] = exact(
        jnp.concatenate([onto_first - image, onto_second + image, -moved_second], axis=0), basis, (0, 0)
    )
    probes = given.shape[2]
    begin = pl.multiple_of(probe[0] * probes, probes)
    for worker in range(out.shape[0]):
        out[worker, 0] = scratch[0, pl.ds(begin, probes), :]
        out[worker, 1] = scratch[1, pl.ds(begin, probes), :]


def fold_body(got, out):
    total = got[0]
    for other in range(1, got.shape[0]):
        total = total + got[other]
    firms, lines = out.shape[0], out.shape[1]
    extra = lines * firms - total.shape[0]
    extra = extra // (firms - 1)
    probes = lines - extra
    for firm in range(firms):
        out[firm, :probes, :] = total[firm * probes : (firm + 1) * probes]
        if extra:
            out[firm, probes:, :] = total[firms * probes :]


def sum_of(got):
    total = got[0]
    for other in range(1, got.shape[0]):
        total = total + got[other]
    return total


def send(out, values):
    for other in range(out.shape[0]):
        out[other] = values.astype(out.dtype)


def first_body(got, first, sent):
    first[...] = sum_of(got)
    send(sent, first[...])


def second_body(got, first, second, quotient, sent):
    total = sum_of(got)
    probes = first.shape[0]
    ratio = total[probes:, :1] / total[probes:, TILE // 2 : TILE // 2 + 1]
    quotient[...] = jnp.broadcast_to(ratio, quotient.shape)
    second[...] = first[...] - total[:probes] / quotient[...]
    send(sent, second[...])


def send_body(values, sent):
    send(sent, values[...])


def third_body(got, sent):
    send(sent, sum_of(got))


def kernel(body, shapes, places, scratch, name, cost=1 << 16):
    return pl.pallas_call(
        body,
        out_shape=shapes,
        in_specs=[pl.BlockSpec(memory_space=place) for place in places],
        out_specs=jax.tree.map(lambda _: pl.BlockSpec(memory_space=pltpu.VMEM), shapes),
        scratch_shapes=scratch,
        compiler_params=pltpu.CompilerParams(vmem_limit_bytes=6 << 20),
        cost_estimate=pl.CostEstimate(flops=cost, transcendentals=0, bytes_accessed=1 << 20),
        name=name,
    )


def exchange(chunks, axis, beside=()):
    chunks, beside = lax.optimization_barrier((chunks, beside))
    got = lax.all_to_all(chunks, axis, 0, 0, tiled=True)
    return lax.optimization_barrier((got, beside))


def local(tiles, tile_rows, tile_firms, worker_ids, sign_words, regular):
    probe_dev = sign_words.shape[0]
    firms = lax.axis_size("firm")
    workers = lax.axis_size("worker")
    probes = lax.axis_size("probe")
    count = tiles.shape[0]
    reg_blocks = regular.reshape(workers, TILE)
    words = jnp.transpose(sign_words, (2, 1, 0))
    at = tuple(lax.axis_index(axis).reshape(1) for axis in ("firm", "worker", "probe"))

    VMEM, SMEM, HBM = pltpu.VMEM, pltpu.SMEM, pltpu.HBM
    rows_vmem = VMEM((ROWB_DEV, probe_dev, TILE), f32)
    cost = 2 * count * probe_dev * TILE * TILE

    def shape(*dims, dtype=f32):
        return jax.ShapeDtypeStruct(dims, dtype)

    def placed(array, where):
        return pltpu.with_memory_space_constraint(array, where)

    def owner_parts(parts, beside):
        chunk = parts.reshape(workers, -1, TILE)
        got, beside = exchange(chunk, "worker", beside)
        extra = chunk.shape[1] - firms * probe_dev
        chunk = kernel(fold_body, shape(firms, probe_dev + extra, TILE), [VMEM], [], "fold")(got)
        return exchange(chunk, "firm", beside)

    def collect(sent, beside):
        column, beside = exchange(sent, "firm", beside)
        dims = (workers, firms, probe_dev, TILE)
        sent = kernel(send_body, shape(*dims, dtype=bf16), [VMEM], [], "spread")(column)
        field, beside = exchange(sent, "worker", beside)
        return field.reshape(workers * firms, probe_dev, TILE), beside

    def bind(body):
        return lambda *refs: body(workers, firms, *refs)

    own = shape(probe_dev, TILE)
    sent_own = shape(firms, probe_dev, TILE, dtype=bf16)
    parts, tiles = kernel(
        bind(start_body), (shape(workers * firms, probe_dev, TILE), VMEM(tiles.shape, bf16)), [HBM] * 5,
        [
            rows_vmem, pltpu.SemaphoreType.DMA((CHUNKS + 4,)), SMEM(tile_rows.shape, jnp.int32),
            SMEM(tile_firms.shape, jnp.int32), SMEM(words.shape, jnp.int32), VMEM(worker_ids.shape, jnp.int32),
        ],
        "start", cost,
    )(*(placed(array, HBM) for array in (tile_rows, tile_firms, words, worker_ids, tiles)))
    got, at = owner_parts(parts, at)
    first, sent = kernel(first_body, (own, sent_own), [VMEM], [], "first")(got)

    field, (first, *at) = collect(sent, (first, *at))
    firm, worker, _ = at
    parts = kernel(
        bind(middle_body), shape(workers * (firms + 1), probe_dev, TILE),
        [SMEM, SMEM, SMEM, SMEM, VMEM, VMEM, VMEM, VMEM, VMEM], [rows_vmem], "middle", 2 * cost,
    )(tile_rows, tile_firms, worker, firm, field, first, reg_blocks, worker_ids, placed(tiles, VMEM))
    got, (first, *at) = owner_parts(parts, (first, *at))
    second, quotient, sent = kernel(second_body, (own, own, sent_own), [VMEM, VMEM], [], "second")(got, first)

    field, (first, second, quotient, *at) = collect(sent, (first, second, quotient, *at))
    sent = kernel(
        bind(rows_body), shape(probes, 3 + ROWB_DEV, probe_dev, TILE),
        [SMEM, SMEM, VMEM, VMEM, VMEM, VMEM, VMEM, VMEM], [], "rows", cost,
    )(tile_rows, tile_firms, field, first, second, quotient, worker_ids, placed(tiles, VMEM))
    given, at = exchange(sent, "probe", at)
    firm, worker, probe = at
    parts = kernel(
        bind(last_body), shape(workers * (firms + 1), probe_dev, TILE),
        [SMEM, SMEM, SMEM, SMEM, SMEM, VMEM, VMEM, VMEM], [rows_vmem], "last", cost,
    )(tile_rows, tile_firms, worker, firm, probe, given, reg_blocks, placed(tiles, VMEM))
    got, (given, *at) = owner_parts(parts, (given, *at))
    sent = kernel(third_body, shape(probes, 2 * probe_dev, TILE), [VMEM], [], "third")(got)
    last, (given, *at) = exchange(sent, "probe", (given, *at))
    outs = kernel(
        final_body, shape(workers, 2, probe_dev, TILE), [SMEM, VMEM, VMEM],
        [VMEM((2, probes * probe_dev, TILE), f32)], "final", cost // 4,
    )(at[2], given, last.reshape(probes, 2, probe_dev, TILE))
    outs, _ = exchange(outs, "worker")
    outs = jnp.transpose(outs, (1, 2, 0, 3)).reshape(2, probe_dev, workers * TILE)
    return (outs[0], outs[1])


def solution(mesh):
    placed = (
        P(("firm", "worker"), None, None),
        P(("firm", "worker"), None),
        P(("firm", "worker"), None),
        P(("firm", "worker"), None),
        P("probe", ("firm", "worker"), None),
        P("firm"),
    )
    return jax.shard_map(
        local,
        mesh=mesh,
        in_specs=placed,
        out_specs=(P("probe", "firm"), P("probe", "firm")),
        check_vma=False,
    )
```

```python
import jax
import jax.numpy as jnp
from jax import lax
from jax.experimental import pallas as pl
from jax.experimental.pallas import tpu as pltpu
from jax.sharding import PartitionSpec as P

TILE = 128
ROWB_DEV = 4
ROWS_DEV = 512
SHARD_WORKERS = 128
BITS = 30
CHUNKS = 4

largest_value = lax.Precision.HIGHEST
f32 = jnp.float32
bf16 = jnp.bfloat16


def dot(left, right, dims, precision=None):
    return lax.dot_general(
        left, right, ((dims[:1], dims[1:]), ((), ())), precision=precision, preferred_element_type=f32
    )


def exact(left, right, dims):
    return dot(left, right, dims, largest_value)


def three_parts(values):
    high = values.astype(bf16)
    rest = values - high.astype(f32)
    middle = rest.astype(bf16)
    low = (rest - middle.astype(f32)).astype(bf16)
    return high, middle, low


def demean(values, worker_ids):
    probes = values.shape[0]
    workers = lax.broadcasted_iota(jnp.int32, (SHARD_WORKERS, ROWS_DEV), 0)
    onehot = jnp.where(workers == worker_ids, 1.0, 0.0).astype(bf16)
    stacked = jnp.concatenate([*(part.astype(f32) for part in three_parts(values)), jnp.ones_like(values)], axis=0)
    sums = dot(stacked.astype(bf16), onehot, (1, 1))
    totals = (sums[2 * probes : 3 * probes] + sums[probes : 2 * probes]) + sums[:probes]
    means = totals / sums[3 * probes :]
    stacked = jnp.concatenate([part.astype(f32) for part in three_parts(means)], axis=0)
    spread = dot(stacked.astype(bf16), onehot, (1, 0))
    return values - ((spread[2 * probes : 3 * probes] + spread[probes : 2 * probes]) + spread[:probes])


def fetch(tiles_hbm, tiles, arrived, small):
    size = tiles.shape[0] // CHUNKS

    def copy(chunk):
        part = pl.ds(chunk * size, size)
        return pltpu.make_async_copy(tiles_hbm.at[part], tiles.at[part], arrived.at[chunk])

    tables = fetch_small(arrived, small)
    for chunk in range(CHUNKS):
        copy(chunk).start()
    for table in tables:
        table.wait()
    return lambda chunk: copy(chunk).wait()


def fetch_small(arrived, small):
    tables = [pltpu.make_async_copy(*both, arrived.at[CHUNKS + item]) for item, both in enumerate(small)]
    for table in tables:
        table.start()
    return tables


def place_of(firm, workers, stride):
    return (firm & (workers - 1)) * stride + (firm >> (workers.bit_length() - 1))


def pair(upper, lower):
    return jnp.concatenate([upper.astype(f32), lower.astype(f32)], axis=0).astype(bf16)


def forward(tile_rows, tile_firms, field, tiles, workers, firms):
    total = None
    for tile in range(0, tiles.shape[0], 2):
        pieces = [field[place_of(tile_firms[0, tile + item], workers, firms)] for item in range(2)]
        probes = pieces[0].shape[0]
        weights = jnp.concatenate([tiles[tile], tiles[tile + 1]], axis=0)
        both = dot(pair(*pieces), weights, (1, 1))
        if total is None:
            total = [jnp.zeros((probes, TILE), f32) for block in range(ROWB_DEV)]
        for item in range(2):
            image = both[item * probes : (item + 1) * probes, item * TILE : (item + 1) * TILE]
            row = tile_rows[0, tile + item]
            total = [old + jnp.where(row == block, image, 0.0) for block, old in enumerate(total)]
    return total


def adjoint(tile_rows, tile_firms, rows, tiles, out, workers, stride, wait=None):
    out[...] = jnp.zeros_like(out)
    probes = rows.shape[1]
    size = tiles.shape[0] // CHUNKS
    for tile in range(0, tiles.shape[0], 2):
        if wait is not None and tile % (2 * size) == 0:
            wait(tile // size)
            wait(tile // size + 1)
        pieces = [rows[tile_rows[0, tile + item]] for item in range(2)]
        weights = jnp.concatenate([tiles[tile], tiles[tile + 1]], axis=1)
        both = dot(pair(*pieces), weights, (1, 0))
        for item in range(2):
            image = both[item * probes : (item + 1) * probes, item * TILE : (item + 1) * TILE]
            place = place_of(tile_firms[0, tile + item], workers, stride)
            out[place] = out[place] + image


def put_rows(rows, values):
    for block in range(ROWB_DEV):
        rows[block] = values[:, block * TILE : (block + 1) * TILE].astype(bf16).astype(f32)


def put_parts(out, total, extras):
    workers, firms = out.shape[0], out.shape[1] - len(extras)
    for worker in range(workers):
        for firm in range(firms):
            out[worker, firm] = total[worker * firms + firm].astype(out.dtype)
        for item, extra in enumerate(extras):
            out[worker, firms + item] = extra.astype(out.dtype)


def add_ridge(out, place, regular, worker, own):
    out[place] = out[place] + regular[pl.ds(worker, 1), :] * own


def start_body(
    workers, firms, rows_hbm, firms_hbm, words_hbm, ids_hbm, tiles_hbm,
    out, tiles, rows, arrived, tile_rows, tile_firms, words, worker_ids,
):
    small = [(rows_hbm, tile_rows), (firms_hbm, tile_firms), (words_hbm, words), (ids_hbm, worker_ids)]
    wait = fetch(tiles_hbm, tiles, arrived, small)
    words_row, blocks, probes = words.shape
    lanes = lax.broadcasted_iota(jnp.int32, (probes, TILE), 1)
    lines = lax.broadcasted_iota(jnp.int32, (probes, TILE), 0)
    word_of = lax.div(lanes, jnp.int32(BITS))
    bit = lanes - word_of * BITS
    chosen = [jnp.zeros((probes, TILE), jnp.int32) for block in range(blocks)]
    for word in range(words_row):
        for probe in range(probes):
            here = (word_of == word) & (lines == probe)
            chosen = [jnp.where(here, words[word, block, probe], old) for block, old in enumerate(chosen)]
    signs = [(2 * (lax.shift_right_logical(old, bit) & 1) - 1).astype(f32) for old in chosen]
    put_rows(rows, demean(jnp.concatenate(signs, axis=1), worker_ids[...]))
    adjoint(tile_rows, tile_firms, rows, tiles, out, workers, firms, wait)


def middle_body(
    workers, firms, tile_rows, tile_firms, worker, firm, field, first, regular, worker_ids, tiles,
    out, rows, feature_sums,
):
    total = forward(tile_rows, tile_firms, field, tiles, workers, firms)
    values = demean(jnp.concatenate(total, axis=1), worker_ids[...])
    put_rows(rows, values)
    adjoint(tile_rows, tile_firms, rows, tiles, feature_sums, workers, firms)
    own = first[...]
    add_ridge(feature_sums, worker[0] * firms + firm[0], regular, worker[0], own)
    squares = own * own
    above = jnp.sum(values * values, axis=1, keepdims=True)
    above = above + jnp.sum(squares * regular[pl.ds(worker[0], 1), :], axis=1, keepdims=True)
    below = jnp.sum(squares, axis=1, keepdims=True)
    lanes = lax.broadcasted_iota(jnp.int32, own.shape, 1)
    put_parts(out, feature_sums, [jnp.where(lanes < TILE // 2, above, below)])


def rows_body(workers, firms, tile_rows, tile_firms, field, first, second, quotient, worker_ids, tiles, out):
    total = forward(tile_rows, tile_firms, field, tiles, workers, firms)
    values = demean(jnp.concatenate(total, axis=1), worker_ids[...])
    for probe in range(out.shape[0]):
        out[probe, 0] = first[...]
        out[probe, 1] = second[...]
        out[probe, 2] = quotient[...]
        for block in range(ROWB_DEV):
            out[probe, 3 + block] = values[:, block * TILE : (block + 1) * TILE]


def last_body(
    workers, firms, tile_rows, tile_firms, worker, firm, probe, given, regular, tiles,
    out, rows, feature_sums,
):
    gather = lambda item: jnp.concatenate([given[other, item] for other in range(given.shape[0])], axis=0)
    own = lambda item: given[probe[0], item]
    first, second = own(0), own(1)
    first_all, second_all = gather(0), gather(1)
    mine = [own(3 + block) for block in range(ROWB_DEV)]
    for block in range(ROWB_DEV):
        rows[block] = mine[block].astype(bf16).astype(f32)
    left = jnp.concatenate([*mine, second * regular[pl.ds(worker[0], 1), :]], axis=1)
    right = jnp.concatenate([*(gather(3 + block) for block in range(ROWB_DEV)), second_all], axis=1)
    extra = jnp.concatenate(
        [
            exact(first, first_all, (1, 1)),
            exact(first, second_all, (1, 1)),
            exact(second, second_all, (1, 1)),
            exact(left, right, (1, 1)),
        ],
        axis=1,
    )
    adjoint(tile_rows, tile_firms, rows, tiles, feature_sums, workers, firms)
    add_ridge(feature_sums, worker[0] * firms + firm[0], regular, worker[0], second)
    put_parts(out, feature_sums, three_parts(extra))


def eliminate(table, pivots):
    size, width = table.shape
    lanes = lax.broadcasted_iota(jnp.int32, (size, width), 1)
    lines = lax.broadcasted_iota(jnp.int32, (size, width), 0)

    def spread(at):
        column = jnp.broadcast_to(table[:, pivots[0] + at : pivots[0] + at + 1], (size, width))
        for begin in pivots[1:]:
            other = jnp.broadcast_to(table[:, begin + at : begin + at + 1], (size, width))
            column = jnp.where(lanes < begin, column, other)
        return column

    for step in range(0, size, 2):
        one, two = spread(step), spread(step + 1)
        first, second = table[step : step + 1, :], table[step + 1 : step + 2, :]
        a, b = one[step : step + 1, :], two[step : step + 1, :]
        c, d = one[step + 1 : step + 2, :], two[step + 1 : step + 2, :]
        inverse = 1.0 / (a * d - b * c)
        upper = (d * first - b * second) * inverse
        lower = (a * second - c * first) * inverse
        table = table - one * upper - two * lower
        table = jnp.where(lines == step, upper, jnp.where(lines == step + 1, lower, table))
    return table


def final_body(probe, given, last, out, scratch):
    size = given.shape[0] * given.shape[2]
    gather = lambda ref, item: jnp.concatenate([ref[other, item] for other in range(ref.shape[0])], axis=0)
    half = lambda matrix: 0.5 * (matrix + matrix.T)
    lines = lax.broadcasted_iota(jnp.int32, (size, size), 0)
    lanes = lax.broadcasted_iota(jnp.int32, (size, size), 1)
    unit = jnp.where(lines == lanes, 1.0, 0.0)
    tables = gather(last, 1)
    current = half(tables[:, :size])
    mixed = tables[:, size : 2 * size]
    other = tables[:, 2 * size : 3 * size]
    other_mapped = tables[:, 3 * size :]
    scale = gather(given, 2)[:, :size]
    same_mapped = half(scale * (current - mixed).T)
    mixed_mapped = scale * (mixed - other)

    def whole(one, cross, two):
        return jnp.concatenate(
            [jnp.concatenate([one, cross], axis=1), jnp.concatenate([cross.T, two], axis=1)], axis=0
        )

    grams = whole(current, mixed, other)
    mapped_grams = whole(same_mapped, mixed_mapped, other_mapped)
    solved = eliminate(jnp.concatenate([same_mapped, current, current, unit], axis=1), (0, 2 * size))
    step_first = solved[:, size : 2 * size]
    inverse = solved[:, 3 * size :]
    onto_second = scale * step_first
    onto_first = unit - onto_second
    mix = jnp.concatenate([onto_first, onto_second], axis=0)
    following = half(exact(mix, exact(grams, mix, (1, 0)), (0, 0)))
    direction = onto_first + exact(inverse, following, (1, 0))
    mix = jnp.concatenate([direction, onto_second], axis=0)
    curvature = half(exact(mix, exact(mapped_grams, mix, (1, 0)), (0, 0)))
    step_second = eliminate(jnp.concatenate([curvature, following], axis=1), (0,))[:, size:]
    moved = exact(mix, step_second, (1, 0))
    moved_first, moved_second = moved[:size], moved[size:]
    image = scale * moved_first
    basis = jnp.concatenate([gather(given, 0), gather(given, 1), gather(last, 0)], axis=0)
    scratch[0] = exact(jnp.concatenate([step_first + moved_first, moved_second], axis=0), basis[: 2 * size], (0, 0))
    scratch[1] = exact(
        jnp.concatenate([onto_first - image, onto_second + image, -moved_second], axis=0), basis, (0, 0)
    )
    probes = given.shape[2]
    begin = pl.multiple_of(probe[0] * probes, probes)
    for worker in range(out.shape[0]):
        out[worker, 0] = scratch[0, pl.ds(begin, probes), :]
        out[worker, 1] = scratch[1, pl.ds(begin, probes), :]


def fold_body(got, out):
    total = sum_of(got)
    firms, probes = out.shape[0], total.shape[1]
    for firm in range(firms):
        out[firm, :probes, :] = total[firm]
    if out.shape[1] > probes:
        extra = total[firms]
        for item in range(firms + 1, total.shape[0]):
            extra = extra + total[item]
        for firm in range(firms):
            out[firm, probes:, :] = extra


def sum_of(got):
    total = got[0].astype(f32)
    for other in range(1, got.shape[0]):
        total = total + got[other].astype(f32)
    return total


def send(out, values):
    for other in range(out.shape[0]):
        out[other] = values.astype(out.dtype)


def first_body(got, first, sent):
    first[...] = sum_of(got)
    send(sent, first[...])


def second_body(got, first, second, quotient, sent):
    total = sum_of(got)
    probes = first.shape[0]
    ratio = total[probes:, :1] / total[probes:, TILE // 2 : TILE // 2 + 1]
    quotient[...] = jnp.broadcast_to(ratio, quotient.shape)
    second[...] = first[...] - total[:probes] / quotient[...]
    send(sent, second[...])


def send_body(values, sent):
    send(sent, values[...])


def third_body(got, sent):
    send(sent, sum_of(got))


def kernel(body, shapes, places, scratch, name, cost=1 << 16):
    return pl.pallas_call(
        body,
        out_shape=shapes,
        in_specs=[pl.BlockSpec(memory_space=place) for place in places],
        out_specs=jax.tree.map(lambda _: pl.BlockSpec(memory_space=pltpu.VMEM), shapes),
        scratch_shapes=scratch,
        compiler_params=pltpu.CompilerParams(vmem_limit_bytes=6 << 20),
        cost_estimate=pl.CostEstimate(flops=cost, transcendentals=0, bytes_accessed=1 << 20),
        name=name,
    )


def exchange(chunks, axis, beside=()):
    chunks, beside = lax.optimization_barrier((chunks, beside))
    got = lax.all_to_all(chunks, axis, 0, 0, tiled=True)
    return lax.optimization_barrier((got, beside))


def local(tiles, tile_rows, tile_firms, worker_ids, sign_words, regular):
    probe_dev = sign_words.shape[0]
    firms = lax.axis_size("firm")
    workers = lax.axis_size("worker")
    probes = lax.axis_size("probe")
    count = tiles.shape[0]
    reg_blocks = regular.reshape(workers, TILE)
    words = jnp.transpose(sign_words, (2, 1, 0))
    at = tuple(lax.axis_index(axis).reshape(1) for axis in ("firm", "worker", "probe"))

    VMEM, SMEM, HBM = pltpu.VMEM, pltpu.SMEM, pltpu.HBM
    rows_vmem = VMEM((ROWB_DEV, probe_dev, TILE), f32)
    sums_vmem = VMEM((workers * firms, probe_dev, TILE), f32)
    cost = 2 * count * probe_dev * TILE * TILE

    def shape(*dims, dtype=f32):
        return jax.ShapeDtypeStruct(dims, dtype)

    def placed(array, where):
        return pltpu.with_memory_space_constraint(array, where)

    def owner_parts(parts, beside):
        got, beside = exchange(parts.reshape(workers, -1, probe_dev, TILE), "worker", beside)
        extra = probe_dev if got.shape[1] > firms else 0
        chunk = kernel(fold_body, shape(firms, probe_dev + extra, TILE), [VMEM], [], "fold")(got)
        return exchange(chunk, "firm", beside)

    def collect(sent, beside):
        column, beside = exchange(sent, "firm", beside)
        dims = (workers, firms, probe_dev, TILE)
        sent = kernel(send_body, shape(*dims, dtype=bf16), [VMEM], [], "spread")(column)
        field, beside = exchange(sent, "worker", beside)
        return field.reshape(workers * firms, probe_dev, TILE), beside

    def bind(body):
        return lambda *refs: body(workers, firms, *refs)

    own = shape(probe_dev, TILE)
    sent_own = shape(firms, probe_dev, TILE, dtype=bf16)
    parts, tiles = kernel(
        bind(start_body), (shape(workers * firms, probe_dev, TILE), VMEM(tiles.shape, bf16)), [HBM] * 5,
        [
            rows_vmem, pltpu.SemaphoreType.DMA((CHUNKS + 4,)), SMEM(tile_rows.shape, jnp.int32),
            SMEM(tile_firms.shape, jnp.int32), SMEM(words.shape, jnp.int32), VMEM(worker_ids.shape, jnp.int32),
        ],
        "start", cost,
    )(*(placed(array, HBM) for array in (tile_rows, tile_firms, words, worker_ids, tiles)))
    got, at = owner_parts(parts, at)
    first, sent = kernel(first_body, (own, sent_own), [VMEM], [], "first")(got)

    field, (first, *at) = collect(sent, (first, *at))
    firm, worker, _ = at
    parts = kernel(
        bind(middle_body), shape(workers, firms + 1, probe_dev, TILE, dtype=bf16),
        [SMEM, SMEM, SMEM, SMEM, VMEM, VMEM, VMEM, VMEM, VMEM], [rows_vmem, sums_vmem], "middle", 2 * cost,
    )(tile_rows, tile_firms, worker, firm, field, first, reg_blocks, worker_ids, placed(tiles, VMEM))
    got, (first, *at) = owner_parts(parts, (first, *at))
    second, quotient, sent = kernel(second_body, (own, own, sent_own), [VMEM, VMEM], [], "second")(got, first)

    field, (first, second, quotient, *at) = collect(sent, (first, second, quotient, *at))
    sent = kernel(
        bind(rows_body), shape(probes, 3 + ROWB_DEV, probe_dev, TILE),
        [SMEM, SMEM, VMEM, VMEM, VMEM, VMEM, VMEM, VMEM], [], "rows", cost,
    )(tile_rows, tile_firms, field, first, second, quotient, worker_ids, placed(tiles, VMEM))
    given, at = exchange(sent, "probe", at)
    firm, worker, probe = at
    parts = kernel(
        bind(last_body), shape(workers, firms + 3, probe_dev, TILE, dtype=bf16),
        [SMEM, SMEM, SMEM, SMEM, SMEM, VMEM, VMEM, VMEM], [rows_vmem, sums_vmem], "last", cost,
    )(tile_rows, tile_firms, worker, firm, probe, given, reg_blocks, placed(tiles, VMEM))
    got, (given, *at) = owner_parts(parts, (given, *at))
    sent = kernel(third_body, shape(probes, 2 * probe_dev, TILE), [VMEM], [], "third")(got)
    last, (given, *at) = exchange(sent, "probe", (given, *at))
    outs = kernel(
        final_body, shape(workers, 2, probe_dev, TILE), [SMEM, VMEM, VMEM],
        [VMEM((2, probes * probe_dev, TILE), f32)], "final", cost // 4,
    )(at[2], given, last.reshape(probes, 2, probe_dev, TILE))
    outs, _ = exchange(outs, "worker")
    outs = jnp.transpose(outs, (1, 2, 0, 3)).reshape(2, probe_dev, workers * TILE)
    return (outs[0], outs[1])


def solution(mesh):
    placed = (
        P(("firm", "worker"), None, None),
        P(("firm", "worker"), None),
        P(("firm", "worker"), None),
        P(("firm", "worker"), None),
        P("probe", ("firm", "worker"), None),
        P("firm"),
    )
    return jax.shard_map(
        local,
        mesh=mesh,
        in_specs=placed,
        out_specs=(P("probe", "firm"), P("probe", "firm")),
        check_vma=False,
    )
```

```python
import jax
import jax.numpy as jnp
from jax import lax
from jax.experimental import pallas as pl
from jax.experimental.pallas import tpu as pltpu
from jax.sharding import PartitionSpec as P

TILE = 128
ROWB_DEV = 4
ROWS_DEV = 512
SHARD_WORKERS = 128
BITS = 30
CHUNKS = 4
WORKERS = 8
FIRMS = 16
NEAR_FIRST = 2
NEAR_SECOND = 4
FIRM_AXES = ("firm_far", "firm_middle", "firm_near")

largest_value = lax.Precision.HIGHEST
f32 = jnp.float32
bf16 = jnp.bfloat16


def dot(left, right, dims, precision=None):
    return lax.dot_general(
        left, right, ((dims[:1], dims[1:]), ((), ())), precision=precision, preferred_element_type=f32
    )


def exact(left, right, dims):
    return dot(left, right, dims, largest_value)


def three_parts(values):
    high = values.astype(bf16)
    rest = values - high.astype(f32)
    middle = rest.astype(bf16)
    low = (rest - middle.astype(f32)).astype(bf16)
    return high, middle, low


def demean(values, worker_ids):
    probes = values.shape[0]
    workers = lax.broadcasted_iota(jnp.int32, (SHARD_WORKERS, ROWS_DEV), 0)
    onehot = jnp.where(workers == worker_ids, 1.0, 0.0).astype(bf16)
    stacked = jnp.concatenate([*(part.astype(f32) for part in three_parts(values)), jnp.ones_like(values)], axis=0)
    sums = dot(stacked.astype(bf16), onehot, (1, 1))
    totals = (sums[2 * probes : 3 * probes] + sums[probes : 2 * probes]) + sums[:probes]
    means = totals / sums[3 * probes :]
    stacked = jnp.concatenate([part.astype(f32) for part in three_parts(means)], axis=0)
    spread = dot(stacked.astype(bf16), onehot, (1, 0))
    return values - ((spread[2 * probes : 3 * probes] + spread[probes : 2 * probes]) + spread[:probes])


def fetch(tiles_hbm, tiles, arrived, small):
    size = tiles.shape[0] // CHUNKS

    def copy(chunk):
        part = pl.ds(chunk * size, size)
        return pltpu.make_async_copy(tiles_hbm.at[part], tiles.at[part], arrived.at[chunk])

    tables = fetch_small(arrived, small)
    for chunk in range(CHUNKS):
        copy(chunk).start()
    for table in tables:
        table.wait()
    return lambda chunk: copy(chunk).wait()


def fetch_small(arrived, small):
    tables = [pltpu.make_async_copy(*both, arrived.at[CHUNKS + item]) for item, both in enumerate(small)]
    for table in tables:
        table.start()
    return tables


def place_of(block, near):
    firm, worker = block >> (WORKERS.bit_length() - 1), block & (WORKERS - 1)
    shift = near.bit_length() - 1
    return ((firm & (near - 1)) * WORKERS + worker) * (FIRMS // near) + (firm >> shift)


def stack(pieces):
    return jnp.concatenate([piece.astype(f32) for piece in pieces], axis=0).astype(bf16)


def forward(tile_rows, tile_firms, field, tiles, near):
    total = None
    for tile in range(0, tiles.shape[0], 2):
        pieces = [field[place_of(tile_firms[0, tile + item], near)] for item in range(2)]
        probes = pieces[0].shape[0]
        weights = jnp.concatenate([tiles[tile], tiles[tile + 1]], axis=0)
        both = dot(stack(pieces), weights, (1, 1))
        if total is None:
            total = [jnp.zeros((probes, TILE), f32) for block in range(ROWB_DEV)]
        for item in range(2):
            image = both[item * probes : (item + 1) * probes, item * TILE : (item + 1) * TILE]
            row = tile_rows[0, tile + item]
            total = [old + jnp.where(row == block, image, 0.0) for block, old in enumerate(total)]
    return total


def adjoint(tile_rows, tile_firms, rows, tiles, out, near, wait=None):
    out[...] = jnp.zeros_like(out)
    probes, lines = out.shape[1], rows.shape[1]
    size = tiles.shape[0] // CHUNKS
    for tile in range(0, tiles.shape[0], 2):
        if wait is not None and tile % (2 * size) == 0:
            wait(tile // size)
            wait(tile // size + 1)
        weights = jnp.concatenate([tiles[tile], tiles[tile + 1]], axis=1)
        both = dot(stack([rows[tile_rows[0, tile + item]] for item in range(2)]), weights, (1, 0))
        for item in range(2):
            place = place_of(tile_firms[0, tile + item], near)
            image = out[place]
            for begin in range(item * lines, (item + 1) * lines, probes):
                image = image + both[begin : begin + probes, item * TILE : (item + 1) * TILE]
            out[place] = image


def put_rows(rows, values):
    for block in range(ROWB_DEV):
        rows[block] = values[:, block * TILE : (block + 1) * TILE].astype(bf16).astype(f32)


def put_two_terms(rows, values):
    high = values.astype(bf16).astype(f32)
    rows[...] = jnp.concatenate([high, (values - high).astype(bf16).astype(f32)], axis=0)


def put_parts(out, total, extras):
    peers, blocks = out.shape[0], out.shape[1] - len(extras)
    for peer in range(peers):
        for block in range(blocks):
            out[peer, block] = total[peer * blocks + block].astype(out.dtype)
        for item, extra in enumerate(extras):
            out[peer, blocks + item] = extra.astype(out.dtype)


def add_ridge(out, firm, worker, near, regular, own):
    place = place_of(firm * WORKERS + worker, near)
    out[place] = out[place] + regular[pl.ds(worker, 1), :] * own


def start_body(
    rows_hbm, firms_hbm, words_hbm, ids_hbm, tiles_hbm,
    out, tiles, rows, arrived, tile_rows, tile_firms, words, worker_ids,
):
    small = [(rows_hbm, tile_rows), (firms_hbm, tile_firms), (words_hbm, words), (ids_hbm, worker_ids)]
    wait = fetch(tiles_hbm, tiles, arrived, small)
    words_row, blocks, probes = words.shape
    lanes = lax.broadcasted_iota(jnp.int32, (probes, TILE), 1)
    lines = lax.broadcasted_iota(jnp.int32, (probes, TILE), 0)
    word_of = lax.div(lanes, jnp.int32(BITS))
    bit = lanes - word_of * BITS
    chosen = [jnp.zeros((probes, TILE), jnp.int32) for block in range(blocks)]
    for word in range(words_row):
        for probe in range(probes):
            here = (word_of == word) & (lines == probe)
            chosen = [jnp.where(here, words[word, block, probe], old) for block, old in enumerate(chosen)]
    signs = [(2 * (lax.shift_right_logical(old, bit) & 1) - 1).astype(f32) for old in chosen]
    put_rows(rows, demean(jnp.concatenate(signs, axis=1), worker_ids[...]))
    adjoint(tile_rows, tile_firms, rows, tiles, out, NEAR_FIRST, wait)


def middle_body(
    tile_rows, tile_firms, worker, firm, field, firsts, regular, worker_ids, tiles,
    out, rows, feature_sums,
):
    total = forward(tile_rows, tile_firms, field, tiles, NEAR_FIRST)
    values = demean(jnp.concatenate(total, axis=1), worker_ids[...])
    put_rows(rows, values)
    adjoint(tile_rows, tile_firms, rows, tiles, feature_sums, NEAR_SECOND)
    own = firsts[lax.div(firm[0], NEAR_FIRST)]
    add_ridge(feature_sums, firm[0], worker[0], NEAR_SECOND, regular, own)
    squares = own * own
    above = jnp.sum(values * values, axis=1, keepdims=True)
    above = above + jnp.sum(squares * regular[pl.ds(worker[0], 1), :], axis=1, keepdims=True)
    below = jnp.sum(squares, axis=1, keepdims=True)
    lanes = lax.broadcasted_iota(jnp.int32, own.shape, 1)
    put_parts(out, feature_sums, [jnp.where(lanes < TILE // 2, above, below)])


def rows_body(tile_rows, tile_firms, field, first, second, quotient, worker_ids, tiles, out):
    total = forward(tile_rows, tile_firms, field, tiles, NEAR_SECOND)
    values = demean(jnp.concatenate(total, axis=1), worker_ids[...])
    for probe in range(out.shape[0]):
        out[probe, 0] = first[...]
        out[probe, 1] = second[...]
        out[probe, 2] = quotient[...]
        for block in range(ROWB_DEV):
            out[probe, 3 + block] = values[:, block * TILE : (block + 1) * TILE]


def last_body(
    tile_rows, tile_firms, worker, firm, probe, given, regular, tiles,
    out, rows, feature_sums,
):
    gather = lambda item: jnp.concatenate([given[other, item] for other in range(given.shape[0])], axis=0)
    own = lambda item: given[probe[0], item]
    first, second = own(0), own(1)
    first_all, second_all = gather(0), gather(1)
    mine = [own(3 + block) for block in range(ROWB_DEV)]
    for block in range(ROWB_DEV):
        put_two_terms(rows.at[block], mine[block])
    left = jnp.concatenate([*mine, second * regular[pl.ds(worker[0], 1), :]], axis=1)
    right = jnp.concatenate([*(gather(3 + block) for block in range(ROWB_DEV)), second_all], axis=1)
    extra = jnp.concatenate(
        [
            exact(first, first_all, (1, 1)),
            exact(first, second_all, (1, 1)),
            exact(second, second_all, (1, 1)),
            exact(left, right, (1, 1)),
        ],
        axis=1,
    )
    adjoint(tile_rows, tile_firms, rows, tiles, feature_sums, 1)
    add_ridge(feature_sums, firm[0], worker[0], 1, regular, second)
    put_parts(out, feature_sums, three_parts(extra))


def eliminate(table, pivots):
    size, width = table.shape
    lanes = lax.broadcasted_iota(jnp.int32, (size, width), 1)
    lines = lax.broadcasted_iota(jnp.int32, (size, width), 0)

    def spread(at):
        column = jnp.broadcast_to(table[:, pivots[0] + at : pivots[0] + at + 1], (size, width))
        for begin in pivots[1:]:
            other = jnp.broadcast_to(table[:, begin + at : begin + at + 1], (size, width))
            column = jnp.where(lanes < begin, column, other)
        return column

    for step in range(0, size, 2):
        one, two = spread(step), spread(step + 1)
        first, second = table[step : step + 1, :], table[step + 1 : step + 2, :]
        a, b = one[step : step + 1, :], two[step : step + 1, :]
        c, d = one[step + 1 : step + 2, :], two[step + 1 : step + 2, :]
        inverse = 1.0 / (a * d - b * c)
        upper = (d * first - b * second) * inverse
        lower = (a * second - c * first) * inverse
        table = table - one * upper - two * lower
        table = jnp.where(lines == step, upper, jnp.where(lines == step + 1, lower, table))
    return table


def final_body(probe, given, last, out, scratch):
    size = given.shape[0] * given.shape[2]
    gather = lambda ref, item: jnp.concatenate([ref[other, item] for other in range(ref.shape[0])], axis=0)
    half = lambda matrix: 0.5 * (matrix + matrix.T)
    lines = lax.broadcasted_iota(jnp.int32, (size, size), 0)
    lanes = lax.broadcasted_iota(jnp.int32, (size, size), 1)
    unit = jnp.where(lines == lanes, 1.0, 0.0)
    tables = gather(last, 1)
    current = half(tables[:, :size])
    mixed = tables[:, size : 2 * size]
    other = tables[:, 2 * size : 3 * size]
    other_mapped = tables[:, 3 * size :]
    scale = gather(given, 2)[:, :size]
    same_mapped = half(scale * (current - mixed).T)
    mixed_mapped = scale * (mixed - other)

    def whole(one, cross, two):
        return jnp.concatenate(
            [jnp.concatenate([one, cross], axis=1), jnp.concatenate([cross.T, two], axis=1)], axis=0
        )

    grams = whole(current, mixed, other)
    mapped_grams = whole(same_mapped, mixed_mapped, other_mapped)
    solved = eliminate(jnp.concatenate([same_mapped, current, current, unit], axis=1), (0, 2 * size))
    step_first = solved[:, size : 2 * size]
    inverse = solved[:, 3 * size :]
    onto_second = scale * step_first
    onto_first = unit - onto_second
    mix = jnp.concatenate([onto_first, onto_second], axis=0)
    following = half(exact(mix, exact(grams, mix, (1, 0)), (0, 0)))
    direction = onto_first + exact(inverse, following, (1, 0))
    mix = jnp.concatenate([direction, onto_second], axis=0)
    curvature = half(exact(mix, exact(mapped_grams, mix, (1, 0)), (0, 0)))
    step_second = eliminate(jnp.concatenate([curvature, following], axis=1), (0,))[:, size:]
    moved = exact(mix, step_second, (1, 0))
    moved_first, moved_second = moved[:size], moved[size:]
    image = scale * moved_first
    basis = jnp.concatenate([gather(given, 0), gather(given, 1), gather(last, 0)], axis=0)
    scratch[0] = exact(jnp.concatenate([step_first + moved_first, moved_second], axis=0), basis[: 2 * size], (0, 0))
    scratch[1] = exact(
        jnp.concatenate([onto_first - image, onto_second + image, -moved_second], axis=0), basis, (0, 0)
    )
    probes = given.shape[2]
    begin = pl.multiple_of(probe[0] * probes, probes)
    for worker in range(out.shape[0]):
        out[worker, 0] = scratch[0, pl.ds(begin, probes), :]
        out[worker, 1] = scratch[1, pl.ds(begin, probes), :]


def fold_body(got, out):
    total = sum_of(got)
    firms, probes = out.shape[0], total.shape[1]
    for firm in range(firms):
        out[firm, :probes, :] = total[firm]
    if out.shape[1] > probes:
        extra = total[firms]
        for item in range(firms + 1, total.shape[0]):
            extra = extra + total[item]
        for firm in range(firms):
            out[firm, probes:, :] = extra


def sum_of(got):
    total = got[0].astype(f32)
    for other in range(1, got.shape[0]):
        total = total + got[other].astype(f32)
    return total


def send(out, values):
    for other in range(out.shape[0]):
        out[other] = values.astype(out.dtype)


def gather_fold_body(got, out):
    send(out, sum_of(got))


def first_body(got, firsts, sent):
    firsts[...] = sum_of(got)
    send(sent, firsts[...])


def second_body(firm, got, firsts, first, second, quotient, sent, seconds):
    total = sum_of(got)
    blocks = total.shape[0] - 1
    ratio = total[blocks, :, :1] / total[blocks, :, TILE // 2 : TILE // 2 + 1]
    quotient[...] = jnp.broadcast_to(ratio, quotient.shape)
    step = NEAR_SECOND // NEAR_FIRST
    near = lax.div(firm[0], NEAR_FIRST) & (step - 1)
    for block in range(blocks):
        seconds[block] = firsts[block * step + near] - total[block] / quotient[...]
    first[...] = firsts[lax.div(firm[0], NEAR_FIRST)]
    second[...] = seconds[lax.div(firm[0], NEAR_SECOND)]
    send(sent, seconds[...])


def third_body(got, sent):
    send(sent, sum_of(got))


def kernel(body, shapes, places, scratch, name, cost=1 << 16):
    return pl.pallas_call(
        body,
        out_shape=shapes,
        in_specs=[pl.BlockSpec(memory_space=place) for place in places],
        out_specs=jax.tree.map(lambda _: pl.BlockSpec(memory_space=pltpu.VMEM), shapes),
        scratch_shapes=scratch,
        compiler_params=pltpu.CompilerParams(vmem_limit_bytes=6 << 20),
        cost_estimate=pl.CostEstimate(flops=cost, transcendentals=0, bytes_accessed=1 << 20),
        name=name,
    )


def exchange(chunks, axis, beside=()):
    chunks, beside = lax.optimization_barrier((chunks, beside))
    got = lax.all_to_all(chunks, axis, 0, 0, tiled=True)
    return lax.optimization_barrier((got, beside))


def local(tiles, tile_rows, tile_firms, worker_ids, sign_words, regular):
    probe_dev = sign_words.shape[0]
    probes = lax.axis_size("probe")
    count = tiles.shape[0]
    blocks = WORKERS * FIRMS
    reg_blocks = regular.reshape(WORKERS, TILE)
    words = jnp.transpose(sign_words, (2, 1, 0))
    at = tuple(lax.axis_index(axis).reshape(1) for axis in (FIRM_AXES, "worker", "probe"))

    VMEM, SMEM, HBM = pltpu.VMEM, pltpu.SMEM, pltpu.HBM
    rows_vmem = VMEM((ROWB_DEV, probe_dev, TILE), f32)
    sums_vmem = VMEM((blocks, probe_dev, TILE), f32)
    cost = 2 * count * probe_dev * TILE * TILE

    def shape(*dims, dtype=f32):
        return jax.ShapeDtypeStruct((*dims, probe_dev, TILE), dtype)

    def placed(array, where):
        return pltpu.with_memory_space_constraint(array, where)

    near_first, far_first = (*FIRM_AXES[2:], "worker"), FIRM_AXES[:2]
    near_second, far_second = (*FIRM_AXES[1:], "worker"), FIRM_AXES[:1]
    peers_first, held_first = NEAR_FIRST * WORKERS, FIRMS // NEAR_FIRST
    peers_second, held_second = NEAR_SECOND * WORKERS, FIRMS // NEAR_SECOND

    parts, tiles = kernel(
        start_body, (shape(blocks), VMEM(tiles.shape, bf16)), [HBM] * 5,
        [
            rows_vmem, pltpu.SemaphoreType.DMA((CHUNKS + 4,)), SMEM(tile_rows.shape, jnp.int32),
            SMEM(tile_firms.shape, jnp.int32), SMEM(words.shape, jnp.int32), VMEM(worker_ids.shape, jnp.int32),
        ],
        "start", cost,
    )(*(placed(array, HBM) for array in (tile_rows, tile_firms, words, worker_ids, tiles)))
    got, at = exchange(parts.reshape(peers_first, held_first, probe_dev, TILE), near_first, at)
    sent = kernel(gather_fold_body, shape(held_first, held_first), [VMEM], [], "fold")(got)
    got, at = exchange(sent, far_first, at)
    firsts, sent = kernel(
        first_body, (shape(held_first), shape(peers_first, held_first, dtype=bf16)), [VMEM], [], "first"
    )(got)

    field, (firsts, *at) = exchange(sent, near_first, (firsts, *at))
    firm, worker, _ = at
    parts = kernel(
        middle_body, shape(peers_second, held_second + 1, dtype=bf16),
        [SMEM, SMEM, SMEM, SMEM, VMEM, VMEM, VMEM, VMEM, VMEM], [rows_vmem, sums_vmem], "middle", 2 * cost,
    )(
        tile_rows, tile_firms, worker, firm, field.reshape(blocks, probe_dev, TILE), firsts, reg_blocks,
        worker_ids, placed(tiles, VMEM),
    )
    got, (firsts, *at) = exchange(parts, near_second, (firsts, *at))
    sent = kernel(gather_fold_body, shape(held_second, held_second + 1), [VMEM], [], "fold")(got)
    got, (firsts, *at) = exchange(sent, far_second, (firsts, *at))
    first, second, quotient, sent = kernel(
        second_body, (shape(), shape(), shape(), shape(peers_second, held_second, dtype=bf16)),
        [SMEM, VMEM, VMEM], [VMEM((held_second, probe_dev, TILE), f32)], "second",
    )(at[0], got, firsts)

    field, (first, second, quotient, *at) = exchange(sent, near_second, (first, second, quotient, *at))
    sent = kernel(
        rows_body, shape(probes, 3 + ROWB_DEV), [SMEM, SMEM, VMEM, VMEM, VMEM, VMEM, VMEM, VMEM], [], "rows", cost
    )(
        tile_rows, tile_firms, field.reshape(blocks, probe_dev, TILE), first, second, quotient, worker_ids,
        placed(tiles, VMEM),
    )
    given, at = exchange(sent, "probe", at)
    firm, worker, probe = at
    parts = kernel(
        last_body, shape(WORKERS, FIRMS + 3, dtype=bf16),
        [SMEM, SMEM, SMEM, SMEM, SMEM, VMEM, VMEM, VMEM],
        [VMEM((ROWB_DEV, 2 * probe_dev, TILE), f32), sums_vmem], "last", cost,
    )(tile_rows, tile_firms, worker, firm, probe, given, reg_blocks, placed(tiles, VMEM))
    got, (given, *at) = exchange(parts, "worker", (given, *at))
    sent = kernel(
        fold_body, jax.ShapeDtypeStruct((FIRMS, 2 * probe_dev, TILE), f32), [VMEM], [], "fold_last"
    )(got)
    got, (given, *at) = exchange(sent, FIRM_AXES, (given, *at))
    sent = kernel(
        third_body, jax.ShapeDtypeStruct((probes, 2 * probe_dev, TILE), f32), [VMEM], [], "third"
    )(got)
    last, (given, *at) = exchange(sent, "probe", (given, *at))
    outs = kernel(
        final_body, shape(WORKERS, 2), [SMEM, VMEM, VMEM],
        [VMEM((2, probes * probe_dev, TILE), f32)], "final", cost // 4,
    )(at[2], given, last.reshape(probes, 2, probe_dev, TILE))
    outs, _ = exchange(outs, "worker")
    outs = jnp.transpose(outs, (1, 2, 0, 3)).reshape(2, probe_dev, WORKERS * TILE)
    return (outs[0], outs[1])


def solution(mesh):
    sizes = (FIRMS // NEAR_SECOND, NEAR_SECOND // NEAR_FIRST, NEAR_FIRST)
    split = jax.sharding.Mesh(
        mesh.devices.reshape(*sizes, WORKERS, mesh.shape["probe"]), (*FIRM_AXES, "worker", "probe")
    )
    shard = (*FIRM_AXES, "worker")
    placed = (
        P(shard, None, None),
        P(shard, None),
        P(shard, None),
        P(shard, None),
        P("probe", shard, None),
        P(FIRM_AXES),
    )
    return jax.shard_map(
        local,
        mesh=split,
        in_specs=placed,
        out_specs=(P("probe", FIRM_AXES), P("probe", FIRM_AXES)),
        check_vma=False,
    )
```

```python
import jax
import jax.numpy as jnp
from jax import lax
from jax.experimental import pallas as pl
from jax.experimental.pallas import tpu as pltpu
from jax.sharding import PartitionSpec as P

TILE = 128
ROWB_DEV = 4
ROWS_DEV = 512
SHARD_WORKERS = 128
BITS = 30
CHUNKS = 4
PANEL = 16
WORKERS = 8
FIRMS = 16
NEAR_FIRST = 2
NEAR_SECOND = 4
FIRM_AXES = ("firm_far", "firm_middle", "firm_near")

largest_value = lax.Precision.HIGHEST
f32 = jnp.float32
bf16 = jnp.bfloat16


def dot(left, right, dims, precision=None):
    return lax.dot_general(
        left, right, ((dims[:1], dims[1:]), ((), ())), precision=precision, preferred_element_type=f32
    )


def exact(left, right, dims):
    return dot(left, right, dims, largest_value)


def three_parts(values):
    high = values.astype(bf16)
    rest = values - high.astype(f32)
    middle = rest.astype(bf16)
    low = (rest - middle.astype(f32)).astype(bf16)
    return high, middle, low


def demean(values, worker_ids):
    probes = values.shape[0]
    workers = lax.broadcasted_iota(jnp.int32, (SHARD_WORKERS, ROWS_DEV), 0)
    onehot = jnp.where(workers == worker_ids, 1.0, 0.0).astype(bf16)
    stacked = jnp.concatenate([*(part.astype(f32) for part in three_parts(values)), jnp.ones_like(values)], axis=0)
    sums = dot(stacked.astype(bf16), onehot, (1, 1))
    totals = (sums[2 * probes : 3 * probes] + sums[probes : 2 * probes]) + sums[:probes]
    means = totals / sums[3 * probes :]
    stacked = jnp.concatenate([part.astype(f32) for part in three_parts(means)], axis=0)
    spread = dot(stacked.astype(bf16), onehot, (1, 0))
    return values - ((spread[2 * probes : 3 * probes] + spread[probes : 2 * probes]) + spread[:probes])


def fetch(tiles_hbm, tiles, arrived, small):
    size = tiles.shape[0] // CHUNKS

    def copy(chunk):
        part = pl.ds(chunk * size, size)
        return pltpu.make_async_copy(tiles_hbm.at[part], tiles.at[part], arrived.at[chunk])

    tables = fetch_small(arrived, small)
    for chunk in range(CHUNKS):
        copy(chunk).start()
    for table in tables:
        table.wait()
    return lambda chunk: copy(chunk).wait()


def fetch_small(arrived, small):
    tables = [pltpu.make_async_copy(*both, arrived.at[CHUNKS + item]) for item, both in enumerate(small)]
    for table in tables:
        table.start()
    return tables


def place_of(block, near):
    firm, worker = block >> (WORKERS.bit_length() - 1), block & (WORKERS - 1)
    shift = near.bit_length() - 1
    return ((firm & (near - 1)) * WORKERS + worker) * (FIRMS // near) + (firm >> shift)


def stack(pieces):
    return jnp.concatenate([piece.astype(f32) for piece in pieces], axis=0).astype(bf16)


def forward(tile_rows, tile_firms, field, tiles, near):
    total = None
    for tile in range(0, tiles.shape[0], 2):
        pieces = [field[place_of(tile_firms[0, tile + item], near)] for item in range(2)]
        probes = pieces[0].shape[0]
        weights = jnp.concatenate([tiles[tile], tiles[tile + 1]], axis=0)
        both = dot(stack(pieces), weights, (1, 1))
        if total is None:
            total = [jnp.zeros((probes, TILE), f32) for block in range(ROWB_DEV)]
        for item in range(2):
            image = both[item * probes : (item + 1) * probes, item * TILE : (item + 1) * TILE]
            row = tile_rows[0, tile + item]
            total = [old + jnp.where(row == block, image, 0.0) for block, old in enumerate(total)]
    return total


def adjoint(tile_rows, tile_firms, rows, tiles, out, near, wait=None):
    out[...] = jnp.zeros_like(out)
    probes, lines = out.shape[1], rows.shape[1]
    size = tiles.shape[0] // CHUNKS
    for tile in range(0, tiles.shape[0], 2):
        if wait is not None and tile % size == 0:
            wait(tile // size)
        weights = jnp.concatenate([tiles[tile], tiles[tile + 1]], axis=1)
        both = dot(stack([rows[tile_rows[0, tile + item]] for item in range(2)]), weights, (1, 0))
        for item in range(2):
            place = place_of(tile_firms[0, tile + item], near)
            image = out[place]
            for begin in range(item * lines, (item + 1) * lines, probes):
                image = image + both[begin : begin + probes, item * TILE : (item + 1) * TILE]
            out[place] = image


def put_rows(rows, values):
    for block in range(ROWB_DEV):
        rows[block] = values[:, block * TILE : (block + 1) * TILE].astype(bf16).astype(f32)


def put_two_terms(rows, values):
    high = values.astype(bf16).astype(f32)
    rows[...] = jnp.concatenate([high, (values - high).astype(bf16).astype(f32)], axis=0)


def put_parts(out, total, extras):
    peers, blocks = out.shape[0], out.shape[1] - len(extras)
    for peer in range(peers):
        for block in range(blocks):
            out[peer, block] = total[peer * blocks + block].astype(out.dtype)
        for item, extra in enumerate(extras):
            out[peer, blocks + item] = extra.astype(out.dtype)


def add_ridge(out, firm, worker, near, regular, own):
    place = place_of(firm * WORKERS + worker, near)
    out[place] = out[place] + regular[pl.ds(worker, 1), :] * own


def start_body(
    rows_hbm, firms_hbm, words_hbm, ids_hbm, tiles_hbm,
    out, tiles, rows, arrived, tile_rows, tile_firms, words, worker_ids,
):
    small = [(rows_hbm, tile_rows), (firms_hbm, tile_firms), (words_hbm, words), (ids_hbm, worker_ids)]
    wait = fetch(tiles_hbm, tiles, arrived, small)
    words_row, blocks, probes = words.shape
    lanes = lax.broadcasted_iota(jnp.int32, (probes, TILE), 1)
    lines = lax.broadcasted_iota(jnp.int32, (probes, TILE), 0)
    word_of = lax.div(lanes, jnp.int32(BITS))
    bit = lanes - word_of * BITS
    chosen = [jnp.zeros((probes, TILE), jnp.int32) for block in range(blocks)]
    for word in range(words_row):
        for probe in range(probes):
            here = (word_of == word) & (lines == probe)
            chosen = [jnp.where(here, words[word, block, probe], old) for block, old in enumerate(chosen)]
    signs = [(2 * (lax.shift_right_logical(old, bit) & 1) - 1).astype(f32) for old in chosen]
    put_rows(rows, demean(jnp.concatenate(signs, axis=1), worker_ids[...]))
    adjoint(tile_rows, tile_firms, rows, tiles, out, NEAR_FIRST, wait)


def middle_body(
    tile_rows, tile_firms, worker, firm, field, firsts, regular, worker_ids, tiles,
    out, rows, feature_sums,
):
    total = forward(tile_rows, tile_firms, field, tiles, NEAR_FIRST)
    values = demean(jnp.concatenate(total, axis=1), worker_ids[...])
    put_rows(rows, values)
    adjoint(tile_rows, tile_firms, rows, tiles, feature_sums, NEAR_SECOND)
    own = firsts[lax.div(firm[0], NEAR_FIRST)]
    add_ridge(feature_sums, firm[0], worker[0], NEAR_SECOND, regular, own)
    squares = own * own
    above = jnp.sum(values * values, axis=1, keepdims=True)
    above = above + jnp.sum(squares * regular[pl.ds(worker[0], 1), :], axis=1, keepdims=True)
    below = jnp.sum(squares, axis=1, keepdims=True)
    lanes = lax.broadcasted_iota(jnp.int32, own.shape, 1)
    put_parts(out, feature_sums, [jnp.where(lanes < TILE // 2, above, below)])


def rows_body(tile_rows, tile_firms, field, first, second, quotient, worker_ids, tiles, out):
    total = forward(tile_rows, tile_firms, field, tiles, NEAR_SECOND)
    values = demean(jnp.concatenate(total, axis=1), worker_ids[...])
    for probe in range(out.shape[0]):
        out[probe, 0] = first[...]
        out[probe, 1] = second[...]
        out[probe, 2] = quotient[...]
        for block in range(ROWB_DEV):
            out[probe, 3 + block] = values[:, block * TILE : (block + 1) * TILE]


def last_body(
    tile_rows, tile_firms, worker, firm, probe, given, regular, tiles,
    out, rows, feature_sums,
):
    gather = lambda item: jnp.concatenate([given[other, item] for other in range(given.shape[0])], axis=0)
    own = lambda item: given[probe[0], item]
    first, second = own(0), own(1)
    first_all, second_all = gather(0), gather(1)
    mine = [own(3 + block) for block in range(ROWB_DEV)]
    for block in range(ROWB_DEV):
        put_two_terms(rows.at[block], mine[block])
    left = jnp.concatenate([*mine, second * regular[pl.ds(worker[0], 1), :]], axis=1)
    right = jnp.concatenate([*(gather(3 + block) for block in range(ROWB_DEV)), second_all], axis=1)
    extra = jnp.concatenate(
        [
            exact(first, first_all, (1, 1)),
            exact(first, second_all, (1, 1)),
            exact(second, second_all, (1, 1)),
            exact(left, right, (1, 1)),
        ],
        axis=1,
    )
    adjoint(tile_rows, tile_firms, rows, tiles, feature_sums, 1)
    add_ridge(feature_sums, firm[0], worker[0], 1, regular, second)
    put_parts(out, feature_sums, three_parts(extra))


def eliminate(table, pivots):
    size, width = table.shape
    lanes = lax.broadcasted_iota(jnp.int32, (size, width), 1)
    lines = lax.broadcasted_iota(jnp.int32, (size, width), 0)

    def spread(at):
        column = jnp.broadcast_to(table[:, pivots[0] + at : pivots[0] + at + 1], (size, width))
        for begin in pivots[1:]:
            other = jnp.broadcast_to(table[:, begin + at : begin + at + 1], (size, width))
            column = jnp.where(lanes < begin, column, other)
        return column

    for start in range(0, size, PANEL):
        columns = [spread(start + item) for item in range(PANEL)]
        for item, column in enumerate(columns):
            at = start + item
            inverse = 1.0 / column[at : at + 1, :]
            line = table[at : at + 1, :] * inverse
            table = jnp.where(lines == at, line, table - column * line)
            for later in range(item + 1, PANEL):
                factor = columns[later][at : at + 1, :] * inverse
                columns[later] = jnp.where(lines == at, factor, columns[later] - column * factor)
    return table


def final_body(probe, given, last, out, scratch):
    size = given.shape[0] * given.shape[2]
    gather = lambda ref, item: jnp.concatenate([ref[other, item] for other in range(ref.shape[0])], axis=0)
    half = lambda matrix: 0.5 * (matrix + matrix.T)
    lines = lax.broadcasted_iota(jnp.int32, (size, size), 0)
    lanes = lax.broadcasted_iota(jnp.int32, (size, size), 1)
    unit = jnp.where(lines == lanes, 1.0, 0.0)
    tables = gather(last, 1)
    current = half(tables[:, :size])
    mixed = tables[:, size : 2 * size]
    other = tables[:, 2 * size : 3 * size]
    other_mapped = tables[:, 3 * size :]
    scale = gather(given, 2)[:, :size]
    same_mapped = half(scale * (current - mixed).T)
    mixed_mapped = scale * (mixed - other)

    def whole(one, cross, two):
        return jnp.concatenate(
            [jnp.concatenate([one, cross], axis=1), jnp.concatenate([cross.T, two], axis=1)], axis=0
        )

    grams = whole(current, mixed, other)
    mapped_grams = whole(same_mapped, mixed_mapped, other_mapped)
    solved = eliminate(jnp.concatenate([same_mapped, current, current, unit], axis=1), (0, 2 * size))
    step_first = solved[:, size : 2 * size]
    inverse = solved[:, 3 * size :]
    onto_second = scale * step_first
    onto_first = unit - onto_second
    mix = jnp.concatenate([onto_first, onto_second], axis=0)
    following = half(exact(mix, exact(grams, mix, (1, 0)), (0, 0)))
    direction = onto_first + exact(inverse, following, (1, 0))
    mix = jnp.concatenate([direction, onto_second], axis=0)
    curvature = half(exact(mix, exact(mapped_grams, mix, (1, 0)), (0, 0)))
    step_second = eliminate(jnp.concatenate([curvature, following], axis=1), (0,))[:, size:]
    moved = exact(mix, step_second, (1, 0))
    moved_first, moved_second = moved[:size], moved[size:]
    image = scale * moved_first
    basis = jnp.concatenate([gather(given, 0), gather(given, 1), gather(last, 0)], axis=0)
    scratch[0] = exact(jnp.concatenate([step_first + moved_first, moved_second], axis=0), basis[: 2 * size], (0, 0))
    scratch[1] = exact(
        jnp.concatenate([onto_first - image, onto_second + image, -moved_second], axis=0), basis, (0, 0)
    )
    probes = given.shape[2]
    begin = pl.multiple_of(probe[0] * probes, probes)
    for worker in range(out.shape[0]):
        out[worker, 0] = scratch[0, pl.ds(begin, probes), :]
        out[worker, 1] = scratch[1, pl.ds(begin, probes), :]


def fold_body(got, out):
    total = sum_of(got)
    firms, probes = out.shape[0], total.shape[1]
    for firm in range(firms):
        out[firm, :probes, :] = total[firm]
    if out.shape[1] > probes:
        extra = total[firms]
        for item in range(firms + 1, total.shape[0]):
            extra = extra + total[item]
        for firm in range(firms):
            out[firm, probes:, :] = extra


def sum_of(got):
    total = got[0].astype(f32)
    for other in range(1, got.shape[0]):
        total = total + got[other].astype(f32)
    return total


def send(out, values):
    for other in range(out.shape[0]):
        out[other] = values.astype(out.dtype)


def gather_fold_body(got, out):
    send(out, sum_of(got))


def first_body(got, firsts, sent):
    firsts[...] = sum_of(got)
    send(sent, firsts[...])


def second_body(firm, got, firsts, first, second, quotient, sent, seconds):
    total = sum_of(got)
    blocks = total.shape[0] - 1
    ratio = total[blocks, :, :1] / total[blocks, :, TILE // 2 : TILE // 2 + 1]
    quotient[...] = jnp.broadcast_to(ratio, quotient.shape)
    step = NEAR_SECOND // NEAR_FIRST
    near = lax.div(firm[0], NEAR_FIRST) & (step - 1)
    for block in range(blocks):
        seconds[block] = firsts[block * step + near] - total[block] / quotient[...]
    first[...] = firsts[lax.div(firm[0], NEAR_FIRST)]
    second[...] = seconds[lax.div(firm[0], NEAR_SECOND)]
    send(sent, seconds[...])


def third_body(got, sent):
    send(sent, sum_of(got))


def kernel(body, shapes, places, scratch, name, cost=1 << 16):
    return pl.pallas_call(
        body,
        out_shape=shapes,
        in_specs=[pl.BlockSpec(memory_space=place) for place in places],
        out_specs=jax.tree.map(lambda _: pl.BlockSpec(memory_space=pltpu.VMEM), shapes),
        scratch_shapes=scratch,
        compiler_params=pltpu.CompilerParams(vmem_limit_bytes=6 << 20),
        cost_estimate=pl.CostEstimate(flops=cost, transcendentals=0, bytes_accessed=1 << 20),
        name=name,
    )


def exchange(chunks, axis, beside=()):
    chunks, beside = lax.optimization_barrier((chunks, beside))
    got = lax.all_to_all(chunks, axis, 0, 0, tiled=True)
    return lax.optimization_barrier((got, beside))


def local(tiles, tile_rows, tile_firms, worker_ids, sign_words, regular):
    probe_dev = sign_words.shape[0]
    probes = lax.axis_size("probe")
    count = tiles.shape[0]
    blocks = WORKERS * FIRMS
    reg_blocks = regular.reshape(WORKERS, TILE)
    words = jnp.transpose(sign_words, (2, 1, 0))
    at = tuple(lax.axis_index(axis).reshape(1) for axis in (FIRM_AXES, "worker", "probe"))

    VMEM, SMEM, HBM = pltpu.VMEM, pltpu.SMEM, pltpu.HBM
    rows_vmem = VMEM((ROWB_DEV, probe_dev, TILE), f32)
    sums_vmem = VMEM((blocks, probe_dev, TILE), f32)
    cost = 2 * count * probe_dev * TILE * TILE

    def shape(*dims, dtype=f32):
        return jax.ShapeDtypeStruct((*dims, probe_dev, TILE), dtype)

    def placed(array, where):
        return pltpu.with_memory_space_constraint(array, where)

    near_first, far_first = (*FIRM_AXES[2:], "worker"), FIRM_AXES[:2]
    near_second, far_second = (*FIRM_AXES[1:], "worker"), FIRM_AXES[:1]
    peers_first, held_first = NEAR_FIRST * WORKERS, FIRMS // NEAR_FIRST
    peers_second, held_second = NEAR_SECOND * WORKERS, FIRMS // NEAR_SECOND

    parts, tiles = kernel(
        start_body, (shape(blocks), VMEM(tiles.shape, bf16)), [HBM] * 5,
        [
            rows_vmem, pltpu.SemaphoreType.DMA((CHUNKS + 4,)), SMEM(tile_rows.shape, jnp.int32),
            SMEM(tile_firms.shape, jnp.int32), SMEM(words.shape, jnp.int32), VMEM(worker_ids.shape, jnp.int32),
        ],
        "start", cost,
    )(*(placed(array, HBM) for array in (tile_rows, tile_firms, words, worker_ids, tiles)))
    got, at = exchange(parts.reshape(peers_first, held_first, probe_dev, TILE), near_first, at)
    sent = kernel(gather_fold_body, shape(held_first, held_first), [VMEM], [], "fold")(got)
    got, at = exchange(sent, far_first, at)
    firsts, sent = kernel(
        first_body, (shape(held_first), shape(peers_first, held_first, dtype=bf16)), [VMEM], [], "first"
    )(got)

    field, (firsts, *at) = exchange(sent, near_first, (firsts, *at))
    firm, worker, _ = at
    parts = kernel(
        middle_body, shape(peers_second, held_second + 1, dtype=bf16),
        [SMEM, SMEM, SMEM, SMEM, VMEM, VMEM, VMEM, VMEM, VMEM], [rows_vmem, sums_vmem], "middle", 2 * cost,
    )(
        tile_rows, tile_firms, worker, firm, field.reshape(blocks, probe_dev, TILE), firsts, reg_blocks,
        worker_ids, placed(tiles, VMEM),
    )
    got, (firsts, *at) = exchange(parts, near_second, (firsts, *at))
    sent = kernel(gather_fold_body, shape(held_second, held_second + 1), [VMEM], [], "fold")(got)
    got, (firsts, *at) = exchange(sent, far_second, (firsts, *at))
    first, second, quotient, sent = kernel(
        second_body, (shape(), shape(), shape(), shape(peers_second, held_second, dtype=bf16)),
        [SMEM, VMEM, VMEM], [VMEM((held_second, probe_dev, TILE), f32)], "second",
    )(at[0], got, firsts)

    field, (first, second, quotient, *at) = exchange(sent, near_second, (first, second, quotient, *at))
    sent = kernel(
        rows_body, shape(probes, 3 + ROWB_DEV), [SMEM, SMEM, VMEM, VMEM, VMEM, VMEM, VMEM, VMEM], [], "rows", cost
    )(
        tile_rows, tile_firms, field.reshape(blocks, probe_dev, TILE), first, second, quotient, worker_ids,
        placed(tiles, VMEM),
    )
    given, at = exchange(sent, "probe", at)
    firm, worker, probe = at
    parts = kernel(
        last_body, shape(WORKERS, FIRMS + 3, dtype=bf16),
        [SMEM, SMEM, SMEM, SMEM, SMEM, VMEM, VMEM, VMEM],
        [VMEM((ROWB_DEV, 2 * probe_dev, TILE), f32), sums_vmem], "last", cost,
    )(tile_rows, tile_firms, worker, firm, probe, given, reg_blocks, placed(tiles, VMEM))
    got, (given, *at) = exchange(parts, "worker", (given, *at))
    sent = kernel(
        fold_body, jax.ShapeDtypeStruct((FIRMS, 2 * probe_dev, TILE), f32), [VMEM], [], "fold_last"
    )(got)
    got, (given, *at) = exchange(sent, FIRM_AXES, (given, *at))
    sent = kernel(
        third_body, jax.ShapeDtypeStruct((probes, 2 * probe_dev, TILE), f32), [VMEM], [], "third"
    )(got)
    last, (given, *at) = exchange(sent, "probe", (given, *at))
    outs = kernel(
        final_body, shape(WORKERS, 2), [SMEM, VMEM, VMEM],
        [VMEM((2, probes * probe_dev, TILE), f32)], "final", cost // 4,
    )(at[2], given, last.reshape(probes, 2, probe_dev, TILE))
    outs, _ = exchange(outs, "worker")
    outs = jnp.transpose(outs, (1, 2, 0, 3)).reshape(2, probe_dev, WORKERS * TILE)
    return (outs[0], outs[1])


def solution(mesh):
    sizes = (FIRMS // NEAR_SECOND, NEAR_SECOND // NEAR_FIRST, NEAR_FIRST)
    split = jax.sharding.Mesh(
        mesh.devices.reshape(*sizes, WORKERS, mesh.shape["probe"]), (*FIRM_AXES, "worker", "probe")
    )
    shard = (*FIRM_AXES, "worker")
    placed = (
        P(shard, None, None),
        P(shard, None),
        P(shard, None),
        P(shard, None),
        P("probe", shard, None),
        P(FIRM_AXES),
    )
    return jax.shard_map(
        local,
        mesh=split,
        in_specs=placed,
        out_specs=(P("probe", FIRM_AXES), P("probe", FIRM_AXES)),
        check_vma=False,
    )
```

```python
import jax
import jax.numpy as jnp
from jax import lax
from jax.experimental import pallas as pl
from jax.experimental.pallas import tpu as pltpu
from jax.sharding import PartitionSpec as P

TILE = 128
ROWB_DEV = 4
ROWS_DEV = 512
SHARD_WORKERS = 128
BITS = 30
CHUNKS = 4
PANEL = 16
WORKERS = 8
FIRMS = 16
NEAR_FIRST = 2
NEAR_SECOND = 2
FIRM_AXES = ("firm_far", "firm_middle", "firm_near")

largest_value = lax.Precision.HIGHEST
f32 = jnp.float32
bf16 = jnp.bfloat16


def dot(left, right, dims, precision=None):
    return lax.dot_general(
        left, right, ((dims[:1], dims[1:]), ((), ())), precision=precision, preferred_element_type=f32
    )


def exact(left, right, dims):
    return dot(left, right, dims, largest_value)


def three_parts(values):
    high = values.astype(bf16)
    rest = values - high.astype(f32)
    middle = rest.astype(bf16)
    low = (rest - middle.astype(f32)).astype(bf16)
    return high, middle, low


def demean(values, worker_ids):
    probes = values.shape[0]
    workers = lax.broadcasted_iota(jnp.int32, (SHARD_WORKERS, ROWS_DEV), 0)
    onehot = jnp.where(workers == worker_ids, 1.0, 0.0).astype(bf16)
    stacked = jnp.concatenate([*(part.astype(f32) for part in three_parts(values)), jnp.ones_like(values)], axis=0)
    sums = dot(stacked.astype(bf16), onehot, (1, 1))
    totals = (sums[2 * probes : 3 * probes] + sums[probes : 2 * probes]) + sums[:probes]
    means = totals / sums[3 * probes :]
    stacked = jnp.concatenate([part.astype(f32) for part in three_parts(means)], axis=0)
    spread = dot(stacked.astype(bf16), onehot, (1, 0))
    return values - ((spread[2 * probes : 3 * probes] + spread[probes : 2 * probes]) + spread[:probes])


def fetch(tiles_hbm, tiles, arrived, small):
    size = tiles.shape[0] // CHUNKS

    def copy(chunk):
        part = pl.ds(chunk * size, size)
        return pltpu.make_async_copy(tiles_hbm.at[part], tiles.at[part], arrived.at[chunk])

    tables = fetch_small(arrived, small)
    for chunk in range(CHUNKS):
        copy(chunk).start()
    for table in tables:
        table.wait()
    return lambda chunk: copy(chunk).wait()


def fetch_small(arrived, small):
    tables = [pltpu.make_async_copy(*both, arrived.at[CHUNKS + item]) for item, both in enumerate(small)]
    for table in tables:
        table.start()
    return tables


def place_of(block, near):
    firm, worker = block >> (WORKERS.bit_length() - 1), block & (WORKERS - 1)
    shift = near.bit_length() - 1
    return ((firm & (near - 1)) * WORKERS + worker) * (FIRMS // near) + (firm >> shift)


def stack(pieces):
    return jnp.concatenate([piece.astype(f32) for piece in pieces], axis=0).astype(bf16)


def forward(tile_rows, tile_firms, field, tiles, near):
    total = None
    for tile in range(0, tiles.shape[0], 2):
        pieces = [field[place_of(tile_firms[0, tile + item], near)] for item in range(2)]
        probes = pieces[0].shape[0]
        weights = jnp.concatenate([tiles[tile], tiles[tile + 1]], axis=0)
        both = dot(stack(pieces), weights, (1, 1))
        if total is None:
            total = [jnp.zeros((probes, TILE), f32) for block in range(ROWB_DEV)]
        for item in range(2):
            image = both[item * probes : (item + 1) * probes, item * TILE : (item + 1) * TILE]
            row = tile_rows[0, tile + item]
            total = [old + jnp.where(row == block, image, 0.0) for block, old in enumerate(total)]
    return total


def adjoint(tile_rows, tile_firms, rows, tiles, out, near, wait=None):
    out[...] = jnp.zeros_like(out)
    probes, lines = out.shape[1], rows.shape[1]
    size = tiles.shape[0] // CHUNKS
    for tile in range(0, tiles.shape[0], 2):
        if wait is not None and tile % size == 0:
            wait(tile // size)
        weights = jnp.concatenate([tiles[tile], tiles[tile + 1]], axis=1)
        both = dot(stack([rows[tile_rows[0, tile + item]] for item in range(2)]), weights, (1, 0))
        for item in range(2):
            place = place_of(tile_firms[0, tile + item], near)
            image = out[place]
            for begin in range(item * lines, (item + 1) * lines, probes):
                image = image + both[begin : begin + probes, item * TILE : (item + 1) * TILE]
            out[place] = image


def put_rows(rows, values):
    for block in range(ROWB_DEV):
        rows[block] = values[:, block * TILE : (block + 1) * TILE].astype(bf16).astype(f32)


def put_two_terms(rows, values):
    high = values.astype(bf16).astype(f32)
    rows[...] = jnp.concatenate([high, (values - high).astype(bf16).astype(f32)], axis=0)


def put_parts(out, total, extras):
    peers, blocks = out.shape[0], out.shape[1] - len(extras)
    for peer in range(peers):
        for block in range(blocks):
            out[peer, block] = total[peer * blocks + block].astype(out.dtype)
        for item, extra in enumerate(extras):
            out[peer, blocks + item] = extra.astype(out.dtype)


def add_ridge(out, firm, worker, near, regular, own):
    place = place_of(firm * WORKERS + worker, near)
    out[place] = out[place] + regular[pl.ds(worker, 1), :] * own


def start_body(
    rows_hbm, firms_hbm, words_hbm, ids_hbm, tiles_hbm,
    out, tiles, rows, arrived, tile_rows, tile_firms, words, worker_ids,
):
    small = [(rows_hbm, tile_rows), (firms_hbm, tile_firms), (words_hbm, words), (ids_hbm, worker_ids)]
    wait = fetch(tiles_hbm, tiles, arrived, small)
    words_row, blocks, probes = words.shape
    lanes = lax.broadcasted_iota(jnp.int32, (probes, TILE), 1)
    lines = lax.broadcasted_iota(jnp.int32, (probes, TILE), 0)
    word_of = lax.div(lanes, jnp.int32(BITS))
    bit = lanes - word_of * BITS
    chosen = [jnp.zeros((probes, TILE), jnp.int32) for block in range(blocks)]
    for word in range(words_row):
        for probe in range(probes):
            here = (word_of == word) & (lines == probe)
            chosen = [jnp.where(here, words[word, block, probe], old) for block, old in enumerate(chosen)]
    signs = [(2 * (lax.shift_right_logical(old, bit) & 1) - 1).astype(f32) for old in chosen]
    put_rows(rows, demean(jnp.concatenate(signs, axis=1), worker_ids[...]))
    adjoint(tile_rows, tile_firms, rows, tiles, out, NEAR_FIRST, wait)


def middle_body(
    tile_rows, tile_firms, worker, firm, field, firsts, regular, worker_ids, tiles,
    out, rows, feature_sums,
):
    total = forward(tile_rows, tile_firms, field, tiles, NEAR_FIRST)
    values = demean(jnp.concatenate(total, axis=1), worker_ids[...])
    put_rows(rows, values)
    adjoint(tile_rows, tile_firms, rows, tiles, feature_sums, NEAR_SECOND)
    own = firsts[lax.div(firm[0], NEAR_FIRST)]
    add_ridge(feature_sums, firm[0], worker[0], NEAR_SECOND, regular, own)
    squares = own * own
    above = jnp.sum(values * values, axis=1, keepdims=True)
    above = above + jnp.sum(squares * regular[pl.ds(worker[0], 1), :], axis=1, keepdims=True)
    below = jnp.sum(squares, axis=1, keepdims=True)
    lanes = lax.broadcasted_iota(jnp.int32, own.shape, 1)
    put_parts(out, feature_sums, [jnp.where(lanes < TILE // 2, above, below)])


def rows_body(tile_rows, tile_firms, field, first, second, quotient, worker_ids, tiles, out):
    total = forward(tile_rows, tile_firms, field, tiles, NEAR_SECOND)
    values = demean(jnp.concatenate(total, axis=1), worker_ids[...])
    for probe in range(out.shape[0]):
        out[probe, 0] = first[...]
        out[probe, 1] = second[...]
        out[probe, 2] = quotient[...]
        for block in range(ROWB_DEV):
            out[probe, 3 + block] = values[:, block * TILE : (block + 1) * TILE]


def last_body(
    tile_rows, tile_firms, worker, firm, probe, given, regular, tiles,
    out, rows, feature_sums,
):
    gather = lambda item: jnp.concatenate([given[other, item] for other in range(given.shape[0])], axis=0)
    own = lambda item: given[probe[0], item]
    first, second = own(0), own(1)
    first_all, second_all = gather(0), gather(1)
    mine = [own(3 + block) for block in range(ROWB_DEV)]
    for block in range(ROWB_DEV):
        put_two_terms(rows.at[block], mine[block])
    left = jnp.concatenate([*mine, second * regular[pl.ds(worker[0], 1), :]], axis=1)
    right = jnp.concatenate([*(gather(3 + block) for block in range(ROWB_DEV)), second_all], axis=1)
    extra = jnp.concatenate(
        [
            exact(first, first_all, (1, 1)),
            exact(first, second_all, (1, 1)),
            exact(second, second_all, (1, 1)),
            exact(left, right, (1, 1)),
        ],
        axis=1,
    )
    adjoint(tile_rows, tile_firms, rows, tiles, feature_sums, 1)
    add_ridge(feature_sums, firm[0], worker[0], 1, regular, second)
    put_parts(out, feature_sums, three_parts(extra))


def eliminate(table, pivots):
    size, width = table.shape
    lanes = lax.broadcasted_iota(jnp.int32, (size, width), 1)
    lines = lax.broadcasted_iota(jnp.int32, (size, width), 0)

    def spread(at):
        column = jnp.broadcast_to(table[:, pivots[0] + at : pivots[0] + at + 1], (size, width))
        for begin in pivots[1:]:
            other = jnp.broadcast_to(table[:, begin + at : begin + at + 1], (size, width))
            column = jnp.where(lanes < begin, column, other)
        return column

    for start in range(0, size, PANEL):
        columns = [spread(start + item) for item in range(PANEL)]
        for item, column in enumerate(columns):
            at = start + item
            inverse = 1.0 / column[at : at + 1, :]
            line = table[at : at + 1, :] * inverse
            table = jnp.where(lines == at, line, table - column * line)
            for later in range(item + 1, PANEL):
                factor = columns[later][at : at + 1, :] * inverse
                columns[later] = jnp.where(lines == at, factor, columns[later] - column * factor)
    return table


def final_body(probe, given, last, out, scratch):
    size = given.shape[0] * given.shape[2]
    gather = lambda ref, item: jnp.concatenate([ref[other, item] for other in range(ref.shape[0])], axis=0)
    half = lambda matrix: 0.5 * (matrix + matrix.T)
    lines = lax.broadcasted_iota(jnp.int32, (size, size), 0)
    lanes = lax.broadcasted_iota(jnp.int32, (size, size), 1)
    unit = jnp.where(lines == lanes, 1.0, 0.0)
    tables = gather(last, 1)
    current = half(tables[:, :size])
    mixed = tables[:, size : 2 * size]
    other = tables[:, 2 * size : 3 * size]
    other_mapped = tables[:, 3 * size :]
    scale = gather(given, 2)[:, :size]
    same_mapped = half(scale * (current - mixed).T)
    mixed_mapped = scale * (mixed - other)

    def whole(one, cross, two):
        return jnp.concatenate(
            [jnp.concatenate([one, cross], axis=1), jnp.concatenate([cross.T, two], axis=1)], axis=0
        )

    grams = whole(current, mixed, other)
    mapped_grams = whole(same_mapped, mixed_mapped, other_mapped)
    solved = eliminate(jnp.concatenate([same_mapped, current, current, unit], axis=1), (0, 2 * size))
    step_first = solved[:, size : 2 * size]
    inverse = solved[:, 3 * size :]
    onto_second = scale * step_first
    onto_first = unit - onto_second
    mix = jnp.concatenate([onto_first, onto_second], axis=0)
    following = half(exact(mix, exact(grams, mix, (1, 0)), (0, 0)))
    direction = onto_first + exact(inverse, following, (1, 0))
    mix = jnp.concatenate([direction, onto_second], axis=0)
    curvature = half(exact(mix, exact(mapped_grams, mix, (1, 0)), (0, 0)))
    step_second = eliminate(jnp.concatenate([curvature, following], axis=1), (0,))[:, size:]
    moved = exact(mix, step_second, (1, 0))
    moved_first, moved_second = moved[:size], moved[size:]
    image = scale * moved_first
    basis = jnp.concatenate([gather(given, 0), gather(given, 1), gather(last, 0)], axis=0)
    scratch[0] = exact(jnp.concatenate([step_first + moved_first, moved_second], axis=0), basis[: 2 * size], (0, 0))
    scratch[1] = exact(
        jnp.concatenate([onto_first - image, onto_second + image, -moved_second], axis=0), basis, (0, 0)
    )
    probes = given.shape[2]
    begin = pl.multiple_of(probe[0] * probes, probes)
    for worker in range(out.shape[0]):
        out[worker, 0] = scratch[0, pl.ds(begin, probes), :]
        out[worker, 1] = scratch[1, pl.ds(begin, probes), :]


def fold_body(got, out):
    total = sum_of(got)
    firms, probes = out.shape[0], total.shape[1]
    for firm in range(firms):
        out[firm, :probes, :] = total[firm]
    if out.shape[1] > probes:
        extra = total[firms]
        for item in range(firms + 1, total.shape[0]):
            extra = extra + total[item]
        for firm in range(firms):
            out[firm, probes:, :] = extra


def sum_of(got):
    total = got[0].astype(f32)
    for other in range(1, got.shape[0]):
        total = total + got[other].astype(f32)
    return total


def send(out, values):
    for other in range(out.shape[0]):
        out[other] = values.astype(out.dtype)


def gather_fold_body(got, out):
    send(out, sum_of(got))


def first_body(got, firsts, sent):
    firsts[...] = sum_of(got)
    send(sent, firsts[...])


def second_body(firm, got, firsts, first, second, quotient, sent, seconds):
    total = sum_of(got)
    blocks = total.shape[0] - 1
    ratio = total[blocks, :, :1] / total[blocks, :, TILE // 2 : TILE // 2 + 1]
    quotient[...] = jnp.broadcast_to(ratio, quotient.shape)
    step = NEAR_SECOND // NEAR_FIRST
    near = lax.div(firm[0], NEAR_FIRST) & (step - 1)
    for block in range(blocks):
        seconds[block] = firsts[block * step + near] - total[block] / quotient[...]
    first[...] = firsts[lax.div(firm[0], NEAR_FIRST)]
    second[...] = seconds[lax.div(firm[0], NEAR_SECOND)]
    send(sent, seconds[...])


def third_body(got, sent):
    send(sent, sum_of(got))


def kernel(body, shapes, places, scratch, name, cost=1 << 16):
    return pl.pallas_call(
        body,
        out_shape=shapes,
        in_specs=[pl.BlockSpec(memory_space=place) for place in places],
        out_specs=jax.tree.map(lambda _: pl.BlockSpec(memory_space=pltpu.VMEM), shapes),
        scratch_shapes=scratch,
        compiler_params=pltpu.CompilerParams(vmem_limit_bytes=6 << 20),
        cost_estimate=pl.CostEstimate(flops=cost, transcendentals=0, bytes_accessed=1 << 20),
        name=name,
    )


def exchange(chunks, axis, beside=()):
    chunks, beside = lax.optimization_barrier((chunks, beside))
    got = lax.all_to_all(chunks, axis, 0, 0, tiled=True)
    return lax.optimization_barrier((got, beside))


def local(tiles, tile_rows, tile_firms, worker_ids, sign_words, regular):
    probe_dev = sign_words.shape[0]
    probes = lax.axis_size("probe")
    count = tiles.shape[0]
    blocks = WORKERS * FIRMS
    reg_blocks = regular.reshape(WORKERS, TILE)
    words = jnp.transpose(sign_words, (2, 1, 0))
    at = tuple(lax.axis_index(axis).reshape(1) for axis in (FIRM_AXES, "worker", "probe"))

    VMEM, SMEM, HBM = pltpu.VMEM, pltpu.SMEM, pltpu.HBM
    rows_vmem = VMEM((ROWB_DEV, probe_dev, TILE), f32)
    sums_vmem = VMEM((blocks, probe_dev, TILE), f32)
    cost = 2 * count * probe_dev * TILE * TILE

    def shape(*dims, dtype=f32):
        return jax.ShapeDtypeStruct((*dims, probe_dev, TILE), dtype)

    def placed(array, where):
        return pltpu.with_memory_space_constraint(array, where)

    near_first, far_first = (*FIRM_AXES[2:], "worker"), FIRM_AXES[:2]
    near_second, far_second = (*FIRM_AXES[1:], "worker"), FIRM_AXES[:1]
    peers_first, held_first = NEAR_FIRST * WORKERS, FIRMS // NEAR_FIRST
    peers_second, held_second = NEAR_SECOND * WORKERS, FIRMS // NEAR_SECOND

    parts, tiles = kernel(
        start_body, (shape(blocks), VMEM(tiles.shape, bf16)), [HBM] * 5,
        [
            rows_vmem, pltpu.SemaphoreType.DMA((CHUNKS + 4,)), SMEM(tile_rows.shape, jnp.int32),
            SMEM(tile_firms.shape, jnp.int32), SMEM(words.shape, jnp.int32), VMEM(worker_ids.shape, jnp.int32),
        ],
        "start", cost,
    )(*(placed(array, HBM) for array in (tile_rows, tile_firms, words, worker_ids, tiles)))
    got, at = exchange(parts.reshape(peers_first, held_first, probe_dev, TILE), near_first, at)
    sent = kernel(gather_fold_body, shape(held_first, held_first), [VMEM], [], "fold")(got)
    got, at = exchange(sent, far_first, at)
    firsts, sent = kernel(
        first_body, (shape(held_first), shape(peers_first, held_first, dtype=bf16)), [VMEM], [], "first"
    )(got)

    field, (firsts, *at) = exchange(sent, near_first, (firsts, *at))
    firm, worker, _ = at
    parts = kernel(
        middle_body, shape(peers_second, held_second + 1),
        [SMEM, SMEM, SMEM, SMEM, VMEM, VMEM, VMEM, VMEM, VMEM], [rows_vmem, sums_vmem], "middle", 2 * cost,
    )(
        tile_rows, tile_firms, worker, firm, field.reshape(blocks, probe_dev, TILE), firsts, reg_blocks,
        worker_ids, placed(tiles, VMEM),
    )
    got, (firsts, *at) = exchange(parts, near_second, (firsts, *at))
    sent = kernel(gather_fold_body, shape(held_second, held_second + 1, dtype=bf16), [VMEM], [], "fold")(got)
    got, (firsts, *at) = exchange(sent, far_second, (firsts, *at))
    first, second, quotient, sent = kernel(
        second_body, (shape(), shape(), shape(), shape(peers_second, held_second, dtype=bf16)),
        [SMEM, VMEM, VMEM], [VMEM((held_second, probe_dev, TILE), f32)], "second",
    )(at[0], got, firsts)

    field, (first, second, quotient, *at) = exchange(sent, near_second, (first, second, quotient, *at))
    sent = kernel(
        rows_body, shape(probes, 3 + ROWB_DEV), [SMEM, SMEM, VMEM, VMEM, VMEM, VMEM, VMEM, VMEM], [], "rows", cost
    )(
        tile_rows, tile_firms, field.reshape(blocks, probe_dev, TILE), first, second, quotient, worker_ids,
        placed(tiles, VMEM),
    )
    given, at = exchange(sent, "probe", at)
    firm, worker, probe = at
    parts = kernel(
        last_body, shape(WORKERS, FIRMS + 3, dtype=bf16),
        [SMEM, SMEM, SMEM, SMEM, SMEM, VMEM, VMEM, VMEM],
        [VMEM((ROWB_DEV, 2 * probe_dev, TILE), f32), sums_vmem], "last", cost,
    )(tile_rows, tile_firms, worker, firm, probe, given, reg_blocks, placed(tiles, VMEM))
    got, (given, *at) = exchange(parts, "worker", (given, *at))
    sent = kernel(
        fold_body, jax.ShapeDtypeStruct((FIRMS, 2 * probe_dev, TILE), f32), [VMEM], [], "fold_last"
    )(got)
    got, (given, *at) = exchange(sent, FIRM_AXES, (given, *at))
    sent = kernel(
        third_body, jax.ShapeDtypeStruct((probes, 2 * probe_dev, TILE), f32), [VMEM], [], "third"
    )(got)
    last, (given, *at) = exchange(sent, "probe", (given, *at))
    outs = kernel(
        final_body, shape(WORKERS, 2), [SMEM, VMEM, VMEM],
        [VMEM((2, probes * probe_dev, TILE), f32)], "final", cost // 4,
    )(at[2], given, last.reshape(probes, 2, probe_dev, TILE))
    outs, _ = exchange(outs, "worker")
    outs = jnp.transpose(outs, (1, 2, 0, 3)).reshape(2, probe_dev, WORKERS * TILE)
    return (outs[0], outs[1])


def solution(mesh):
    sizes = (FIRMS // NEAR_SECOND, NEAR_SECOND // NEAR_FIRST, NEAR_FIRST)
    split = jax.sharding.Mesh(
        mesh.devices.reshape(*sizes, WORKERS, mesh.shape["probe"]), (*FIRM_AXES, "worker", "probe")
    )
    shard = (*FIRM_AXES, "worker")
    placed = (
        P(shard, None, None),
        P(shard, None),
        P(shard, None),
        P(shard, None),
        P("probe", shard, None),
        P(FIRM_AXES),
    )
    return jax.shard_map(
        local,
        mesh=split,
        in_specs=placed,
        out_specs=(P("probe", FIRM_AXES), P("probe", FIRM_AXES)),
        check_vma=False,
    )
```

```python
import jax
import jax.numpy as jnp
from jax import lax
from jax.experimental import pallas as pl
from jax.experimental.pallas import tpu as pltpu
from jax.sharding import PartitionSpec as P

TILE = 128
ROWB_DEV = 4
ROWS_DEV = 512
SHARD_WORKERS = 128
BITS = 30
CHUNKS = 4
PANEL = 16
WORKERS = 8
FIRMS = 16
NEAR_FIRST = 2
NEAR_SECOND = 2
FIRM_AXES = ("firm_far", "firm_middle", "firm_near")

largest_value = lax.Precision.HIGHEST
f32 = jnp.float32
bf16 = jnp.bfloat16


def dot(left, right, dims, precision=None):
    return lax.dot_general(
        left, right, ((dims[:1], dims[1:]), ((), ())), precision=precision, preferred_element_type=f32
    )


def exact(left, right, dims):
    return dot(left, right, dims, largest_value)


def three_parts(values):
    high = values.astype(bf16)
    rest = values - high.astype(f32)
    middle = rest.astype(bf16)
    low = (rest - middle.astype(f32)).astype(bf16)
    return high, middle, low


def demean(values, worker_ids):
    probes = values.shape[0]
    workers = lax.broadcasted_iota(jnp.int32, (SHARD_WORKERS, ROWS_DEV), 0)
    onehot = jnp.where(workers == worker_ids, 1.0, 0.0).astype(bf16)
    stacked = jnp.concatenate([*(part.astype(f32) for part in three_parts(values)), jnp.ones_like(values)], axis=0)
    sums = dot(stacked.astype(bf16), onehot, (1, 1))
    totals = (sums[2 * probes : 3 * probes] + sums[probes : 2 * probes]) + sums[:probes]
    means = totals / sums[3 * probes :]
    stacked = jnp.concatenate([part.astype(f32) for part in three_parts(means)], axis=0)
    spread = dot(stacked.astype(bf16), onehot, (1, 0))
    return values - ((spread[2 * probes : 3 * probes] + spread[probes : 2 * probes]) + spread[:probes])


def fetch(tiles_hbm, tiles, arrived, small):
    size = tiles.shape[0] // CHUNKS

    def copy(chunk):
        part = pl.ds(chunk * size, size)
        return pltpu.make_async_copy(tiles_hbm.at[part], tiles.at[part], arrived.at[chunk])

    tables = fetch_small(arrived, small)
    for chunk in range(CHUNKS):
        copy(chunk).start()
    for table in tables:
        table.wait()
    return lambda chunk: copy(chunk).wait()


def fetch_small(arrived, small):
    tables = [pltpu.make_async_copy(*both, arrived.at[CHUNKS + item]) for item, both in enumerate(small)]
    for table in tables:
        table.start()
    return tables


def place_of(block, near):
    firm, worker = block >> (WORKERS.bit_length() - 1), block & (WORKERS - 1)
    shift = near.bit_length() - 1
    return ((firm & (near - 1)) * WORKERS + worker) * (FIRMS // near) + (firm >> shift)


def stack(pieces):
    return jnp.concatenate([piece.astype(f32) for piece in pieces], axis=0).astype(bf16)


def forward(tile_rows, tile_firms, field, tiles, near):
    total = None
    for tile in range(0, tiles.shape[0], 2):
        pieces = [field[place_of(tile_firms[0, tile + item], near)] for item in range(2)]
        probes = pieces[0].shape[0]
        weights = jnp.concatenate([tiles[tile], tiles[tile + 1]], axis=0)
        both = dot(stack(pieces), weights, (1, 1))
        if total is None:
            total = [jnp.zeros((probes, TILE), f32) for block in range(ROWB_DEV)]
        for item in range(2):
            image = both[item * probes : (item + 1) * probes, item * TILE : (item + 1) * TILE]
            row = tile_rows[0, tile + item]
            total = [old + jnp.where(row == block, image, 0.0) for block, old in enumerate(total)]
    return total


def adjoint(tile_rows, tile_firms, rows, tiles, out, near, wait=None):
    out[...] = jnp.zeros_like(out)
    probes, lines = out.shape[1], rows.shape[1]
    size = tiles.shape[0] // CHUNKS
    for tile in range(0, tiles.shape[0], 2):
        if wait is not None and tile % size == 0:
            wait(tile // size)
        weights = jnp.concatenate([tiles[tile], tiles[tile + 1]], axis=1)
        both = dot(stack([rows[tile_rows[0, tile + item]] for item in range(2)]), weights, (1, 0))
        for item in range(2):
            place = place_of(tile_firms[0, tile + item], near)
            image = out[place]
            for begin in range(item * lines, (item + 1) * lines, probes):
                image = image + both[begin : begin + probes, item * TILE : (item + 1) * TILE]
            out[place] = image


def put_rows(rows, values):
    for block in range(ROWB_DEV):
        rows[block] = values[:, block * TILE : (block + 1) * TILE].astype(bf16).astype(f32)


def put_two_terms(rows, values):
    high = values.astype(bf16).astype(f32)
    rows[...] = jnp.concatenate([high, (values - high).astype(bf16).astype(f32)], axis=0)


def put_parts(out, total, extras):
    peers, blocks = out.shape[0], out.shape[1] - len(extras)
    for peer in range(peers):
        for block in range(blocks):
            out[peer, block] = total[peer * blocks + block].astype(out.dtype)
        for item, extra in enumerate(extras):
            out[peer, blocks + item] = extra.astype(out.dtype)


def add_ridge(out, firm, worker, near, regular, own):
    place = place_of(firm * WORKERS + worker, near)
    out[place] = out[place] + regular[pl.ds(worker, 1), :] * own


def start_body(
    rows_hbm, firms_hbm, words_hbm, ids_hbm, tiles_hbm,
    out, tiles, rows, arrived, tile_rows, tile_firms, words, worker_ids,
):
    small = [(rows_hbm, tile_rows), (firms_hbm, tile_firms), (words_hbm, words), (ids_hbm, worker_ids)]
    wait = fetch(tiles_hbm, tiles, arrived, small)
    words_row, blocks, probes = words.shape
    lanes = lax.broadcasted_iota(jnp.int32, (probes, TILE), 1)
    lines = lax.broadcasted_iota(jnp.int32, (probes, TILE), 0)
    word_of = lax.div(lanes, jnp.int32(BITS))
    bit = lanes - word_of * BITS
    chosen = [jnp.zeros((probes, TILE), jnp.int32) for block in range(blocks)]
    for word in range(words_row):
        for probe in range(probes):
            here = (word_of == word) & (lines == probe)
            chosen = [jnp.where(here, words[word, block, probe], old) for block, old in enumerate(chosen)]
    signs = [(2 * (lax.shift_right_logical(old, bit) & 1) - 1).astype(f32) for old in chosen]
    put_rows(rows, demean(jnp.concatenate(signs, axis=1), worker_ids[...]))
    adjoint(tile_rows, tile_firms, rows, tiles, out, NEAR_FIRST, wait)


def middle_body(
    tile_rows, tile_firms, worker, firm, field, firsts, regular, worker_ids, tiles,
    out, rows, feature_sums,
):
    total = forward(tile_rows, tile_firms, field, tiles, NEAR_FIRST)
    values = demean(jnp.concatenate(total, axis=1), worker_ids[...])
    put_rows(rows, values)
    adjoint(tile_rows, tile_firms, rows, tiles, feature_sums, NEAR_SECOND)
    own = firsts[lax.div(firm[0], NEAR_FIRST)]
    add_ridge(feature_sums, firm[0], worker[0], NEAR_SECOND, regular, own)
    squares = own * own
    above = jnp.sum(values * values, axis=1, keepdims=True)
    above = above + jnp.sum(squares * regular[pl.ds(worker[0], 1), :], axis=1, keepdims=True)
    below = jnp.sum(squares, axis=1, keepdims=True)
    lanes = lax.broadcasted_iota(jnp.int32, own.shape, 1)
    put_parts(out, feature_sums, [jnp.where(lanes < TILE // 2, above, below)])


def rows_body(tile_rows, tile_firms, field, first, second, quotient, worker_ids, tiles, out):
    total = forward(tile_rows, tile_firms, field, tiles, NEAR_SECOND)
    values = demean(jnp.concatenate(total, axis=1), worker_ids[...])
    for probe in range(out.shape[0]):
        out[probe, 0] = first[...]
        out[probe, 1] = second[...]
        out[probe, 2] = quotient[...]
        for block in range(ROWB_DEV):
            out[probe, 3 + block] = values[:, block * TILE : (block + 1) * TILE]


def last_body(
    tile_rows, tile_firms, worker, firm, probe, given, regular, tiles,
    out, rows, feature_sums,
):
    gather = lambda item: jnp.concatenate([given[other, item] for other in range(given.shape[0])], axis=0)
    own = lambda item: given[probe[0], item]
    first, second = own(0), own(1)
    first_all, second_all = gather(0), gather(1)
    mine = [own(3 + block) for block in range(ROWB_DEV)]
    for block in range(ROWB_DEV):
        put_two_terms(rows.at[block], mine[block])
    left = jnp.concatenate([*mine, second * regular[pl.ds(worker[0], 1), :]], axis=1)
    right = jnp.concatenate([*(gather(3 + block) for block in range(ROWB_DEV)), second_all], axis=1)
    extra = jnp.concatenate(
        [
            exact(first, first_all, (1, 1)),
            exact(first, second_all, (1, 1)),
            exact(second, second_all, (1, 1)),
            exact(left, right, (1, 1)),
        ],
        axis=1,
    )
    adjoint(tile_rows, tile_firms, rows, tiles, feature_sums, 1)
    add_ridge(feature_sums, firm[0], worker[0], 1, regular, second)
    put_parts(out, feature_sums, three_parts(extra))


def eliminate(table, pivots):
    size, width = table.shape
    lanes = lax.broadcasted_iota(jnp.int32, (size, width), 1)
    lines = lax.broadcasted_iota(jnp.int32, (size, width), 0)

    def spread(at):
        column = jnp.broadcast_to(table[:, pivots[0] + at : pivots[0] + at + 1], (size, width))
        for begin in pivots[1:]:
            other = jnp.broadcast_to(table[:, begin + at : begin + at + 1], (size, width))
            column = jnp.where(lanes < begin, column, other)
        return column

    for start in range(0, size, PANEL):
        columns = [spread(start + item) for item in range(PANEL)]
        for item, column in enumerate(columns):
            at = start + item
            inverse = 1.0 / column[at : at + 1, :]
            line = table[at : at + 1, :] * inverse
            table = jnp.where(lines == at, line, table - column * line)
            for later in range(item + 1, PANEL):
                factor = columns[later][at : at + 1, :] * inverse
                columns[later] = jnp.where(lines == at, factor, columns[later] - column * factor)
    return table


def final_body(probe, given, last, solution_out, residual_out, basis, mixes):
    size = given.shape[0] * given.shape[2]
    gather = lambda ref, item: jnp.concatenate([ref[other, item] for other in range(given.shape[0])], axis=0)
    half = lambda matrix: 0.5 * (matrix + matrix.T)
    lines = lax.broadcasted_iota(jnp.int32, (size, size), 0)
    lanes = lax.broadcasted_iota(jnp.int32, (size, size), 1)
    unit = jnp.where(lines == lanes, 1.0, 0.0)
    tables = gather(last, 1)
    current = half(tables[:, :size])
    mixed = tables[:, size : 2 * size]
    other = tables[:, 2 * size : 3 * size]
    other_mapped = tables[:, 3 * size :]
    scale = gather(given, 2)[:, :size]
    same_mapped = half(scale * (current - mixed).T)
    mixed_mapped = scale * (mixed - other)

    def whole(one, cross, two):
        return jnp.concatenate(
            [jnp.concatenate([one, cross], axis=1), jnp.concatenate([cross.T, two], axis=1)], axis=0
        )

    grams = whole(current, mixed, other)
    mapped_grams = whole(same_mapped, mixed_mapped, other_mapped)
    solved = eliminate(jnp.concatenate([same_mapped, current, current, unit], axis=1), (0, 2 * size))
    step_first = solved[:, size : 2 * size]
    inverse = solved[:, 3 * size :]
    onto_second = scale * step_first
    onto_first = unit - onto_second
    mix = jnp.concatenate([onto_first, onto_second], axis=0)
    following = half(exact(mix, exact(grams, mix, (1, 0)), (0, 0)))
    direction = onto_first + exact(inverse, following, (1, 0))
    mix = jnp.concatenate([direction, onto_second], axis=0)
    curvature = half(exact(mix, exact(mapped_grams, mix, (1, 0)), (0, 0)))
    step_second = eliminate(jnp.concatenate([curvature, following], axis=1), (0,))[:, size:]
    moved = exact(mix, step_second, (1, 0))
    moved_first, moved_second = moved[:size], moved[size:]
    image = scale * moved_first
    probes = given.shape[2]
    for other in range(last.shape[0]):
        worker, part = other // given.shape[0], other % given.shape[0]
        for item, kind in enumerate((2, 3, 0)):
            line = item * size + part * probes
            basis[line : line + probes, worker * TILE : (worker + 1) * TILE] = last[other, kind]
    empty = jnp.zeros((size, size), f32)
    mixes[0] = jnp.concatenate([step_first + moved_first, moved_second, empty, empty], axis=0).T
    mixes[1] = jnp.concatenate([onto_first - image, onto_second + image, -moved_second, empty], axis=0).T
    begin = pl.multiple_of(probe[0] * probes, probes)
    both = jnp.concatenate([mixes[item, pl.ds(begin, probes), :][:, : 3 * size] for item in range(2)], axis=0)
    outs = exact(both, basis[...], (1, 0))
    solution_out[...] = outs[:probes]
    residual_out[...] = outs[probes:]


def fold_body(got, out):
    total = sum_of(got)
    firms, probes = out.shape[0], total.shape[1]
    for firm in range(firms):
        out[firm, :probes, :] = total[firm]
    if out.shape[1] > probes:
        extra = total[firms]
        for item in range(firms + 1, total.shape[0]):
            extra = extra + total[item]
        for firm in range(firms):
            out[firm, probes:, :] = extra


def sum_of(got):
    total = got[0].astype(f32)
    for other in range(1, got.shape[0]):
        total = total + got[other].astype(f32)
    return total


def send(out, values):
    for other in range(out.shape[0]):
        out[other] = values.astype(out.dtype)


def gather_fold_body(got, out):
    send(out, sum_of(got))


def first_body(got, firsts, sent):
    firsts[...] = sum_of(got)
    send(sent, firsts[...])


def second_body(firm, got, firsts, first, second, quotient, sent, seconds):
    total = sum_of(got)
    blocks = total.shape[0] - 1
    ratio = total[blocks, :, :1] / total[blocks, :, TILE // 2 : TILE // 2 + 1]
    quotient[...] = jnp.broadcast_to(ratio, quotient.shape)
    step = NEAR_SECOND // NEAR_FIRST
    near = lax.div(firm[0], NEAR_FIRST) & (step - 1)
    for block in range(blocks):
        seconds[block] = firsts[block * step + near] - total[block] / quotient[...]
    first[...] = firsts[lax.div(firm[0], NEAR_FIRST)]
    second[...] = seconds[lax.div(firm[0], NEAR_SECOND)]
    send(sent, seconds[...])


def third_body(got, first, second, sent):
    total = sum_of(got)
    probes = first.shape[0]
    for other in range(sent.shape[0]):
        sent[other, 0] = total[:probes]
        sent[other, 1] = total[probes:]
        sent[other, 2] = first[...]
        sent[other, 3] = second[...]


def kernel(body, shapes, places, scratch, name, cost=1 << 16):
    return pl.pallas_call(
        body,
        out_shape=shapes,
        in_specs=[pl.BlockSpec(memory_space=place) for place in places],
        out_specs=jax.tree.map(lambda _: pl.BlockSpec(memory_space=pltpu.VMEM), shapes),
        scratch_shapes=scratch,
        compiler_params=pltpu.CompilerParams(vmem_limit_bytes=6 << 20),
        cost_estimate=pl.CostEstimate(flops=cost, transcendentals=0, bytes_accessed=1 << 20),
        name=name,
    )


def exchange(chunks, axis, beside=()):
    chunks, beside = lax.optimization_barrier((chunks, beside))
    got = lax.all_to_all(chunks, axis, 0, 0, tiled=True)
    return lax.optimization_barrier((got, beside))


def local(tiles, tile_rows, tile_firms, worker_ids, sign_words, regular):
    probe_dev = sign_words.shape[0]
    probes = lax.axis_size("probe")
    count = tiles.shape[0]
    blocks = WORKERS * FIRMS
    reg_blocks = regular.reshape(WORKERS, TILE)
    words = jnp.transpose(sign_words, (2, 1, 0))
    at = tuple(lax.axis_index(axis).reshape(1) for axis in (FIRM_AXES, "worker", "probe"))

    VMEM, SMEM, HBM = pltpu.VMEM, pltpu.SMEM, pltpu.HBM
    rows_vmem = VMEM((ROWB_DEV, probe_dev, TILE), f32)
    sums_vmem = VMEM((blocks, probe_dev, TILE), f32)
    cost = 2 * count * probe_dev * TILE * TILE

    def shape(*dims, dtype=f32):
        return jax.ShapeDtypeStruct((*dims, probe_dev, TILE), dtype)

    def placed(array, where):
        return pltpu.with_memory_space_constraint(array, where)

    near_first, far_first = (*FIRM_AXES[2:], "worker"), FIRM_AXES[:2]
    near_second, far_second = (*FIRM_AXES[1:], "worker"), FIRM_AXES[:1]
    peers_first, held_first = NEAR_FIRST * WORKERS, FIRMS // NEAR_FIRST
    peers_second, held_second = NEAR_SECOND * WORKERS, FIRMS // NEAR_SECOND

    parts, tiles = kernel(
        start_body, (shape(blocks), VMEM(tiles.shape, bf16)), [HBM] * 5,
        [
            rows_vmem, pltpu.SemaphoreType.DMA((CHUNKS + 4,)), SMEM(tile_rows.shape, jnp.int32),
            SMEM(tile_firms.shape, jnp.int32), SMEM(words.shape, jnp.int32), VMEM(worker_ids.shape, jnp.int32),
        ],
        "start", cost,
    )(*(placed(array, HBM) for array in (tile_rows, tile_firms, words, worker_ids, tiles)))
    got, at = exchange(parts.reshape(peers_first, held_first, probe_dev, TILE), near_first, at)
    sent = kernel(gather_fold_body, shape(held_first, held_first), [VMEM], [], "fold")(got)
    got, at = exchange(sent, far_first, at)
    firsts, sent = kernel(
        first_body, (shape(held_first), shape(peers_first, held_first, dtype=bf16)), [VMEM], [], "first"
    )(got)

    field, (firsts, *at) = exchange(sent, near_first, (firsts, *at))
    firm, worker, _ = at
    parts = kernel(
        middle_body, shape(peers_second, held_second + 1),
        [SMEM, SMEM, SMEM, SMEM, VMEM, VMEM, VMEM, VMEM, VMEM], [rows_vmem, sums_vmem], "middle", 2 * cost,
    )(
        tile_rows, tile_firms, worker, firm, field.reshape(blocks, probe_dev, TILE), firsts, reg_blocks,
        worker_ids, placed(tiles, VMEM),
    )
    got, (firsts, *at) = exchange(parts, near_second, (firsts, *at))
    sent = kernel(gather_fold_body, shape(held_second, held_second + 1, dtype=bf16), [VMEM], [], "fold")(got)
    got, (firsts, *at) = exchange(sent, far_second, (firsts, *at))
    first, second, quotient, sent = kernel(
        second_body, (shape(), shape(), shape(), shape(peers_second, held_second, dtype=bf16)),
        [SMEM, VMEM, VMEM], [VMEM((held_second, probe_dev, TILE), f32)], "second",
    )(at[0], got, firsts)

    field, (first, second, quotient, *at) = exchange(sent, near_second, (first, second, quotient, *at))
    sent = kernel(
        rows_body, shape(probes, 3 + ROWB_DEV), [SMEM, SMEM, VMEM, VMEM, VMEM, VMEM, VMEM, VMEM], [], "rows", cost
    )(
        tile_rows, tile_firms, field.reshape(blocks, probe_dev, TILE), first, second, quotient, worker_ids,
        placed(tiles, VMEM),
    )
    given, (first, second, *at) = exchange(sent, "probe", (first, second, *at))
    firm, worker, probe = at
    parts = kernel(
        last_body, shape(WORKERS, FIRMS + 3, dtype=bf16),
        [SMEM, SMEM, SMEM, SMEM, SMEM, VMEM, VMEM, VMEM],
        [VMEM((ROWB_DEV, 2 * probe_dev, TILE), f32), sums_vmem], "last", cost,
    )(tile_rows, tile_firms, worker, firm, probe, given, reg_blocks, placed(tiles, VMEM))
    got, (first, second, given, *at) = exchange(parts, "worker", (first, second, given, *at))
    sent = kernel(
        fold_body, jax.ShapeDtypeStruct((FIRMS, 2 * probe_dev, TILE), f32), [VMEM], [], "fold_last"
    )(got)
    got, (first, second, given, *at) = exchange(sent, FIRM_AXES, (first, second, given, *at))
    sent = kernel(third_body, shape(WORKERS * probes, 4), [VMEM, VMEM, VMEM], [], "third")(got, first, second)
    last, (given, *at) = exchange(sent, ("worker", "probe"), (given, *at))
    out = jax.ShapeDtypeStruct((probe_dev, WORKERS * TILE), f32)
    total = probes * probe_dev
    return kernel(
        final_body, (out, out), [SMEM, VMEM, VMEM],
        [VMEM((3 * total, WORKERS * TILE), f32), VMEM((2, total, 4 * total), f32)], "final", cost // 4,
    )(at[2], given, last)


def solution(mesh):
    sizes = (FIRMS // NEAR_SECOND, NEAR_SECOND // NEAR_FIRST, NEAR_FIRST)
    split = jax.sharding.Mesh(
        mesh.devices.reshape(*sizes, WORKERS, mesh.shape["probe"]), (*FIRM_AXES, "worker", "probe")
    )
    shard = (*FIRM_AXES, "worker")
    placed = (
        P(shard, None, None),
        P(shard, None),
        P(shard, None),
        P(shard, None),
        P("probe", shard, None),
        P(FIRM_AXES),
    )
    return jax.shard_map(
        local,
        mesh=split,
        in_specs=placed,
        out_specs=(P("probe", FIRM_AXES), P("probe", FIRM_AXES)),
        check_vma=False,
    )
```

```python
import jax
import jax.numpy as jnp
from jax import lax
from jax.experimental import pallas as pl
from jax.experimental.pallas import tpu as pltpu
from jax.sharding import PartitionSpec as P

TILE = 128
ROWB_DEV = 4
ROWS_DEV = 512
SHARD_WORKERS = 128
BITS = 30
CHUNKS = 4
PANEL = 16
WORKERS = 8
FIRMS = 16
NEAR_FIRST = 2
NEAR_SECOND = 2
FIRM_AXES = ("firm_far", "firm_middle", "firm_near")

largest_value = lax.Precision.HIGHEST
f32 = jnp.float32
bf16 = jnp.bfloat16


def dot(left, right, dims, precision=None):
    return lax.dot_general(
        left, right, ((dims[:1], dims[1:]), ((), ())), precision=precision, preferred_element_type=f32
    )


def exact(left, right, dims):
    return dot(left, right, dims, largest_value)


def three_parts(values):
    high = values.astype(bf16)
    rest = values - high.astype(f32)
    middle = rest.astype(bf16)
    low = (rest - middle.astype(f32)).astype(bf16)
    return high, middle, low


def demean(values, worker_ids):
    probes = values.shape[0]
    workers = lax.broadcasted_iota(jnp.int32, (SHARD_WORKERS, ROWS_DEV), 0)
    onehot = jnp.where(workers == worker_ids, 1.0, 0.0).astype(bf16)
    stacked = jnp.concatenate([*(part.astype(f32) for part in three_parts(values)), jnp.ones_like(values)], axis=0)
    sums = dot(stacked.astype(bf16), onehot, (1, 1))
    totals = (sums[2 * probes : 3 * probes] + sums[probes : 2 * probes]) + sums[:probes]
    means = totals / sums[3 * probes :]
    stacked = jnp.concatenate([part.astype(f32) for part in three_parts(means)], axis=0)
    spread = dot(stacked.astype(bf16), onehot, (1, 0))
    return values - ((spread[2 * probes : 3 * probes] + spread[probes : 2 * probes]) + spread[:probes])


def fetch(tiles_hbm, tiles, arrived, small):
    size = tiles.shape[0] // CHUNKS

    def copy(chunk):
        part = pl.ds(chunk * size, size)
        return pltpu.make_async_copy(tiles_hbm.at[part], tiles.at[part], arrived.at[chunk])

    tables = fetch_small(arrived, small)
    for chunk in range(CHUNKS):
        copy(chunk).start()
    for table in tables:
        table.wait()
    return lambda chunk: copy(chunk).wait()


def fetch_small(arrived, small):
    tables = [pltpu.make_async_copy(*both, arrived.at[CHUNKS + item]) for item, both in enumerate(small)]
    for table in tables:
        table.start()
    return tables


def place_of(block, near):
    firm, worker = block >> (WORKERS.bit_length() - 1), block & (WORKERS - 1)
    shift = near.bit_length() - 1
    return ((firm & (near - 1)) * WORKERS + worker) * (FIRMS // near) + (firm >> shift)


def stack(pieces):
    return jnp.concatenate([piece.astype(f32) for piece in pieces], axis=0).astype(bf16)


def forward(tile_rows, tile_firms, field, tiles, near):
    total = None
    for tile in range(0, tiles.shape[0], 2):
        pieces = [field[place_of(tile_firms[0, tile + item], near)] for item in range(2)]
        probes = pieces[0].shape[0]
        weights = jnp.concatenate([tiles[tile], tiles[tile + 1]], axis=0)
        both = dot(stack(pieces), weights, (1, 1))
        if total is None:
            total = [jnp.zeros((probes, TILE), f32) for block in range(ROWB_DEV)]
        for item in range(2):
            image = both[item * probes : (item + 1) * probes, item * TILE : (item + 1) * TILE]
            row = tile_rows[0, tile + item]
            total = [old + jnp.where(row == block, image, 0.0) for block, old in enumerate(total)]
    return total


def adjoint(tile_rows, tile_firms, rows, tiles, out, near, wait=None):
    out[...] = jnp.zeros_like(out)
    probes, lines = out.shape[1], rows.shape[1]
    size = tiles.shape[0] // CHUNKS
    for tile in range(0, tiles.shape[0], 2):
        if wait is not None and tile % size == 0:
            wait(tile // size)
        weights = jnp.concatenate([tiles[tile], tiles[tile + 1]], axis=1)
        both = dot(stack([rows[tile_rows[0, tile + item]] for item in range(2)]), weights, (1, 0))
        for item in range(2):
            place = place_of(tile_firms[0, tile + item], near)
            image = out[place]
            for begin in range(item * lines, (item + 1) * lines, probes):
                image = image + both[begin : begin + probes, item * TILE : (item + 1) * TILE]
            out[place] = image


def put_rows(rows, values):
    for block in range(ROWB_DEV):
        rows[block] = values[:, block * TILE : (block + 1) * TILE].astype(bf16).astype(f32)


def put_two_terms(rows, values):
    high = values.astype(bf16).astype(f32)
    rows[...] = jnp.concatenate([high, (values - high).astype(bf16).astype(f32)], axis=0)


def put_parts(out, total, extras):
    peers, blocks = out.shape[0], out.shape[1] - len(extras)
    for peer in range(peers):
        for block in range(blocks):
            out[peer, block] = total[peer * blocks + block].astype(out.dtype)
        for item, extra in enumerate(extras):
            out[peer, blocks + item] = extra.astype(out.dtype)


def add_ridge(out, firm, worker, near, regular, own):
    place = place_of(firm * WORKERS + worker, near)
    out[place] = out[place] + regular[pl.ds(worker, 1), :] * own


def start_body(
    rows_hbm, firms_hbm, words_hbm, ids_hbm, tiles_hbm,
    out, tiles, rows, arrived, tile_rows, tile_firms, words, worker_ids,
):
    small = [(rows_hbm, tile_rows), (firms_hbm, tile_firms), (words_hbm, words), (ids_hbm, worker_ids)]
    wait = fetch(tiles_hbm, tiles, arrived, small)
    words_row, blocks, probes = words.shape
    lanes = lax.broadcasted_iota(jnp.int32, (probes, TILE), 1)
    lines = lax.broadcasted_iota(jnp.int32, (probes, TILE), 0)
    word_of = lax.div(lanes, jnp.int32(BITS))
    bit = lanes - word_of * BITS
    chosen = [jnp.zeros((probes, TILE), jnp.int32) for block in range(blocks)]
    for word in range(words_row):
        for probe in range(probes):
            here = (word_of == word) & (lines == probe)
            chosen = [jnp.where(here, words[word, block, probe], old) for block, old in enumerate(chosen)]
    signs = [(2 * (lax.shift_right_logical(old, bit) & 1) - 1).astype(f32) for old in chosen]
    put_rows(rows, demean(jnp.concatenate(signs, axis=1), worker_ids[...]))
    adjoint(tile_rows, tile_firms, rows, tiles, out, NEAR_FIRST, wait)


def middle_body(
    tile_rows, tile_firms, worker, firm, field, firsts, regular, worker_ids, tiles,
    out, rows, feature_sums,
):
    total = forward(tile_rows, tile_firms, field, tiles, NEAR_FIRST)
    values = demean(jnp.concatenate(total, axis=1), worker_ids[...])
    put_rows(rows, values)
    adjoint(tile_rows, tile_firms, rows, tiles, feature_sums, NEAR_SECOND)
    own = firsts[lax.div(firm[0], NEAR_FIRST)]
    add_ridge(feature_sums, firm[0], worker[0], NEAR_SECOND, regular, own)
    squares = own * own
    above = jnp.sum(values * values, axis=1, keepdims=True)
    above = above + jnp.sum(squares * regular[pl.ds(worker[0], 1), :], axis=1, keepdims=True)
    below = jnp.sum(squares, axis=1, keepdims=True)
    lanes = lax.broadcasted_iota(jnp.int32, own.shape, 1)
    put_parts(out, feature_sums, [jnp.where(lanes < TILE // 2, above, below)])


def rows_body(tile_rows, tile_firms, field, first, second, quotient, worker_ids, tiles, out):
    total = forward(tile_rows, tile_firms, field, tiles, NEAR_SECOND)
    values = demean(jnp.concatenate(total, axis=1), worker_ids[...])
    for probe in range(out.shape[0]):
        out[probe, 0] = first[...]
        out[probe, 1] = second[...]
        out[probe, 2] = quotient[...]
        for block in range(ROWB_DEV):
            out[probe, 3 + block] = values[:, block * TILE : (block + 1) * TILE]


def last_body(
    tile_rows, tile_firms, worker, firm, probe, given, regular, tiles,
    out, rows, feature_sums,
):
    gather = lambda item: jnp.concatenate([given[other, item] for other in range(given.shape[0])], axis=0)
    own = lambda item: given[probe[0], item]
    first, second = own(0), own(1)
    first_all, second_all = gather(0), gather(1)
    mine = [own(3 + block) for block in range(ROWB_DEV)]
    for block in range(ROWB_DEV):
        put_two_terms(rows.at[block], mine[block])
    left = jnp.concatenate([*mine, second * regular[pl.ds(worker[0], 1), :]], axis=1)
    right = jnp.concatenate([*(gather(3 + block) for block in range(ROWB_DEV)), second_all], axis=1)
    extra = jnp.concatenate(
        [
            exact(first, first_all, (1, 1)),
            exact(first, second_all, (1, 1)),
            exact(second, second_all, (1, 1)),
            exact(left, right, (1, 1)),
        ],
        axis=1,
    )
    adjoint(tile_rows, tile_firms, rows, tiles, feature_sums, NEAR_FIRST)
    add_ridge(feature_sums, firm[0], worker[0], NEAR_FIRST, regular, second)
    put_parts(out, feature_sums, [extra])


def eliminate(table, pivots):
    size, width = table.shape
    lanes = lax.broadcasted_iota(jnp.int32, (size, width), 1)
    lines = lax.broadcasted_iota(jnp.int32, (size, width), 0)

    def spread(at):
        column = jnp.broadcast_to(table[:, pivots[0] + at : pivots[0] + at + 1], (size, width))
        for begin in pivots[1:]:
            other = jnp.broadcast_to(table[:, begin + at : begin + at + 1], (size, width))
            column = jnp.where(lanes < begin, column, other)
        return column

    for start in range(0, size, PANEL):
        columns = [spread(start + item) for item in range(PANEL)]
        for item, column in enumerate(columns):
            at = start + item
            inverse = 1.0 / column[at : at + 1, :]
            line = table[at : at + 1, :] * inverse
            table = jnp.where(lines == at, line, table - column * line)
            for later in range(item + 1, PANEL):
                factor = columns[later][at : at + 1, :] * inverse
                columns[later] = jnp.where(lines == at, factor, columns[later] - column * factor)
    return table


def final_body(probe, given, last, solution_out, residual_out, basis, mixes):
    size = given.shape[0] * given.shape[2]
    gather = lambda ref, item: jnp.concatenate([ref[other, item] for other in range(given.shape[0])], axis=0)
    half = lambda matrix: 0.5 * (matrix + matrix.T)
    lines = lax.broadcasted_iota(jnp.int32, (size, size), 0)
    lanes = lax.broadcasted_iota(jnp.int32, (size, size), 1)
    unit = jnp.where(lines == lanes, 1.0, 0.0)
    tables = gather(last, 1)
    current = half(tables[:, :size])
    mixed = tables[:, size : 2 * size]
    other = tables[:, 2 * size : 3 * size]
    other_mapped = tables[:, 3 * size :]
    scale = gather(given, 2)[:, :size]
    same_mapped = half(scale * (current - mixed).T)
    mixed_mapped = scale * (mixed - other)

    def whole(one, cross, two):
        return jnp.concatenate(
            [jnp.concatenate([one, cross], axis=1), jnp.concatenate([cross.T, two], axis=1)], axis=0
        )

    grams = whole(current, mixed, other)
    mapped_grams = whole(same_mapped, mixed_mapped, other_mapped)
    solved = eliminate(jnp.concatenate([same_mapped, current, current, unit], axis=1), (0, 2 * size))
    step_first = solved[:, size : 2 * size]
    inverse = solved[:, 3 * size :]
    onto_second = scale * step_first
    onto_first = unit - onto_second
    mix = jnp.concatenate([onto_first, onto_second], axis=0)
    following = half(exact(mix, exact(grams, mix, (1, 0)), (0, 0)))
    direction = onto_first + exact(inverse, following, (1, 0))
    mix = jnp.concatenate([direction, onto_second], axis=0)
    curvature = half(exact(mix, exact(mapped_grams, mix, (1, 0)), (0, 0)))
    step_second = eliminate(jnp.concatenate([curvature, following], axis=1), (0,))[:, size:]
    moved = exact(mix, step_second, (1, 0))
    moved_first, moved_second = moved[:size], moved[size:]
    image = scale * moved_first
    probes = given.shape[2]
    for other in range(last.shape[0]):
        worker, part = other // given.shape[0], other % given.shape[0]
        for item, kind in enumerate((2, 3, 0)):
            line = item * size + part * probes
            basis[line : line + probes, worker * TILE : (worker + 1) * TILE] = last[other, kind]
    empty = jnp.zeros((size, size), f32)
    mixes[0] = jnp.concatenate([step_first + moved_first, moved_second, empty, empty], axis=0).T
    mixes[1] = jnp.concatenate([onto_first - image, onto_second + image, -moved_second, empty], axis=0).T
    begin = pl.multiple_of(probe[0] * probes, probes)
    both = jnp.concatenate([mixes[item, pl.ds(begin, probes), :][:, : 3 * size] for item in range(2)], axis=0)
    outs = exact(both, basis[...], (1, 0))
    solution_out[...] = outs[:probes]
    residual_out[...] = outs[probes:]


def fold_body(got, out):
    total = sum_of(got)
    firms, probes = out.shape[0], total.shape[1]
    for firm in range(firms):
        out[firm, :probes, :] = total[firm]
    if out.shape[1] > probes:
        extra = total[firms]
        for item in range(firms + 1, total.shape[0]):
            extra = extra + total[item]
        for firm in range(firms):
            out[firm, probes:, :] = extra


def sum_of(got):
    total = got[0].astype(f32)
    for other in range(1, got.shape[0]):
        total = total + got[other].astype(f32)
    return total


def send(out, values):
    for other in range(out.shape[0]):
        out[other] = values.astype(out.dtype)


def gather_fold_body(got, out):
    send(out, sum_of(got))


def first_body(got, firsts, sent):
    firsts[...] = sum_of(got)
    send(sent, firsts[...])


def second_body(firm, got, firsts, first, second, quotient, sent, seconds):
    total = sum_of(got)
    blocks = total.shape[0] - 1
    ratio = total[blocks, :, :1] / total[blocks, :, TILE // 2 : TILE // 2 + 1]
    quotient[...] = jnp.broadcast_to(ratio, quotient.shape)
    step = NEAR_SECOND // NEAR_FIRST
    near = lax.div(firm[0], NEAR_FIRST) & (step - 1)
    for block in range(blocks):
        seconds[block] = firsts[block * step + near] - total[block] / quotient[...]
    first[...] = firsts[lax.div(firm[0], NEAR_FIRST)]
    second[...] = seconds[lax.div(firm[0], NEAR_SECOND)]
    send(sent, seconds[...])


def third_body(got, first, second, sent):
    total = sum_of(got)
    probes = first.shape[0]
    for other in range(sent.shape[0]):
        sent[other, 0] = total[:probes]
        sent[other, 1] = total[probes:]
        sent[other, 2] = first[...]
        sent[other, 3] = second[...]


def kernel(body, shapes, places, scratch, name, cost=1 << 16):
    return pl.pallas_call(
        body,
        out_shape=shapes,
        in_specs=[pl.BlockSpec(memory_space=place) for place in places],
        out_specs=jax.tree.map(lambda _: pl.BlockSpec(memory_space=pltpu.VMEM), shapes),
        scratch_shapes=scratch,
        compiler_params=pltpu.CompilerParams(vmem_limit_bytes=6 << 20),
        cost_estimate=pl.CostEstimate(flops=cost, transcendentals=0, bytes_accessed=1 << 20),
        name=name,
    )


def exchange(chunks, axis, beside=()):
    chunks, beside = lax.optimization_barrier((chunks, beside))
    got = lax.all_to_all(chunks, axis, 0, 0, tiled=True)
    return lax.optimization_barrier((got, beside))


def local(tiles, tile_rows, tile_firms, worker_ids, sign_words, regular):
    probe_dev = sign_words.shape[0]
    probes = lax.axis_size("probe")
    count = tiles.shape[0]
    blocks = WORKERS * FIRMS
    reg_blocks = regular.reshape(WORKERS, TILE)
    words = jnp.transpose(sign_words, (2, 1, 0))
    at = tuple(lax.axis_index(axis).reshape(1) for axis in (FIRM_AXES, "worker", "probe"))

    VMEM, SMEM, HBM = pltpu.VMEM, pltpu.SMEM, pltpu.HBM
    rows_vmem = VMEM((ROWB_DEV, probe_dev, TILE), f32)
    sums_vmem = VMEM((blocks, probe_dev, TILE), f32)
    cost = 2 * count * probe_dev * TILE * TILE

    def shape(*dims, dtype=f32):
        return jax.ShapeDtypeStruct((*dims, probe_dev, TILE), dtype)

    def placed(array, where):
        return pltpu.with_memory_space_constraint(array, where)

    near_first, far_first = (*FIRM_AXES[2:], "worker"), FIRM_AXES[:2]
    near_second, far_second = (*FIRM_AXES[1:], "worker"), FIRM_AXES[:1]
    peers_first, held_first = NEAR_FIRST * WORKERS, FIRMS // NEAR_FIRST
    peers_second, held_second = NEAR_SECOND * WORKERS, FIRMS // NEAR_SECOND

    parts, tiles = kernel(
        start_body, (shape(blocks), VMEM(tiles.shape, bf16)), [HBM] * 5,
        [
            rows_vmem, pltpu.SemaphoreType.DMA((CHUNKS + 4,)), SMEM(tile_rows.shape, jnp.int32),
            SMEM(tile_firms.shape, jnp.int32), SMEM(words.shape, jnp.int32), VMEM(worker_ids.shape, jnp.int32),
        ],
        "start", cost,
    )(*(placed(array, HBM) for array in (tile_rows, tile_firms, words, worker_ids, tiles)))
    got, at = exchange(parts.reshape(peers_first, held_first, probe_dev, TILE), near_first, at)
    sent = kernel(gather_fold_body, shape(held_first, held_first), [VMEM], [], "fold")(got)
    got, at = exchange(sent, far_first, at)
    firsts, sent = kernel(
        first_body, (shape(held_first), shape(peers_first, held_first, dtype=bf16)), [VMEM], [], "first"
    )(got)

    field, (firsts, *at) = exchange(sent, near_first, (firsts, *at))
    firm, worker, _ = at
    parts = kernel(
        middle_body, shape(peers_second, held_second + 1),
        [SMEM, SMEM, SMEM, SMEM, VMEM, VMEM, VMEM, VMEM, VMEM], [rows_vmem, sums_vmem], "middle", 2 * cost,
    )(
        tile_rows, tile_firms, worker, firm, field.reshape(blocks, probe_dev, TILE), firsts, reg_blocks,
        worker_ids, placed(tiles, VMEM),
    )
    got, (firsts, *at) = exchange(parts, near_second, (firsts, *at))
    sent = kernel(gather_fold_body, shape(held_second, held_second + 1, dtype=bf16), [VMEM], [], "fold")(got)
    got, (firsts, *at) = exchange(sent, far_second, (firsts, *at))
    first, second, quotient, sent = kernel(
        second_body, (shape(), shape(), shape(), shape(peers_second, held_second, dtype=bf16)),
        [SMEM, VMEM, VMEM], [VMEM((held_second, probe_dev, TILE), f32)], "second",
    )(at[0], got, firsts)

    field, (first, second, quotient, *at) = exchange(sent, near_second, (first, second, quotient, *at))
    sent = kernel(
        rows_body, shape(probes, 3 + ROWB_DEV), [SMEM, SMEM, VMEM, VMEM, VMEM, VMEM, VMEM, VMEM], [], "rows", cost
    )(
        tile_rows, tile_firms, field.reshape(blocks, probe_dev, TILE), first, second, quotient, worker_ids,
        placed(tiles, VMEM),
    )
    given, (first, second, *at) = exchange(sent, "probe", (first, second, *at))
    firm, worker, probe = at
    parts = kernel(
        last_body, shape(peers_first, held_first + 1),
        [SMEM, SMEM, SMEM, SMEM, SMEM, VMEM, VMEM, VMEM],
        [VMEM((ROWB_DEV, 2 * probe_dev, TILE), f32), sums_vmem], "last", cost,
    )(tile_rows, tile_firms, worker, firm, probe, given, reg_blocks, placed(tiles, VMEM))
    got, (first, second, given, *at) = exchange(parts, near_first, (first, second, given, *at))
    sent = kernel(
        fold_body, jax.ShapeDtypeStruct((held_first, 2 * probe_dev, TILE), f32), [VMEM], [], "fold_last"
    )(got)
    got, (first, second, given, *at) = exchange(sent, far_first, (first, second, given, *at))
    sent = kernel(third_body, shape(WORKERS * probes, 4), [VMEM, VMEM, VMEM], [], "third")(got, first, second)
    last, (given, *at) = exchange(sent, ("worker", "probe"), (given, *at))
    out = jax.ShapeDtypeStruct((probe_dev, WORKERS * TILE), f32)
    total = probes * probe_dev
    return kernel(
        final_body, (out, out), [SMEM, VMEM, VMEM],
        [VMEM((3 * total, WORKERS * TILE), f32), VMEM((2, total, 4 * total), f32)], "final", cost // 4,
    )(at[2], given, last)


def solution(mesh):
    sizes = (FIRMS // NEAR_SECOND, NEAR_SECOND // NEAR_FIRST, NEAR_FIRST)
    split = jax.sharding.Mesh(
        mesh.devices.reshape(*sizes, WORKERS, mesh.shape["probe"]), (*FIRM_AXES, "worker", "probe")
    )
    shard = (*FIRM_AXES, "worker")
    placed = (
        P(shard, None, None),
        P(shard, None),
        P(shard, None),
        P(shard, None),
        P("probe", shard, None),
        P(FIRM_AXES),
    )
    return jax.shard_map(
        local,
        mesh=split,
        in_specs=placed,
        out_specs=(P("probe", FIRM_AXES), P("probe", FIRM_AXES)),
        check_vma=False,
    )
```

```python
import jax
import jax.numpy as jnp
from jax import lax
from jax.experimental import pallas as pl
from jax.experimental.pallas import tpu as pltpu
from jax.sharding import PartitionSpec as P

TILE = 128
ROWB_DEV = 4
ROWS_DEV = 512
SHARD_WORKERS = 128
BITS = 30
CHUNKS = 4
PANEL = 16
WORKERS = 8
FIRMS = 16
NEAR_FIRST = 2
NEAR_SECOND = 2
FIRM_AXES = ("firm_far", "firm_middle", "firm_near")

largest_value = lax.Precision.HIGHEST
f32 = jnp.float32
bf16 = jnp.bfloat16


def dot(left, right, dims, precision=None):
    return lax.dot_general(
        left, right, ((dims[:1], dims[1:]), ((), ())), precision=precision, preferred_element_type=f32
    )


def exact(left, right, dims):
    return dot(left, right, dims, largest_value)


def three_parts(values):
    high = values.astype(bf16)
    rest = values - high.astype(f32)
    middle = rest.astype(bf16)
    low = (rest - middle.astype(f32)).astype(bf16)
    return high, middle, low


def demean(values, worker_ids):
    probes = values.shape[0]
    workers = lax.broadcasted_iota(jnp.int32, (SHARD_WORKERS, ROWS_DEV), 0)
    onehot = jnp.where(workers == worker_ids, 1.0, 0.0).astype(bf16)
    stacked = jnp.concatenate([*(part.astype(f32) for part in three_parts(values)), jnp.ones_like(values)], axis=0)
    sums = dot(stacked.astype(bf16), onehot, (1, 1))
    totals = (sums[2 * probes : 3 * probes] + sums[probes : 2 * probes]) + sums[:probes]
    means = totals / sums[3 * probes :]
    stacked = jnp.concatenate([part.astype(f32) for part in three_parts(means)], axis=0)
    spread = dot(stacked.astype(bf16), onehot, (1, 0))
    return values - ((spread[2 * probes : 3 * probes] + spread[probes : 2 * probes]) + spread[:probes])


def fetch(tiles_hbm, tiles, arrived, small):
    size = tiles.shape[0] // CHUNKS

    def copy(chunk):
        part = pl.ds(chunk * size, size)
        return pltpu.make_async_copy(tiles_hbm.at[part], tiles.at[part], arrived.at[chunk])

    tables = fetch_small(arrived, small)
    for chunk in range(CHUNKS):
        copy(chunk).start()
    for table in tables:
        table.wait()
    return lambda chunk: copy(chunk).wait()


def fetch_small(arrived, small):
    tables = [pltpu.make_async_copy(*both, arrived.at[CHUNKS + item]) for item, both in enumerate(small)]
    for table in tables:
        table.start()
    return tables


def place_of(block, near):
    firm, worker = block >> (WORKERS.bit_length() - 1), block & (WORKERS - 1)
    shift = near.bit_length() - 1
    return ((firm & (near - 1)) * WORKERS + worker) * (FIRMS // near) + (firm >> shift)


def stack(pieces):
    return jnp.concatenate([piece.astype(f32) for piece in pieces], axis=0).astype(bf16)


def forward(tile_rows, tile_firms, field, tiles, near):
    total = None
    for tile in range(0, tiles.shape[0], 2):
        pieces = [field[place_of(tile_firms[0, tile + item], near)] for item in range(2)]
        probes = pieces[0].shape[0]
        weights = jnp.concatenate([tiles[tile], tiles[tile + 1]], axis=0)
        both = dot(stack(pieces), weights, (1, 1))
        if total is None:
            total = [jnp.zeros((probes, TILE), f32) for block in range(ROWB_DEV)]
        for item in range(2):
            image = both[item * probes : (item + 1) * probes, item * TILE : (item + 1) * TILE]
            row = tile_rows[0, tile + item]
            total = [old + jnp.where(row == block, image, 0.0) for block, old in enumerate(total)]
    return total


def adjoint(tile_rows, tile_firms, rows, tiles, out, near, wait=None):
    out[...] = jnp.zeros_like(out)
    probes, lines = out.shape[1], rows.shape[1]
    size = tiles.shape[0] // CHUNKS
    for tile in range(0, tiles.shape[0], 2):
        if wait is not None and tile % size == 0:
            wait(tile // size)
        weights = jnp.concatenate([tiles[tile], tiles[tile + 1]], axis=1)
        both = dot(stack([rows[tile_rows[0, tile + item]] for item in range(2)]), weights, (1, 0))
        for item in range(2):
            place = place_of(tile_firms[0, tile + item], near)
            image = out[place]
            for begin in range(item * lines, (item + 1) * lines, probes):
                image = image + both[begin : begin + probes, item * TILE : (item + 1) * TILE]
            out[place] = image


def put_rows(rows, values):
    for block in range(ROWB_DEV):
        rows[block] = values[:, block * TILE : (block + 1) * TILE].astype(bf16).astype(f32)


def put_two_terms(rows, values):
    high = values.astype(bf16).astype(f32)
    rows[...] = jnp.concatenate([high, (values - high).astype(bf16).astype(f32)], axis=0)


def put_parts(out, total, extras):
    peers, blocks = out.shape[0], out.shape[1] - len(extras)
    for peer in range(peers):
        for block in range(blocks):
            out[peer, block] = total[peer * blocks + block].astype(out.dtype)
        for item, extra in enumerate(extras):
            out[peer, blocks + item] = extra.astype(out.dtype)


def add_ridge(out, firm, worker, near, regular, own):
    place = place_of(firm * WORKERS + worker, near)
    out[place] = out[place] + regular[pl.ds(worker, 1), :] * own


def start_body(
    rows_hbm, firms_hbm, words_hbm, ids_hbm, tiles_hbm,
    out, tiles, rows, arrived, tile_rows, tile_firms, words, worker_ids,
):
    small = [(rows_hbm, tile_rows), (firms_hbm, tile_firms), (words_hbm, words), (ids_hbm, worker_ids)]
    wait = fetch(tiles_hbm, tiles, arrived, small)
    words_row, blocks, probes = words.shape
    lanes = lax.broadcasted_iota(jnp.int32, (probes, TILE), 1)
    lines = lax.broadcasted_iota(jnp.int32, (probes, TILE), 0)
    word_of = lax.div(lanes, jnp.int32(BITS))
    bit = lanes - word_of * BITS
    chosen = [jnp.zeros((probes, TILE), jnp.int32) for block in range(blocks)]
    for word in range(words_row):
        for probe in range(probes):
            here = (word_of == word) & (lines == probe)
            chosen = [jnp.where(here, words[word, block, probe], old) for block, old in enumerate(chosen)]
    signs = [(2 * (lax.shift_right_logical(old, bit) & 1) - 1).astype(f32) for old in chosen]
    put_rows(rows, demean(jnp.concatenate(signs, axis=1), worker_ids[...]))
    adjoint(tile_rows, tile_firms, rows, tiles, out, NEAR_FIRST, wait)


def middle_body(
    tile_rows, tile_firms, worker, firm, field, firsts, regular, worker_ids, tiles,
    out, rows, feature_sums,
):
    total = forward(tile_rows, tile_firms, field, tiles, NEAR_FIRST)
    values = demean(jnp.concatenate(total, axis=1), worker_ids[...])
    put_rows(rows, values)
    adjoint(tile_rows, tile_firms, rows, tiles, feature_sums, NEAR_SECOND)
    own = firsts[lax.div(firm[0], NEAR_FIRST)]
    add_ridge(feature_sums, firm[0], worker[0], NEAR_SECOND, regular, own)
    squares = own * own
    above = jnp.sum(values * values, axis=1, keepdims=True)
    above = above + jnp.sum(squares * regular[pl.ds(worker[0], 1), :], axis=1, keepdims=True)
    below = jnp.sum(squares, axis=1, keepdims=True)
    lanes = lax.broadcasted_iota(jnp.int32, own.shape, 1)
    put_parts(out, feature_sums, [jnp.where(lanes < TILE // 2, above, below)])


def rows_body(tile_rows, tile_firms, field, first, second, quotient, worker_ids, tiles, out):
    total = forward(tile_rows, tile_firms, field, tiles, NEAR_SECOND)
    values = demean(jnp.concatenate(total, axis=1), worker_ids[...])
    for probe in range(out.shape[0]):
        out[probe, 0] = first[...]
        out[probe, 1] = second[...]
        out[probe, 2] = quotient[...]
        for block in range(ROWB_DEV):
            out[probe, 3 + block] = values[:, block * TILE : (block + 1) * TILE]


def last_body(
    tile_rows, tile_firms, worker, firm, probe, given, regular, tiles,
    out, rows, feature_sums,
):
    gather = lambda item: jnp.concatenate([given[other, item] for other in range(given.shape[0])], axis=0)
    own = lambda item: given[probe[0], item]
    first, second = own(0), own(1)
    first_all, second_all = gather(0), gather(1)
    mine = [own(3 + block) for block in range(ROWB_DEV)]
    for block in range(ROWB_DEV):
        put_two_terms(rows.at[block], mine[block])
    left = jnp.concatenate([*mine, second * regular[pl.ds(worker[0], 1), :]], axis=1)
    right = jnp.concatenate([*(gather(3 + block) for block in range(ROWB_DEV)), second_all], axis=1)
    extra = jnp.concatenate(
        [
            exact(first, first_all, (1, 1)),
            exact(first, second_all, (1, 1)),
            exact(second, second_all, (1, 1)),
            exact(left, right, (1, 1)),
        ],
        axis=1,
    )
    adjoint(tile_rows, tile_firms, rows, tiles, feature_sums, NEAR_FIRST)
    add_ridge(feature_sums, firm[0], worker[0], NEAR_FIRST, regular, second)
    put_parts(out, feature_sums, three_parts(extra))


def eliminate(table, pivots):
    size, width = table.shape
    lanes = lax.broadcasted_iota(jnp.int32, (size, width), 1)
    lines = lax.broadcasted_iota(jnp.int32, (size, width), 0)

    def spread(at):
        column = jnp.broadcast_to(table[:, pivots[0] + at : pivots[0] + at + 1], (size, width))
        for begin in pivots[1:]:
            other = jnp.broadcast_to(table[:, begin + at : begin + at + 1], (size, width))
            column = jnp.where(lanes < begin, column, other)
        return column

    for start in range(0, size, PANEL):
        columns = [spread(start + item) for item in range(PANEL)]
        for item, column in enumerate(columns):
            at = start + item
            inverse = 1.0 / column[at : at + 1, :]
            line = table[at : at + 1, :] * inverse
            table = jnp.where(lines == at, line, table - column * line)
            for later in range(item + 1, PANEL):
                factor = columns[later][at : at + 1, :] * inverse
                columns[later] = jnp.where(lines == at, factor, columns[later] - column * factor)
    return table


def final_body(probe, given, last, solution_out, residual_out, basis, mixes):
    size = given.shape[0] * given.shape[2]
    gather = lambda ref, item: jnp.concatenate([ref[other, item] for other in range(given.shape[0])], axis=0)
    half = lambda matrix: 0.5 * (matrix + matrix.T)
    lines = lax.broadcasted_iota(jnp.int32, (size, size), 0)
    lanes = lax.broadcasted_iota(jnp.int32, (size, size), 1)
    unit = jnp.where(lines == lanes, 1.0, 0.0)
    tables = gather(last, 1)
    current = half(tables[:, :size])
    mixed = tables[:, size : 2 * size]
    other = tables[:, 2 * size : 3 * size]
    other_mapped = tables[:, 3 * size :]
    scale = gather(given, 2)[:, :size]
    same_mapped = half(scale * (current - mixed).T)
    mixed_mapped = scale * (mixed - other)

    def whole(one, cross, two):
        return jnp.concatenate(
            [jnp.concatenate([one, cross], axis=1), jnp.concatenate([cross.T, two], axis=1)], axis=0
        )

    grams = whole(current, mixed, other)
    mapped_grams = whole(same_mapped, mixed_mapped, other_mapped)
    solved = eliminate(jnp.concatenate([same_mapped, current, current, unit], axis=1), (0, 2 * size))
    step_first = solved[:, size : 2 * size]
    inverse = solved[:, 3 * size :]
    onto_second = scale * step_first
    onto_first = unit - onto_second
    mix = jnp.concatenate([onto_first, onto_second], axis=0)
    following = half(exact(mix, exact(grams, mix, (1, 0)), (0, 0)))
    direction = onto_first + exact(inverse, following, (1, 0))
    mix = jnp.concatenate([direction, onto_second], axis=0)
    curvature = half(exact(mix, exact(mapped_grams, mix, (1, 0)), (0, 0)))
    step_second = eliminate(jnp.concatenate([curvature, following], axis=1), (0,))[:, size:]
    moved = exact(mix, step_second, (1, 0))
    moved_first, moved_second = moved[:size], moved[size:]
    image = scale * moved_first
    probes = given.shape[2]
    for other in range(last.shape[0]):
        worker, part = other // given.shape[0], other % given.shape[0]
        for item, kind in enumerate((2, 3, 0)):
            line = item * size + part * probes
            basis[line : line + probes, worker * TILE : (worker + 1) * TILE] = last[other, kind]
    empty = jnp.zeros((size, size), f32)
    mixes[0] = jnp.concatenate([step_first + moved_first, moved_second, empty, empty], axis=0).T
    mixes[1] = jnp.concatenate([onto_first - image, onto_second + image, -moved_second, empty], axis=0).T
    begin = pl.multiple_of(probe[0] * probes, probes)
    both = jnp.concatenate([mixes[item, pl.ds(begin, probes), :][:, : 3 * size] for item in range(2)], axis=0)
    outs = exact(both, basis[...], (1, 0))
    solution_out[...] = outs[:probes]
    residual_out[...] = outs[probes:]


def fold_body(got, out):
    total = sum_of(got)
    firms, probes = out.shape[0], total.shape[1]
    for firm in range(firms):
        out[firm, :probes, :] = total[firm]
    if out.shape[1] > probes:
        extra = total[firms]
        for item in range(firms + 1, total.shape[0]):
            extra = extra + total[item]
        for firm in range(firms):
            out[firm, probes:, :] = extra


def sum_of(got):
    total = got[0].astype(f32)
    for other in range(1, got.shape[0]):
        total = total + got[other].astype(f32)
    return total


def send(out, values):
    for other in range(out.shape[0]):
        out[other] = values.astype(out.dtype)


def gather_fold_body(got, out):
    send(out, sum_of(got))


def first_body(got, firsts, sent):
    firsts[...] = sum_of(got)
    send(sent, firsts[...])


def second_body(firm, got, firsts, first, second, quotient, sent, seconds):
    total = sum_of(got)
    blocks = total.shape[0] - 1
    ratio = total[blocks, :, :1] / total[blocks, :, TILE // 2 : TILE // 2 + 1]
    quotient[...] = jnp.broadcast_to(ratio, quotient.shape)
    step = NEAR_SECOND // NEAR_FIRST
    near = lax.div(firm[0], NEAR_FIRST) & (step - 1)
    for block in range(blocks):
        seconds[block] = firsts[block * step + near] - total[block] / quotient[...]
    first[...] = firsts[lax.div(firm[0], NEAR_FIRST)]
    second[...] = seconds[lax.div(firm[0], NEAR_SECOND)]
    send(sent, seconds[...])


def third_body(got, first, second, sent):
    total = sum_of(got)
    probes = first.shape[0]
    for other in range(sent.shape[0]):
        sent[other, 0] = total[:probes]
        sent[other, 1] = total[probes:]
        sent[other, 2] = first[...]
        sent[other, 3] = second[...]


def kernel(body, shapes, places, scratch, name, cost=1 << 16):
    return pl.pallas_call(
        body,
        out_shape=shapes,
        in_specs=[pl.BlockSpec(memory_space=place) for place in places],
        out_specs=jax.tree.map(lambda _: pl.BlockSpec(memory_space=pltpu.VMEM), shapes),
        scratch_shapes=scratch,
        compiler_params=pltpu.CompilerParams(vmem_limit_bytes=6 << 20),
        cost_estimate=pl.CostEstimate(flops=cost, transcendentals=0, bytes_accessed=1 << 20),
        name=name,
    )


def exchange(chunks, axis, beside=()):
    chunks, beside = lax.optimization_barrier((chunks, beside))
    got = lax.all_to_all(chunks, axis, 0, 0, tiled=True)
    return lax.optimization_barrier((got, beside))


def local(tiles, tile_rows, tile_firms, worker_ids, sign_words, regular):
    probe_dev = sign_words.shape[0]
    probes = lax.axis_size("probe")
    count = tiles.shape[0]
    blocks = WORKERS * FIRMS
    reg_blocks = regular.reshape(WORKERS, TILE)
    words = jnp.transpose(sign_words, (2, 1, 0))
    at = tuple(lax.axis_index(axis).reshape(1) for axis in (FIRM_AXES, "worker", "probe"))

    VMEM, SMEM, HBM = pltpu.VMEM, pltpu.SMEM, pltpu.HBM
    rows_vmem = VMEM((ROWB_DEV, probe_dev, TILE), f32)
    sums_vmem = VMEM((blocks, probe_dev, TILE), f32)
    cost = 2 * count * probe_dev * TILE * TILE

    def shape(*dims, dtype=f32):
        return jax.ShapeDtypeStruct((*dims, probe_dev, TILE), dtype)

    def placed(array, where):
        return pltpu.with_memory_space_constraint(array, where)

    near_first, far_first = (*FIRM_AXES[2:], "worker"), FIRM_AXES[:2]
    near_second, far_second = (*FIRM_AXES[1:], "worker"), FIRM_AXES[:1]
    peers_first, held_first = NEAR_FIRST * WORKERS, FIRMS // NEAR_FIRST
    peers_second, held_second = NEAR_SECOND * WORKERS, FIRMS // NEAR_SECOND

    parts, tiles = kernel(
        start_body, (shape(blocks), VMEM(tiles.shape, bf16)), [HBM] * 5,
        [
            rows_vmem, pltpu.SemaphoreType.DMA((CHUNKS + 4,)), SMEM(tile_rows.shape, jnp.int32),
            SMEM(tile_firms.shape, jnp.int32), SMEM(words.shape, jnp.int32), VMEM(worker_ids.shape, jnp.int32),
        ],
        "start", cost,
    )(*(placed(array, HBM) for array in (tile_rows, tile_firms, words, worker_ids, tiles)))
    got, at = exchange(parts.reshape(peers_first, held_first, probe_dev, TILE), near_first, at)
    sent = kernel(gather_fold_body, shape(held_first, held_first), [VMEM], [], "fold")(got)
    got, at = exchange(sent, far_first, at)
    firsts, sent = kernel(
        first_body, (shape(held_first), shape(peers_first, held_first, dtype=bf16)), [VMEM], [], "first"
    )(got)

    field, (firsts, *at) = exchange(sent, near_first, (firsts, *at))
    firm, worker, _ = at
    parts = kernel(
        middle_body, shape(peers_second, held_second + 1),
        [SMEM, SMEM, SMEM, SMEM, VMEM, VMEM, VMEM, VMEM, VMEM], [rows_vmem, sums_vmem], "middle", 2 * cost,
    )(
        tile_rows, tile_firms, worker, firm, field.reshape(blocks, probe_dev, TILE), firsts, reg_blocks,
        worker_ids, placed(tiles, VMEM),
    )
    got, (firsts, *at) = exchange(parts, near_second, (firsts, *at))
    sent = kernel(gather_fold_body, shape(held_second, held_second + 1, dtype=bf16), [VMEM], [], "fold")(got)
    got, (firsts, *at) = exchange(sent, far_second, (firsts, *at))
    first, second, quotient, sent = kernel(
        second_body, (shape(), shape(), shape(), shape(peers_second, held_second, dtype=bf16)),
        [SMEM, VMEM, VMEM], [VMEM((held_second, probe_dev, TILE), f32)], "second",
    )(at[0], got, firsts)

    field, (first, second, quotient, *at) = exchange(sent, near_second, (first, second, quotient, *at))
    sent = kernel(
        rows_body, shape(probes, 3 + ROWB_DEV), [SMEM, SMEM, VMEM, VMEM, VMEM, VMEM, VMEM, VMEM], [], "rows", cost
    )(
        tile_rows, tile_firms, field.reshape(blocks, probe_dev, TILE), first, second, quotient, worker_ids,
        placed(tiles, VMEM),
    )
    given, (first, second, *at) = exchange(sent, "probe", (first, second, *at))
    firm, worker, probe = at
    parts = kernel(
        last_body, shape(peers_first, held_first + 3, dtype=bf16),
        [SMEM, SMEM, SMEM, SMEM, SMEM, VMEM, VMEM, VMEM],
        [VMEM((ROWB_DEV, 2 * probe_dev, TILE), f32), sums_vmem], "last", cost,
    )(tile_rows, tile_firms, worker, firm, probe, given, reg_blocks, placed(tiles, VMEM))
    got, (first, second, given, *at) = exchange(parts, near_first, (first, second, given, *at))
    sent = kernel(
        fold_body, jax.ShapeDtypeStruct((held_first, 2 * probe_dev, TILE), f32), [VMEM], [], "fold_last"
    )(got)
    got, (first, second, given, *at) = exchange(sent, far_first, (first, second, given, *at))
    sent = kernel(third_body, shape(WORKERS * probes, 4), [VMEM, VMEM, VMEM], [], "third")(got, first, second)
    last, (given, *at) = exchange(sent, ("worker", "probe"), (given, *at))
    out = jax.ShapeDtypeStruct((probe_dev, WORKERS * TILE), f32)
    total = probes * probe_dev
    return kernel(
        final_body, (out, out), [SMEM, VMEM, VMEM],
        [VMEM((3 * total, WORKERS * TILE), f32), VMEM((2, total, 4 * total), f32)], "final", cost // 4,
    )(at[2], given, last)


def solution(mesh):
    sizes = (FIRMS // NEAR_SECOND, NEAR_SECOND // NEAR_FIRST, NEAR_FIRST)
    split = jax.sharding.Mesh(
        mesh.devices.reshape(*sizes, WORKERS, mesh.shape["probe"]), (*FIRM_AXES, "worker", "probe")
    )
    shard = (*FIRM_AXES, "worker")
    placed = (
        P(shard, None, None),
        P(shard, None),
        P(shard, None),
        P(shard, None),
        P("probe", shard, None),
        P(FIRM_AXES),
    )
    return jax.shard_map(
        local,
        mesh=split,
        in_specs=placed,
        out_specs=(P("probe", FIRM_AXES), P("probe", FIRM_AXES)),
        check_vma=False,
    )
```

```python
import jax
import jax.numpy as jnp
from jax import lax
from jax.experimental import pallas as pl
from jax.experimental.pallas import tpu as pltpu
from jax.sharding import PartitionSpec as P

TILE = 128
ROWB_DEV = 4
ROWS_DEV = 512
SHARD_WORKERS = 128
BITS = 30
CHUNKS = 8
PANEL = 16
WORKERS = 8
FIRMS = 16
NEAR_FIRST = 2
NEAR_SECOND = 2
FIRM_AXES = ("firm_far", "firm_middle", "firm_near")

largest_value = lax.Precision.HIGHEST
f32 = jnp.float32
bf16 = jnp.bfloat16


def dot(left, right, dims, precision=None):
    return lax.dot_general(
        left, right, ((dims[:1], dims[1:]), ((), ())), precision=precision, preferred_element_type=f32
    )


def exact(left, right, dims):
    return dot(left, right, dims, largest_value)


def three_parts(values):
    high = values.astype(bf16)
    rest = values - high.astype(f32)
    middle = rest.astype(bf16)
    low = (rest - middle.astype(f32)).astype(bf16)
    return high, middle, low


def demean(values, worker_ids):
    probes = values.shape[0]
    workers = lax.broadcasted_iota(jnp.int32, (SHARD_WORKERS, ROWS_DEV), 0)
    onehot = jnp.where(workers == worker_ids, 1.0, 0.0).astype(bf16)
    stacked = jnp.concatenate([*(part.astype(f32) for part in three_parts(values)), jnp.ones_like(values)], axis=0)
    sums = dot(stacked.astype(bf16), onehot, (1, 1))
    totals = (sums[2 * probes : 3 * probes] + sums[probes : 2 * probes]) + sums[:probes]
    means = totals / sums[3 * probes :]
    stacked = jnp.concatenate([part.astype(f32) for part in three_parts(means)], axis=0)
    spread = dot(stacked.astype(bf16), onehot, (1, 0))
    return values - ((spread[2 * probes : 3 * probes] + spread[probes : 2 * probes]) + spread[:probes])


def fetch(tiles_hbm, tiles, arrived, small):
    size = tiles.shape[0] // CHUNKS

    def copy(chunk):
        part = pl.ds(chunk * size, size)
        return pltpu.make_async_copy(tiles_hbm.at[part], tiles.at[part], arrived.at[chunk])

    tables = fetch_small(arrived, small)
    for chunk in range(CHUNKS):
        copy(chunk).start()
    for table in tables:
        table.wait()
    return lambda chunk: copy(chunk).wait()


def fetch_small(arrived, small):
    tables = [pltpu.make_async_copy(*both, arrived.at[CHUNKS + item]) for item, both in enumerate(small)]
    for table in tables:
        table.start()
    return tables


def place_of(block, near):
    firm, worker = block >> (WORKERS.bit_length() - 1), block & (WORKERS - 1)
    shift = near.bit_length() - 1
    return ((firm & (near - 1)) * WORKERS + worker) * (FIRMS // near) + (firm >> shift)


def stack(pieces):
    return jnp.concatenate([piece.astype(f32) for piece in pieces], axis=0).astype(bf16)


def forward(tile_rows, tile_firms, field, tiles, near):
    total = None
    for tile in range(0, tiles.shape[0], 2):
        pieces = [field[place_of(tile_firms[0, tile + item], near)] for item in range(2)]
        probes = pieces[0].shape[0]
        weights = jnp.concatenate([tiles[tile], tiles[tile + 1]], axis=0)
        both = dot(stack(pieces), weights, (1, 1))
        if total is None:
            total = [jnp.zeros((probes, TILE), f32) for block in range(ROWB_DEV)]
        for item in range(2):
            image = both[item * probes : (item + 1) * probes, item * TILE : (item + 1) * TILE]
            row = tile_rows[0, tile + item]
            total = [old + jnp.where(row == block, image, 0.0) for block, old in enumerate(total)]
    return total


def adjoint(tile_rows, tile_firms, rows, tiles, out, near, wait=None):
    out[...] = jnp.zeros_like(out)
    probes, lines = out.shape[1], rows.shape[1]
    size = tiles.shape[0] // CHUNKS
    for tile in range(0, tiles.shape[0], 2):
        if wait is not None and tile % size == 0:
            wait(tile // size)
        weights = jnp.concatenate([tiles[tile], tiles[tile + 1]], axis=1)
        both = dot(stack([rows[tile_rows[0, tile + item]] for item in range(2)]), weights, (1, 0))
        for item in range(2):
            place = place_of(tile_firms[0, tile + item], near)
            image = out[place]
            for begin in range(item * lines, (item + 1) * lines, probes):
                image = image + both[begin : begin + probes, item * TILE : (item + 1) * TILE]
            out[place] = image


def put_rows(rows, values):
    for block in range(ROWB_DEV):
        rows[block] = values[:, block * TILE : (block + 1) * TILE].astype(bf16).astype(f32)


def put_two_terms(rows, values):
    high = values.astype(bf16).astype(f32)
    rows[...] = jnp.concatenate([high, (values - high).astype(bf16).astype(f32)], axis=0)


def put_parts(out, total, extras):
    peers, blocks = out.shape[0], out.shape[1] - len(extras)
    for peer in range(peers):
        for block in range(blocks):
            out[peer, block] = total[peer * blocks + block].astype(out.dtype)
        for item, extra in enumerate(extras):
            out[peer, blocks + item] = extra.astype(out.dtype)


def add_ridge(out, firm, worker, near, regular, own):
    place = place_of(firm * WORKERS + worker, near)
    out[place] = out[place] + regular[pl.ds(worker, 1), :] * own


def start_body(
    rows_hbm, firms_hbm, words_hbm, ids_hbm, tiles_hbm,
    out, tiles, rows, arrived, tile_rows, tile_firms, words, worker_ids,
):
    small = [(rows_hbm, tile_rows), (firms_hbm, tile_firms), (words_hbm, words), (ids_hbm, worker_ids)]
    wait = fetch(tiles_hbm, tiles, arrived, small)
    words_row, blocks, probes = words.shape
    lanes = lax.broadcasted_iota(jnp.int32, (probes, TILE), 1)
    lines = lax.broadcasted_iota(jnp.int32, (probes, TILE), 0)
    word_of = lax.div(lanes, jnp.int32(BITS))
    bit = lanes - word_of * BITS
    chosen = [jnp.zeros((probes, TILE), jnp.int32) for block in range(blocks)]
    for word in range(words_row):
        for probe in range(probes):
            here = (word_of == word) & (lines == probe)
            chosen = [jnp.where(here, words[word, block, probe], old) for block, old in enumerate(chosen)]
    signs = [(2 * (lax.shift_right_logical(old, bit) & 1) - 1).astype(f32) for old in chosen]
    put_rows(rows, demean(jnp.concatenate(signs, axis=1), worker_ids[...]))
    adjoint(tile_rows, tile_firms, rows, tiles, out, NEAR_FIRST, wait)


def middle_body(
    tile_rows, tile_firms, worker, firm, field, firsts, regular, worker_ids, tiles,
    out, rows, feature_sums,
):
    total = forward(tile_rows, tile_firms, field, tiles, NEAR_FIRST)
    values = demean(jnp.concatenate(total, axis=1), worker_ids[...])
    put_rows(rows, values)
    adjoint(tile_rows, tile_firms, rows, tiles, feature_sums, NEAR_SECOND)
    own = firsts[lax.div(firm[0], NEAR_FIRST)]
    add_ridge(feature_sums, firm[0], worker[0], NEAR_SECOND, regular, own)
    squares = own * own
    above = jnp.sum(values * values, axis=1, keepdims=True)
    above = above + jnp.sum(squares * regular[pl.ds(worker[0], 1), :], axis=1, keepdims=True)
    below = jnp.sum(squares, axis=1, keepdims=True)
    lanes = lax.broadcasted_iota(jnp.int32, own.shape, 1)
    put_parts(out, feature_sums, [jnp.where(lanes < TILE // 2, above, below)])


def rows_body(tile_rows, tile_firms, field, first, second, quotient, worker_ids, tiles, out):
    total = forward(tile_rows, tile_firms, field, tiles, NEAR_SECOND)
    values = demean(jnp.concatenate(total, axis=1), worker_ids[...])
    for probe in range(out.shape[0]):
        out[probe, 0] = first[...]
        out[probe, 1] = second[...]
        out[probe, 2] = quotient[...]
        for block in range(ROWB_DEV):
            out[probe, 3 + block] = values[:, block * TILE : (block + 1) * TILE]


def last_body(
    tile_rows, tile_firms, worker, firm, probe, given, regular, tiles,
    out, rows, feature_sums,
):
    gather = lambda item: jnp.concatenate([given[other, item] for other in range(given.shape[0])], axis=0)
    own = lambda item: given[probe[0], item]
    first, second = own(0), own(1)
    first_all, second_all = gather(0), gather(1)
    mine = [own(3 + block) for block in range(ROWB_DEV)]
    for block in range(ROWB_DEV):
        put_two_terms(rows.at[block], mine[block])
    left = jnp.concatenate([*mine, second * regular[pl.ds(worker[0], 1), :]], axis=1)
    right = jnp.concatenate([*(gather(3 + block) for block in range(ROWB_DEV)), second_all], axis=1)
    extra = jnp.concatenate(
        [
            exact(first, first_all, (1, 1)),
            exact(first, second_all, (1, 1)),
            exact(second, second_all, (1, 1)),
            exact(left, right, (1, 1)),
        ],
        axis=1,
    )
    adjoint(tile_rows, tile_firms, rows, tiles, feature_sums, 1)
    add_ridge(feature_sums, firm[0], worker[0], 1, regular, second)
    put_parts(out, feature_sums, three_parts(extra))


def eliminate(table, pivots):
    size, width = table.shape
    lanes = lax.broadcasted_iota(jnp.int32, (size, width), 1)
    lines = lax.broadcasted_iota(jnp.int32, (size, width), 0)

    def spread(at):
        column = jnp.broadcast_to(table[:, pivots[0] + at : pivots[0] + at + 1], (size, width))
        for begin in pivots[1:]:
            other = jnp.broadcast_to(table[:, begin + at : begin + at + 1], (size, width))
            column = jnp.where(lanes < begin, column, other)
        return column

    for start in range(0, size, PANEL):
        columns = [spread(start + item) for item in range(PANEL)]
        for item, column in enumerate(columns):
            at = start + item
            inverse = 1.0 / column[at : at + 1, :]
            line = table[at : at + 1, :] * inverse
            table = jnp.where(lines == at, line, table - column * line)
            for later in range(item + 1, PANEL):
                factor = columns[later][at : at + 1, :] * inverse
                columns[later] = jnp.where(lines == at, factor, columns[later] - column * factor)
    return table


def final_body(probe, given, last, solution_out, residual_out, basis, mixes):
    size = given.shape[0] * given.shape[2]
    gather = lambda ref, item: jnp.concatenate([ref[other, item] for other in range(given.shape[0])], axis=0)
    half = lambda matrix: 0.5 * (matrix + matrix.T)
    lines = lax.broadcasted_iota(jnp.int32, (size, size), 0)
    lanes = lax.broadcasted_iota(jnp.int32, (size, size), 1)
    unit = jnp.where(lines == lanes, 1.0, 0.0)
    tables = gather(last, 1)
    current = half(tables[:, :size])
    mixed = tables[:, size : 2 * size]
    other = tables[:, 2 * size : 3 * size]
    other_mapped = tables[:, 3 * size :]
    scale = gather(given, 2)[:, :size]
    same_mapped = half(scale * (current - mixed).T)
    mixed_mapped = scale * (mixed - other)

    def whole(one, cross, two):
        return jnp.concatenate(
            [jnp.concatenate([one, cross], axis=1), jnp.concatenate([cross.T, two], axis=1)], axis=0
        )

    grams = whole(current, mixed, other)
    mapped_grams = whole(same_mapped, mixed_mapped, other_mapped)
    solved = eliminate(jnp.concatenate([same_mapped, current, current, unit], axis=1), (0, 2 * size))
    step_first = solved[:, size : 2 * size]
    inverse = solved[:, 3 * size :]
    onto_second = scale * step_first
    onto_first = unit - onto_second
    mix = jnp.concatenate([onto_first, onto_second], axis=0)
    following = half(exact(mix, exact(grams, mix, (1, 0)), (0, 0)))
    direction = onto_first + exact(inverse, following, (1, 0))
    mix = jnp.concatenate([direction, onto_second], axis=0)
    curvature = half(exact(mix, exact(mapped_grams, mix, (1, 0)), (0, 0)))
    step_second = eliminate(jnp.concatenate([curvature, following], axis=1), (0,))[:, size:]
    moved = exact(mix, step_second, (1, 0))
    moved_first, moved_second = moved[:size], moved[size:]
    image = scale * moved_first
    probes = given.shape[2]
    for other in range(last.shape[0]):
        worker, part = other // given.shape[0], other % given.shape[0]
        for item, kind in enumerate((2, 3, 0)):
            line = item * size + part * probes
            basis[line : line + probes, worker * TILE : (worker + 1) * TILE] = last[other, kind]
    empty = jnp.zeros((size, size), f32)
    mixes[0] = jnp.concatenate([step_first + moved_first, moved_second, empty, empty], axis=0).T
    mixes[1] = jnp.concatenate([onto_first - image, onto_second + image, -moved_second, empty], axis=0).T
    begin = pl.multiple_of(probe[0] * probes, probes)
    both = jnp.concatenate([mixes[item, pl.ds(begin, probes), :][:, : 3 * size] for item in range(2)], axis=0)
    outs = exact(both, basis[...], (1, 0))
    solution_out[...] = outs[:probes]
    residual_out[...] = outs[probes:]


def fold_body(got, out):
    total = sum_of(got)
    firms, probes = out.shape[0], total.shape[1]
    for firm in range(firms):
        out[firm, :probes, :] = total[firm]
    if out.shape[1] > probes:
        extra = total[firms]
        for item in range(firms + 1, total.shape[0]):
            extra = extra + total[item]
        for firm in range(firms):
            out[firm, probes:, :] = extra


def sum_of(got):
    total = got[0].astype(f32)
    for other in range(1, got.shape[0]):
        total = total + got[other].astype(f32)
    return total


def send(out, values):
    for other in range(out.shape[0]):
        out[other] = values.astype(out.dtype)


def gather_fold_body(got, out):
    send(out, sum_of(got))


def first_body(got, firsts, sent):
    firsts[...] = sum_of(got)
    send(sent, firsts[...])


def second_body(firm, got, firsts, first, second, quotient, sent, seconds):
    total = sum_of(got)
    blocks = total.shape[0] - 1
    ratio = total[blocks, :, :1] / total[blocks, :, TILE // 2 : TILE // 2 + 1]
    quotient[...] = jnp.broadcast_to(ratio, quotient.shape)
    step = NEAR_SECOND // NEAR_FIRST
    near = lax.div(firm[0], NEAR_FIRST) & (step - 1)
    for block in range(blocks):
        seconds[block] = firsts[block * step + near] - total[block] / quotient[...]
    first[...] = firsts[lax.div(firm[0], NEAR_FIRST)]
    second[...] = seconds[lax.div(firm[0], NEAR_SECOND)]
    send(sent, seconds[...])


def third_body(got, first, second, sent):
    total = sum_of(got)
    probes = first.shape[0]
    for other in range(sent.shape[0]):
        sent[other, 0] = total[:probes]
        sent[other, 1] = total[probes:]
        sent[other, 2] = first[...]
        sent[other, 3] = second[...]


def kernel(body, shapes, places, scratch, name, cost=1 << 16):
    return pl.pallas_call(
        body,
        out_shape=shapes,
        in_specs=[pl.BlockSpec(memory_space=place) for place in places],
        out_specs=jax.tree.map(lambda _: pl.BlockSpec(memory_space=pltpu.VMEM), shapes),
        scratch_shapes=scratch,
        compiler_params=pltpu.CompilerParams(vmem_limit_bytes=6 << 20),
        cost_estimate=pl.CostEstimate(flops=cost, transcendentals=0, bytes_accessed=1 << 20),
        name=name,
    )


def exchange(chunks, axis, beside=()):
    chunks, beside = lax.optimization_barrier((chunks, beside))
    got = lax.all_to_all(chunks, axis, 0, 0, tiled=True)
    return lax.optimization_barrier((got, beside))


def local(tiles, tile_rows, tile_firms, worker_ids, sign_words, regular):
    probe_dev = sign_words.shape[0]
    probes = lax.axis_size("probe")
    count = tiles.shape[0]
    blocks = WORKERS * FIRMS
    reg_blocks = regular.reshape(WORKERS, TILE)
    words = jnp.transpose(sign_words, (2, 1, 0))
    at = tuple(lax.axis_index(axis).reshape(1) for axis in (FIRM_AXES, "worker", "probe"))

    VMEM, SMEM, HBM = pltpu.VMEM, pltpu.SMEM, pltpu.HBM
    rows_vmem = VMEM((ROWB_DEV, probe_dev, TILE), f32)
    sums_vmem = VMEM((blocks, probe_dev, TILE), f32)
    cost = 2 * count * probe_dev * TILE * TILE

    def shape(*dims, dtype=f32):
        return jax.ShapeDtypeStruct((*dims, probe_dev, TILE), dtype)

    def placed(array, where):
        return pltpu.with_memory_space_constraint(array, where)

    near_first, far_first = (*FIRM_AXES[2:], "worker"), FIRM_AXES[:2]
    near_second, far_second = (*FIRM_AXES[1:], "worker"), FIRM_AXES[:1]
    peers_first, held_first = NEAR_FIRST * WORKERS, FIRMS // NEAR_FIRST
    peers_second, held_second = NEAR_SECOND * WORKERS, FIRMS // NEAR_SECOND

    parts, tiles = kernel(
        start_body, (shape(blocks), VMEM(tiles.shape, bf16)), [HBM] * 5,
        [
            rows_vmem, pltpu.SemaphoreType.DMA((CHUNKS + 4,)), SMEM(tile_rows.shape, jnp.int32),
            SMEM(tile_firms.shape, jnp.int32), SMEM(words.shape, jnp.int32), VMEM(worker_ids.shape, jnp.int32),
        ],
        "start", cost,
    )(*(placed(array, HBM) for array in (tile_rows, tile_firms, words, worker_ids, tiles)))
    got, at = exchange(parts.reshape(peers_first, held_first, probe_dev, TILE), near_first, at)
    sent = kernel(gather_fold_body, shape(held_first, held_first), [VMEM], [], "fold")(got)
    got, at = exchange(sent, far_first, at)
    firsts, sent = kernel(
        first_body, (shape(held_first), shape(peers_first, held_first, dtype=bf16)), [VMEM], [], "first"
    )(got)

    field, (firsts, *at) = exchange(sent, near_first, (firsts, *at))
    firm, worker, _ = at
    parts = kernel(
        middle_body, shape(peers_second, held_second + 1),
        [SMEM, SMEM, SMEM, SMEM, VMEM, VMEM, VMEM, VMEM, VMEM], [rows_vmem, sums_vmem], "middle", 2 * cost,
    )(
        tile_rows, tile_firms, worker, firm, field.reshape(blocks, probe_dev, TILE), firsts, reg_blocks,
        worker_ids, placed(tiles, VMEM),
    )
    got, (firsts, *at) = exchange(parts, near_second, (firsts, *at))
    sent = kernel(gather_fold_body, shape(held_second, held_second + 1, dtype=bf16), [VMEM], [], "fold")(got)
    got, (firsts, *at) = exchange(sent, far_second, (firsts, *at))
    first, second, quotient, sent = kernel(
        second_body, (shape(), shape(), shape(), shape(peers_second, held_second, dtype=bf16)),
        [SMEM, VMEM, VMEM], [VMEM((held_second, probe_dev, TILE), f32)], "second",
    )(at[0], got, firsts)

    field, (first, second, quotient, *at) = exchange(sent, near_second, (first, second, quotient, *at))
    sent = kernel(
        rows_body, shape(probes, 3 + ROWB_DEV), [SMEM, SMEM, VMEM, VMEM, VMEM, VMEM, VMEM, VMEM], [], "rows", cost
    )(
        tile_rows, tile_firms, field.reshape(blocks, probe_dev, TILE), first, second, quotient, worker_ids,
        placed(tiles, VMEM),
    )
    given, (first, second, *at) = exchange(sent, "probe", (first, second, *at))
    firm, worker, probe = at
    parts = kernel(
        last_body, shape(WORKERS, FIRMS + 3, dtype=bf16),
        [SMEM, SMEM, SMEM, SMEM, SMEM, VMEM, VMEM, VMEM],
        [VMEM((ROWB_DEV, 2 * probe_dev, TILE), f32), sums_vmem], "last", cost,
    )(tile_rows, tile_firms, worker, firm, probe, given, reg_blocks, placed(tiles, VMEM))
    got, (first, second, given, *at) = exchange(parts, "worker", (first, second, given, *at))
    sent = kernel(
        fold_body, jax.ShapeDtypeStruct((FIRMS, 2 * probe_dev, TILE), f32), [VMEM], [], "fold_last"
    )(got)
    got, (first, second, given, *at) = exchange(sent, FIRM_AXES, (first, second, given, *at))
    sent = kernel(third_body, shape(WORKERS * probes, 4), [VMEM, VMEM, VMEM], [], "third")(got, first, second)
    last, (given, *at) = exchange(sent, ("worker", "probe"), (given, *at))
    out = jax.ShapeDtypeStruct((probe_dev, WORKERS * TILE), f32)
    total = probes * probe_dev
    return kernel(
        final_body, (out, out), [SMEM, VMEM, VMEM],
        [VMEM((3 * total, WORKERS * TILE), f32), VMEM((2, total, 4 * total), f32)], "final", cost // 4,
    )(at[2], given, last)


def solution(mesh):
    sizes = (FIRMS // NEAR_SECOND, NEAR_SECOND // NEAR_FIRST, NEAR_FIRST)
    split = jax.sharding.Mesh(
        mesh.devices.reshape(*sizes, WORKERS, mesh.shape["probe"]), (*FIRM_AXES, "worker", "probe")
    )
    shard = (*FIRM_AXES, "worker")
    placed = (
        P(shard, None, None),
        P(shard, None),
        P(shard, None),
        P(shard, None),
        P("probe", shard, None),
        P(FIRM_AXES),
    )
    return jax.shard_map(
        local,
        mesh=split,
        in_specs=placed,
        out_specs=(P("probe", FIRM_AXES), P("probe", FIRM_AXES)),
        check_vma=False,
    )
```
